32 devices in a mesh: fsdp: 8 (over y, x, core), tp: 4 (over z).
Axes of the slice: x: 2, y: 2, z: 4, core: 2. Of those that a mesh axis runs over, the one named last changes fastest.
Arguments:
- inputs: bfloat16 [2, 4096, 1024], P(None, ('fsdp', 'tp')), may hold values from -6 to 6
- cotangent: bfloat16 [2, 4096, 1024], P(None, ('fsdp', 'tp')), may hold values from -6 to 6
- lengths: int32 [2], replicated, may hold values from 1024 to 4096, as said below
- routes: int32 [2, 4096, 8], P(None, 'fsdp'), may hold values from 0 to 15, all different within a row; in each aligned block of 512 rows (0 to 511, 512 to 1023, ..., all dimensions but the last counted through in order) at most 384 rows name the same one
- attn_gain: bfloat16 [1024], P(('fsdp', 'tp')), may hold values from 0.5 to 1.5
- moe_gain: bfloat16 [1024], P(('fsdp', 'tp')), may hold values from 0.5 to 1.5
- router_weight: bfloat16 [1024, 16], P(('fsdp', 'tp')), may hold values from -0.09375 to 0.09375
- query_weight: bfloat16 [1024, 1024], P('fsdp', 'tp'), may hold values from -0.1875 to 0.1875
- key_weight: bfloat16 [1024, 512], P('fsdp', 'tp'), may hold values from -0.1875 to 0.1875
- value_weight: bfloat16 [1024, 512], P('fsdp', 'tp'), may hold values from -0.1875 to 0.1875
- output_weight: bfloat16 [1024, 1024], P('tp', 'fsdp'), may hold values from -3 to 3
- gate_weight: bfloat16 [16, 1024, 512], P(None, 'fsdp', 'tp'), may hold values from -0.1875 to 0.1875
- up_weight: bfloat16 [16, 1024, 512], P(None, 'fsdp', 'tp'), may hold values from -0.1875 to 0.1875
- down_weight: bfloat16 [16, 512, 1024], P(None, 'tp', 'fsdp'), may hold values from -0.75 to 0.75
Outputs:
- outputs: bfloat16 [2, 4096, 1024], P(None, ('fsdp', 'tp'))
- input_grad: float32 [2, 4096, 1024], P(None, ('fsdp', 'tp'))
- attn_gain_grad: float32 [1024], P(('fsdp', 'tp'))
- moe_gain_grad: float32 [1024], P(('fsdp', 'tp'))
- router_grad: float32 [1024, 16], P(('fsdp', 'tp'))
- query_grad: float32 [1024, 1024], P('fsdp', 'tp')
- key_grad: float32 [1024, 512], P('fsdp', 'tp')
- value_grad: float32 [1024, 512], P('fsdp', 'tp')
- output_grad: float32 [1024, 1024], P('tp', 'fsdp')
- gate_grad: float32 [16, 1024, 512], P(None, 'fsdp', 'tp')
- up_grad: float32 [16, 1024, 512], P(None, 'fsdp', 'tp')
- down_grad: float32 [16, 512, 1024], P(None, 'tp', 'fsdp')
The draws below stay inside these ranges and needn't reach their ends.
Inputs may be any that keep to these rules, and one draw needn't show every extreme that they name: `lengths`: one slot has exactly 4096 valid tokens; the others have 4096/4 to 4096. `routes`: each token names 8 different experts. Within the 512 tokens of one slot on one index of fsdp (aligned blocks), no expert is named by more than 384 tokens, a bound that some block reaches.
All inputs are finite; a program needn't handle non-finite values.
Results may differ from the reference program's by a relative error of at most 0.029.
Values may be sent and summed in bfloat16 or wider, within the bound.
A program may use at most 320 MiB of HBM per device.

```python
import math
import jax
import jax.numpy as jnp
import numpy as np
from jax import lax

D = 1024
HQ = 16
HK = 8
HD = 64
FF = 512
TOPK = 8
E = 16
MB = 2
SPAN = 512
SEQ = 4096
CAP = 384


def draw_lengths(key, part):
    first, second = jax.random.split(key)
    drawn = jax.random.randint(first, (MB,), SEQ // 4, SEQ + 1)
    longest = jax.random.randint(second, (), 0, MB)
    return jnp.where(jnp.arange(MB) == longest, SEQ, drawn).astype(jnp.int32)


def levels(key, shape, cuts, smallest, top_value):
    loudness = 1.0
    for position, blocks in cuts:
        steps = jax.random.uniform(jax.random.fold_in(jax.random.fold_in(key, 6), position), (blocks,), jnp.float32, smallest / len(cuts), top_value / len(cuts))
        loudness = loudness * jnp.repeat(jnp.exp(steps), shape[position] // blocks).reshape((-1,) + (1,) * (len(shape) - 1 - position))
    return loudness


def routed_block(rng, own, number, rows, number_of, top, most, lean):
    sequence = jax.random.permutation(rng, number_of)
    heavy_load, common = portions_of(number_of, rows * top, most, lean, True), portions_of(number_of, rows * top, most, lean, False)
    places = jnp.arange(number_of)

    def named(sizes, rotation):
        used = int((sizes > 0).sum())
        fixed = max(1, used // 4)
        moved = fixed + (places - fixed + rotation * (used - fixed)) % max(1, number_of - fixed)
        return jnp.zeros((number_of,), jnp.int32).at[sequence[jnp.where(places < fixed, places, moved)]].set(jnp.asarray(sizes, jnp.int32))

    sizes = jnp.where(number % 4 == 0, named(heavy_load, number // 4), named(common, number - number // 4 - 1))
    mixed = jax.random.permutation(jax.random.fold_in(own, 3), number_of)
    source_of, taker = mixed[0:number_of // 2 * 2:2], mixed[1:number_of // 2 * 2:2]
    room = jnp.minimum(sizes[source_of] - 1, most - sizes[taker]) // 2
    room = jnp.where((source_of == sequence[0]) | (taker == sequence[0]) | (sizes[taker] == 0), 0, jnp.maximum(room, 0))
    moved = jax.random.randint(jax.random.fold_in(own, 4), (number_of // 2,), 0, 1 << 20) % (room + 1)
    sizes = sizes.at[source_of].add(-moved).at[taker].add(moved)
    members = jnp.searchsorted(jnp.cumsum(sizes), jnp.arange(rows * top), side="right").astype(jnp.int32)
    table = members.reshape(top, rows).T
    table = table[jax.random.permutation(jax.random.fold_in(own, 1), rows)]
    rotation = jax.random.randint(jax.random.fold_in(own, 2), (rows, 1), 0, top)
    return jnp.take_along_axis(table, (jnp.arange(top)[None, :] + rotation) % top, axis=1)


def portions_of(number_of, total, bound, slope, full):
    weights = [(1 << 20) // math.isqrt(standing ** slope) + 1 for standing in range(1, number_of + 1)]
    largest = bound if full else min(bound, max(-(-total // number_of), total * weights[0] // sum(weights)))
    least = 1 if total - largest >= number_of - 1 else 0
    counts, rest = [largest] + [least] * (number_of - 1), total - largest - least * (number_of - 1)
    while rest > 0:
        movable = [i for i in range(1, number_of) if counts[i] < largest] or [i for i in range(1, number_of) if counts[i] < bound]
        whole, budget = sum([weights[i] for i in movable]), rest
        for i in movable:
            extra = min(bound - counts[i], max(1, budget * weights[i] // whole), rest)
            counts[i] = counts[i] + extra
            rest = rest - extra
    return np.array(counts)


def gaussian(key, extent, deviation, most, shards=(), kind=jnp.bfloat16):
    entries = deviation * jax.random.normal(key, extent, jnp.float32)
    if shards:
        entries = entries * levels(key, extent, shards, -0.22, 0.18)
    return jnp.clip(entries, -most, most).astype(kind)


def setup_inputs(seed: int = 0) -> dict:
    arg_keys = jax.random.split(jax.random.key(seed), 15)
    inputs = gaussian(arg_keys[0], (MB, SEQ, D), 1.0, 6.0, ((1, 32),))
    cotangent = gaussian(arg_keys[1], (MB, SEQ, D), 1.0, 6.0, ((1, 32),))
    lengths = draw_lengths(jax.random.fold_in(arg_keys[14], 71), 0)
    routes_keys = jax.random.split(jax.random.fold_in(arg_keys[3], 1), MB * SEQ // SPAN)
    routes_turns = jax.random.permutation(jax.random.fold_in(arg_keys[3], 3), MB * SEQ // SPAN)
    routes = jax.vmap(lambda own, number: routed_block(jax.random.fold_in(arg_keys[3], 2), own, number, SPAN, E, TOPK, CAP, 2))(routes_keys, routes_turns).reshape((MB, SEQ, TOPK))
    attn_gain = jnp.clip(1.0 + 0.1 * jax.random.normal(arg_keys[4], (D,), jnp.float32), 0.5, 1.5).astype(jnp.bfloat16)
    moe_gain = jnp.clip(1.0 + 0.1 * jax.random.normal(arg_keys[5], (D,), jnp.float32), 0.5, 1.5).astype(jnp.bfloat16)
    router_weight = gaussian(arg_keys[6], (D, E), (4 * D) ** -0.5, 0.09375, ((0, 32),))
    query_weight = gaussian(arg_keys[7], (D, HQ * HD), D ** -0.5, 0.1875, ((0, 8), (1, 4)))
    key_weight = gaussian(arg_keys[8], (D, HK * HD), D ** -0.5, 0.1875, ((0, 8), (1, 4)))
    value_weight = gaussian(arg_keys[9], (D, HK * HD), D ** -0.5, 0.1875, ((0, 8), (1, 4)))
    output_weight = gaussian(arg_keys[10], (HQ * HD, D), (max(4, HQ * HD // 256)) ** -0.5, 3.0, ((0, 4), (1, 8)))
    gate_weight = gaussian(arg_keys[11], (E, D, FF), D ** -0.5, 0.1875, ((1, 8), (2, 4)))
    up_weight = gaussian(arg_keys[12], (E, D, FF), D ** -0.5, 0.1875, ((1, 8), (2, 4)))
    down_weight = gaussian(arg_keys[13], (E, FF, D), (FF // 8) ** -0.5, 0.75, ((1, 4), (2, 8)))
    return {"inputs": inputs, "cotangent": cotangent, "lengths": lengths, "routes": routes, "attn_gain": attn_gain, "moe_gain": moe_gain, "router_weight": router_weight, "query_weight": query_weight, "key_weight": key_weight, "value_weight": value_weight, "output_weight": output_weight, "gate_weight": gate_weight, "up_weight": up_weight, "down_weight": down_weight}


@jax.custom_vjp
def low(v):
    return lax.optimization_barrier(v.astype(jnp.bfloat16)).astype(jnp.float32)

@jax.custom_vjp
def low_back(v):
    return v

def low_keep(v):
    return (low(v), None)

def low_pass(kept, grad):
    return (grad,)

def back_keep(v):
    return (v, None)

def back_low(kept, grad):
    return (low(grad),)
low.defvjp(low_keep, low_pass)
low_back.defvjp(back_keep, back_low)
epsilon = 1e-06
negative_fill = -1e+30
theta_base = 10000.0
highest = lax.Precision.HIGHEST

def rotate(values, positions, direction):
    half = values.shape[-1] // 2
    freqs = theta_base ** (-jnp.arange(half, dtype=jnp.float32) * 2.0 / values.shape[-1])
    angles = positions.astype(jnp.float32)[:, None] * freqs[None, :]
    cosine = jnp.cos(angles)[:, None, :]
    sine = direction * jnp.sin(angles)[:, None, :]
    first = values[..., :half]
    second = values[..., half:]
    return jnp.concatenate([first * cosine - second * sine, second * cosine + first * sine], axis=-1)

def rms_scale(values):
    return values * lax.rsqrt(lax.optimization_barrier(jnp.mean(values * values, axis=-1, keepdims=True)) + epsilon)

def softmax_last(values):
    shifted = values - lax.optimization_barrier(jnp.max(values, axis=-1, keepdims=True))
    exps = jnp.exp(shifted)
    return exps / lax.optimization_barrier(jnp.sum(exps, axis=-1, keepdims=True))

def layer(inputs, params, length, route_rows):
    attn_gain, moe_gain, router_weight, query_weight, key_weight, value_weight, output_weight, gate_weight, up_weight, down_weight = params
    positions = jnp.arange(SEQ, dtype=jnp.int32)
    group = HQ // HK
    scale = HD ** (-0.5)
    normed = low(rms_scale(inputs) * attn_gain)
    query = low_back(jnp.dot(normed, query_weight, precision=highest)).reshape(SEQ, HQ, HD)
    query = low(rotate(query, positions, 1.0))
    keys = low_back(jnp.dot(normed, key_weight, precision=highest)).reshape(SEQ, HK, HD)
    keys = low(rotate(keys, positions, 1.0))
    values = low(low_back(jnp.dot(normed, value_weight, precision=highest))).reshape(SEQ, HK, HD)
    block = min(SEQ, 512)
    count = SEQ // block
    query_blocks = query.reshape(count, block, HK, group, HD)
    starts = jnp.arange(count, dtype=jnp.int32) * block

    def attend(pieces):
        query_block, start = pieces
        raw = jnp.einsum('qhgd,khd->hgqk', query_block, keys, precision=highest)
        scores = low_back(raw) * scale
        query_pos = start + jnp.arange(block, dtype=jnp.int32)
        allowed = (positions[None, :] <= query_pos[:, None]) & (positions[None, :] < length)
        scores = jnp.where(allowed, scores, negative_fill)
        probs = low(softmax_last(scores))
        return jnp.einsum('hgqk,khd->qhgd', probs, values, precision=highest)
    attended = lax.map(jax.checkpoint(attend), (query_blocks, starts))
    attended = low(low_back(attended.reshape(SEQ, HQ * HD)))
    projected = low_back(jnp.dot(attended, output_weight, precision=highest))
    middle = inputs + projected
    normed_moe = low(rms_scale(middle) * moe_gain)
    logits = low_back(jnp.dot(normed_moe, router_weight, precision=highest))
    chosen = jnp.take_along_axis(logits, route_rows, axis=1)
    gates = softmax_last(chosen)
    onehot = (route_rows[:, :, None] == jnp.arange(E, dtype=jnp.int32)[None, None, :]).astype(jnp.float32)
    columns = lax.optimization_barrier(jnp.sum(gates[:, :, None] * onehot, axis=1))

    def expert(total, pieces):
        gate_part, up_part, down_part, column = pieces
        gate_pre = low_back(jnp.dot(normed_moe, gate_part, precision=highest))
        up_pre = low_back(jnp.dot(normed_moe, up_part, precision=highest))
        hidden = low(gate_pre * jax.nn.sigmoid(gate_pre) * up_pre)
        outcome = low_back(jnp.dot(hidden, down_part, precision=highest))
        return (total + column[:, None] * outcome, None)
    mixed, unused = lax.scan(jax.checkpoint(expert), jnp.zeros((SEQ, D), jnp.float32), (gate_weight, up_weight, down_weight, columns.T))
    mixed = low_back(mixed)
    valid = (positions < length).astype(jnp.float32)[:, None]
    return (middle + mixed) * valid

def reference(inputs, cotangent, lengths, routes, attn_gain, moe_gain, router_weight, query_weight, key_weight, value_weight, output_weight, gate_weight, up_weight, down_weight):
    params = tuple((weight.astype(jnp.float32) for weight in (attn_gain, moe_gain, router_weight, query_weight, key_weight, value_weight, output_weight, gate_weight, up_weight, down_weight)))

    def micro_step(totals, pieces):
        batch_in, batch_cot, length, route_rows = pieces

        def apply(values, weights):
            return layer(values, weights, length, route_rows)
        result, pullback = jax.vjp(apply, batch_in.astype(jnp.float32), params)
        grad_in, grad_params = pullback(batch_cot.astype(jnp.float32))
        new_totals = tuple((total + part for total, part in zip(totals, grad_params)))
        return (new_totals, (result.astype(jnp.bfloat16), grad_in))
    zeros = tuple((jnp.zeros_like(weight) for weight in params))
    totals, stacked = lax.scan(micro_step, zeros, (inputs, cotangent, lengths, routes))
    return (stacked[0], stacked[1], totals[0], totals[1], totals[2], totals[3], totals[4], totals[5], totals[6], totals[7], totals[8], totals[9])
```

```python
import functools

import jax
import jax.numpy as jnp
from jax import lax
from jax.experimental import pallas as pl
from jax.experimental.pallas import tpu as pltpu
from jax.sharding import PartitionSpec as P

HD = 64
LANES = 128
PAIR = 2
EPS = 1e-06
FILL = -1e30
THETA = 10000.0
VMEM_CAP = 60 * 1024 * 1024
f32 = jnp.float32
bf16 = jnp.bfloat16


def dot_nn(a, b):
    return lax.dot_general(a, b, (((1,), (0,)), ((), ())), preferred_element_type=f32)


def dot_nt(a, b):
    return lax.dot_general(a, b, (((1,), (1,)), ((), ())), preferred_element_type=f32)


def swap_halves(values):
    lane = lax.broadcasted_iota(jnp.int32, values.shape, values.ndim - 1)
    ahead = pltpu.roll(values, values.shape[-1] - HD // 2, values.ndim - 1)
    back = pltpu.roll(values, HD // 2, values.ndim - 1)
    return jnp.where(lane % HD < HD // 2, ahead, back)


def rope_tables(positions):
    half = HD // 2
    freqs = THETA ** (-jnp.arange(half, dtype=f32) * 2.0 / HD)
    angles = positions.astype(f32)[:, None] * freqs[None, :]
    cosine, sine = jnp.cos(angles), jnp.sin(angles)
    cos_row = jnp.concatenate([cosine] * 4, axis=1)
    sin_row = jnp.concatenate([-sine, sine] * 2, axis=1)
    return cos_row, sin_row


def qkv_kernel(x_ref, gain_ref, w_ref, cos_ref, sin_ref, normed_ref, q_ref, kv_ref):
    micro = x_ref.shape[1]
    cos_row, sin_row = cos_ref[...], sin_ref[...]
    for m in range(micro):
        x = x_ref[0, m].astype(f32)
        inverse = lax.rsqrt(jnp.mean(x * x, axis=-1, keepdims=True) + EPS)
        normed = (x * inverse * gain_ref[...]).astype(bf16)
        normed_ref[0, m] = normed
        pre = dot_nn(normed, w_ref[...])
        for part in range(3):
            cols = pre[:, part * LANES : (part + 1) * LANES]
            turned = cols * cos_row + swap_halves(cols) * sin_row
            if part < 2:
                q_ref[0, m, :, part * LANES : (part + 1) * LANES] = (turned * HD ** (-0.5)).astype(bf16)
            else:
                kv_ref[0, m, :, 0:LANES] = turned.astype(bf16)
        kv_ref[0, m, :, LANES : 2 * LANES] = pre[:, 3 * LANES : 4 * LANES].astype(bf16)


def project_qkv(x_all, gain, weight, cos_row, sin_row):
    parts, micro, rows, width = x_all.shape
    block = lambda cols: pl.BlockSpec((1, micro, rows, cols), lambda i: (i, 0, 0, 0))
    whole = lambda shape: pl.BlockSpec(shape, lambda i: (0, 0))
    table = pl.BlockSpec((rows, LANES), lambda i: (i, 0))
    return pl.pallas_call(
        qkv_kernel,
        grid=(parts,),
        in_specs=[block(width), whole((1, width)), whole(weight.shape), table, table],
        out_specs=[block(width), block(2 * LANES), block(2 * LANES)],
        out_shape=[
            jax.ShapeDtypeStruct((parts, micro, rows, width), bf16),
            jax.ShapeDtypeStruct((parts, micro, rows, 2 * LANES), bf16),
            jax.ShapeDtypeStruct((parts, micro, rows, 2 * LANES), bf16),
        ],
        compiler_params=pltpu.CompilerParams(vmem_limit_bytes=VMEM_CAP),
        name="project_qkv",
    )(x_all, gain, weight, cos_row, sin_row)


def head_rows(values, head):
    key_head, member = head // 2, head % 2
    pair = values[:, key_head * LANES : (key_head + 1) * LANES]
    if member != key_head:
        pair = pltpu.roll(pair, HD, 1)
    lane = lax.broadcasted_iota(jnp.int32, pair.shape, 1)
    return jnp.where(lane // HD == key_head, pair, jnp.zeros_like(pair))


def join_heads(first, second, key_head):
    if key_head == 0:
        second = pltpu.roll(second, HD, 1)
    else:
        first = pltpu.roll(first, HD, 1)
    lane = lax.broadcasted_iota(jnp.int32, first.shape, 1)
    return jnp.where(lane < HD, first, second)


def allowed_keys(span, key_start, query_start, length):
    key_pos = key_start + lax.broadcasted_iota(jnp.int32, (span, span), 0)
    query_pos = query_start + lax.broadcasted_iota(jnp.int32, (span, span), 1)
    return (key_pos <= query_pos) & (key_pos < length)


def attend_kernel(info_ref, q_ref, kv_ref, out_ref, log_ref, heads, best, total, accum):
    m, j = pl.program_id(0), pl.program_id(1)
    last = pl.num_programs(1) - 1
    mine, length = info_ref[0], info_ref[1 + m]
    parts, _, rows, cols = q_ref.shape
    span = parts * rows
    count = 4

    @pl.when(j == 0)
    def _():
        values = q_ref[...].reshape(span, cols).astype(f32)
        for head in range(count):
            heads[head] = head_rows(values, head).astype(bf16)
        best[...] = jnp.full(best.shape, FILL, f32)
        total[...] = jnp.zeros(total.shape, f32)
        accum[...] = jnp.zeros(accum.shape, f32)

    def block(masked):
        keys = kv_ref[0].reshape(span, 2 * LANES)[:, :LANES]
        values_t = kv_ref[0].reshape(span, 2 * LANES)[:, LANES:].astype(f32).T.astype(bf16)
        if masked:
            allowed = allowed_keys(span, j * span, mine * span, length)
        for head in range(count):
            scores = dot_nt(keys, heads[head])
            if masked:
                scores = jnp.where(allowed, scores, FILL)
            old = best[head : head + 1]
            new = jnp.maximum(old, jnp.max(scores, axis=0, keepdims=True))
            factor = jnp.exp(old - new)
            weights = jnp.exp(scores - new)
            if masked:
                weights = jnp.where(allowed, weights, 0.0)
            best[head : head + 1] = new
            total[head : head + 1] = total[head : head + 1] * factor + jnp.sum(weights, axis=0, keepdims=True)
            accum[head] = accum[head] * factor + dot_nn(values_t, weights.astype(bf16))

    wanted = (j <= mine) & (mine * span < length) & (j * span < length)
    edge = (j == mine) | ((j + 1) * span > length)

    @pl.when(wanted & edge)
    def _():
        block(True)

    @pl.when(wanted & jnp.logical_not(edge))
    def _():
        block(False)

    @pl.when(j == last)
    def _():
        live = mine * span < length
        for key_head in range(2):
            pair = []
            for member in range(2):
                head = key_head * 2 + member
                sums = jnp.where(live, total[head : head + 1], 1.0)
                log_ref[0, head : head + 1] = best[head : head + 1] + jnp.log(sums)
                pair.append((accum[head] * (1.0 / sums)).T)
            joined = join_heads(pair[0], pair[1], key_head)
            out_ref[:, :, :, key_head * LANES : (key_head + 1) * LANES] = joined.astype(bf16).reshape(
                parts, 1, rows, LANES
            )


def attend(info, query, kv_all):
    parts, micro, rows, cols = query.shape
    blocks, span = kv_all.shape[0], parts * rows

    def kv_map(m, j, info_ref):
        return (jnp.minimum(j, info_ref[0]), 0, m, 0, 0)

    return pl.pallas_call(
        attend_kernel,
        grid_spec=pltpu.PrefetchScalarGridSpec(
            num_scalar_prefetch=1,
            grid=(micro, blocks),
            in_specs=[
                pl.BlockSpec((parts, 1, rows, cols), lambda m, j, info_ref: (0, m, 0, 0)),
                pl.BlockSpec((1, parts, 1, rows, 2 * LANES), kv_map),
            ],
            out_specs=[
                pl.BlockSpec((parts, 1, rows, cols), lambda m, j, info_ref: (0, m, 0, 0)),
                pl.BlockSpec((1, 8, span), lambda m, j, info_ref: (m, 0, 0)),
            ],
            scratch_shapes=[
                pltpu.VMEM((4, span, LANES), bf16),
                pltpu.VMEM((8, span), f32),
                pltpu.VMEM((8, span), f32),
                pltpu.VMEM((4, LANES, span), f32),
            ],
        ),
        out_shape=[
            jax.ShapeDtypeStruct(query.shape, bf16),
            jax.ShapeDtypeStruct((micro, 8, span), f32),
        ],
        compiler_params=pltpu.CompilerParams(vmem_limit_bytes=VMEM_CAP),
        name="attend",
    )(info, query, kv_all)


def attend_back_kernel(
    info_ref, q_ref, kv_ref, out_ref, log_ref, grad_ref, cos_ref, sin_ref, dq_ref, dkv_ref, heads, grads, delta, accum
):
    m, j = pl.program_id(0), pl.program_id(1)
    last = pl.num_programs(1) - 1
    mine, length = info_ref[0], info_ref[1 + m]
    parts, _, rows, cols = q_ref.shape
    span = parts * rows
    count = 4

    @pl.when(j == 0)
    def _():
        values = q_ref[...].reshape(span, cols).astype(f32)
        attended = out_ref[...].reshape(span, cols).astype(f32)
        grad = grad_ref[...].reshape(span, cols).astype(f32)
        product = grad * attended
        for head in range(count):
            heads[head] = head_rows(values, head).astype(bf16)
            grads[head] = head_rows(grad, head).astype(bf16)
            delta[head : head + 1] = jnp.sum(head_rows(product, head).T, axis=0, keepdims=True)
        accum[...] = jnp.zeros(accum.shape, f32)

    def block(masked):
        keys = kv_ref[0].reshape(span, 2 * LANES)[:, :LANES]
        values = kv_ref[0].reshape(span, 2 * LANES)[:, LANES:]
        keys_t = keys.astype(f32).T.astype(bf16)
        if masked:
            allowed = allowed_keys(span, j * span, mine * span, length)
        grad_keys = jnp.zeros((span, LANES), f32)
        grad_values = jnp.zeros((span, LANES), f32)
        for head in range(count):
            scores = dot_nt(keys, heads[head])
            probs = jnp.exp(scores - log_ref[0, head : head + 1])
            if masked:
                probs = jnp.where(allowed, probs, 0.0)
            grad_probs = dot_nt(values, grads[head])
            grad_scores = (probs * (grad_probs - delta[head : head + 1])).astype(bf16)
            grad_values = grad_values + dot_nn(probs.astype(bf16), grads[head])
            grad_keys = grad_keys + dot_nn(grad_scores, heads[head])
            accum[head] = accum[head] + dot_nn(keys_t, grad_scores)
        dkv_ref[0, :, :, :, 0:LANES] = grad_keys.astype(bf16).reshape(parts, 1, rows, LANES)
        dkv_ref[0, :, :, :, LANES : 2 * LANES] = grad_values.astype(bf16).reshape(parts, 1, rows, LANES)

    wanted = (j <= mine) & (mine * span < length) & (j * span < length)
    edge = (j == mine) | ((j + 1) * span > length)

    @pl.when(wanted & edge)
    def _():
        block(True)

    @pl.when(wanted & jnp.logical_not(edge))
    def _():
        block(False)

    @pl.when(jnp.logical_not(wanted))
    def _():
        dkv_ref[...] = jnp.zeros(dkv_ref.shape, bf16)

    @pl.when(j == last)
    def _():
        for key_head in range(2):
            pair = [accum[key_head * 2 + member].T for member in range(2)]
            joined = join_heads(pair[0], pair[1], key_head) * HD ** (-0.5)
            turned = joined * cos_ref[...] - swap_halves(joined) * sin_ref[...]
            dq_ref[:, :, :, key_head * LANES : (key_head + 1) * LANES] = turned.astype(bf16).reshape(
                parts, 1, rows, LANES
            )


def attend_back(info, query, kv_all, attended, log_total, grad, cos_row, sin_row):
    parts, micro, rows, cols = query.shape
    blocks, span = kv_all.shape[0], parts * rows

    def kv_map(m, j, info_ref):
        return (jnp.minimum(j, info_ref[0]), 0, m, 0, 0)

    row_spec = pl.BlockSpec((parts, 1, rows, cols), lambda m, j, info_ref: (0, m, 0, 0))
    table = pl.BlockSpec((span, LANES), lambda m, j, info_ref: (0, 0))
    return pl.pallas_call(
        attend_back_kernel,
        grid_spec=pltpu.PrefetchScalarGridSpec(
            num_scalar_prefetch=1,
            grid=(micro, blocks),
            in_specs=[
                row_spec,
                pl.BlockSpec((1, parts, 1, rows, 2 * LANES), kv_map),
                row_spec,
                pl.BlockSpec((1, 8, span), lambda m, j, info_ref: (m, 0, 0)),
                row_spec,
                table,
                table,
            ],
            out_specs=[
                row_spec,
                pl.BlockSpec((1, parts, 1, rows, 2 * LANES), lambda m, j, info_ref: (j, 0, m, 0, 0)),
            ],
            scratch_shapes=[
                pltpu.VMEM((4, span, LANES), bf16),
                pltpu.VMEM((4, span, LANES), bf16),
                pltpu.VMEM((8, span), f32),
                pltpu.VMEM((4, LANES, span), f32),
            ],
        ),
        out_shape=[
            jax.ShapeDtypeStruct(query.shape, bf16),
            jax.ShapeDtypeStruct(kv_all.shape, bf16),
        ],
        compiler_params=pltpu.CompilerParams(vmem_limit_bytes=VMEM_CAP),
        name="attend_back",
    )(info, query, kv_all, attended, log_total, grad, cos_row, sin_row)


def expert_kernel(
    x_ref, gm_ref, gates_ref, w_ref, mixed_ref, gin_ref, dw_ref, x_t, gm_t, mixed, gin, gate_sums, low_h, low_g, low_u
):
    step = pl.program_id(0)
    last = pl.num_programs(0) - 1
    rows, width = x_ref.shape
    wide = PAIR * LANES
    chunk = 256

    @pl.when(step == 0)
    def _():
        x_t[...] = x_ref[...].T
        gm_t[...] = gm_ref[...].T
        mixed[...] = jnp.zeros(mixed.shape, f32)
        gin[...] = jnp.zeros(gin.shape, f32)
        gate_sums[...] = jnp.zeros(gate_sums.shape, f32)

    w_gate_up = w_ref[:, : 2 * wide]
    w_down = w_ref[:, 2 * wide :]

    def rows_step(i, _):
        here = pl.ds(pl.multiple_of(i * chunk, chunk), chunk)
        pre = dot_nn(x_ref[here, :], w_gate_up)
        gate_pre, up_pre = pre[:, :wide], pre[:, wide:]
        back = dot_nn(gm_ref[here, :], w_down)
        sig = 1.0 / (1.0 + jnp.exp(-gate_pre))
        silu = gate_pre * sig
        hidden = silu * up_pre
        lane = lax.broadcasted_iota(jnp.int32, (chunk, LANES), 1)
        product = hidden * back
        spread = []
        sums = gate_sums[here, :]
        for member in range(PAIR):
            hit = lane == step * PAIR + member
            gate = jnp.sum(jnp.where(hit, gates_ref[here, :], 0.0), axis=1, keepdims=True)
            spread.append(jnp.broadcast_to(gate, (chunk, LANES)))
            amount = jnp.sum(product[:, member * LANES : (member + 1) * LANES], axis=1, keepdims=True)
            sums = sums + jnp.where(hit, amount, 0.0)
        gate_sums[here, :] = sums
        gates = jnp.concatenate(spread, axis=1)
        grad_hidden = gates * back
        low_hidden = (gates * hidden).astype(bf16)
        grad_up = (grad_hidden * silu).astype(bf16)
        grad_gate = (grad_hidden * up_pre * (sig * (1.0 + gate_pre * (1.0 - sig)))).astype(bf16)
        low_h[here, :] = low_hidden
        low_g[here, 0:wide] = grad_gate
        low_g[here, wide : 2 * wide] = grad_up
        mixed[here, :] += dot_nt(low_hidden, w_down)
        gin[here, :] += dot_nt(low_g[here, :], w_gate_up)
        return 0

    lax.fori_loop(0, rows // chunk, rows_step, 0)

    def weight_step(i, _):
        here = pl.ds(pl.multiple_of(i * chunk, chunk), chunk)
        dw_ref[here, 0 : 2 * wide] = dot_nn(x_t[here, :], low_g[...]).astype(bf16)
        dw_ref[here, 2 * wide : 3 * wide] = dot_nn(gm_t[here, :], low_h[...]).astype(bf16)
        return 0

    lax.fori_loop(0, width // chunk, weight_step, 0)

    @pl.when(step == last)
    def _():
        mixed_ref[...] = mixed[...].astype(bf16)
        gin_ref[:, 0:width] = gin[...].astype(bf16)
        gin_ref[:, width : width + LANES] = gate_sums[...].astype(bf16)


def experts_both(x_all, gm_all, gates, weight):
    rows, width = x_all.shape
    wide = PAIR * LANES
    steps = weight.shape[1] // (3 * wide)
    whole = lambda cols: pl.BlockSpec((rows, cols), lambda i: (0, 0))
    part = pl.BlockSpec((width, 3 * wide), lambda i: (0, i))
    return pl.pallas_call(
        expert_kernel,
        grid=(steps,),
        in_specs=[whole(width), whole(width), whole(LANES), part],
        out_specs=[whole(width), whole(width + LANES), part],
        out_shape=[
            jax.ShapeDtypeStruct((rows, width), bf16),
            jax.ShapeDtypeStruct((rows, width + LANES), bf16),
            jax.ShapeDtypeStruct(weight.shape, bf16),
        ],
        scratch_shapes=[
            pltpu.VMEM((width, rows), bf16),
            pltpu.VMEM((width, rows), bf16),
            pltpu.VMEM((rows, width), f32),
            pltpu.VMEM((rows, width), f32),
            pltpu.VMEM((rows, LANES), f32),
            pltpu.VMEM((rows, wide), bf16),
            pltpu.VMEM((rows, 2 * wide), bf16),
            pltpu.VMEM((rows, 2 * wide), bf16),
        ],
        compiler_params=pltpu.CompilerParams(vmem_limit_bytes=VMEM_CAP),
        name="experts",
    )(x_all, gm_all, gates, weight)


def norm_scale(values):
    return lax.rsqrt(jnp.mean(values * values, axis=-1, keepdims=True) + EPS)


def norm_back(values, inverse, gain, grad):
    weighted = grad * gain
    inner = jnp.mean(weighted * values, axis=-1, keepdims=True)
    grad_values = inverse * weighted - values * (inverse * inverse * inverse) * inner
    return grad_values, jnp.sum((grad * values * inverse).reshape(-1, values.shape[-1]), axis=0)


def gates_of(logits, picked):
    shifted = jnp.where(picked, logits, FILL)
    peak = jnp.max(shifted, axis=-1, keepdims=True)
    exps = jnp.where(picked, jnp.exp(shifted - peak), 0.0)
    return exps / jnp.sum(exps, axis=-1, keepdims=True)


def gather_tp(values):
    return lax.all_gather(values, "tp", axis=0, tiled=False)


def scatter_tp(values):
    return lax.psum_scatter(values, "tp", scatter_dimension=0, tiled=False)


def local(
    inputs,
    cotangent,
    lengths,
    routes,
    attn_gain,
    moe_gain,
    router_weight,
    query_weight,
    key_weight,
    value_weight,
    output_weight,
    gate_weight,
    up_weight,
    down_weight,
):
    tensor_count = lax.axis_size("tp")
    tensor_rank = lax.axis_index("tp")
    shard_rank = lax.axis_index("fsdp")
    micro, rows, width = inputs.shape
    span = rows * tensor_count
    experts, shard_width, hidden = gate_weight.shape
    total_rows = tensor_count * micro * rows

    small = jnp.concatenate([attn_gain[:, None], moe_gain[:, None], router_weight], axis=1)
    small_all = lax.all_gather(small, ("fsdp", "tp"), axis=0, tiled=True)
    gain_attn = small_all[:, 0].astype(f32)
    gain_moe = small_all[:, 1].astype(f32)
    router_full = small_all[:, 2:]
    attn_local = jnp.concatenate([query_weight, key_weight, value_weight, output_weight.T], axis=1)
    attn_full = lax.all_gather(attn_local, "fsdp", axis=0, tiled=True)
    qkv_cols = attn_local.shape[1] - output_weight.shape[0]
    qkv_full, out_full = attn_full[:, :qkv_cols], attn_full[:, qkv_cols:]
    stacked = jnp.stack(
        [gate_weight.transpose(1, 0, 2), up_weight.transpose(1, 0, 2), down_weight.transpose(2, 0, 1)], axis=1
    )
    expert_local = (
        stacked.reshape(shard_width, 3, experts // PAIR, PAIR, hidden)
        .transpose(0, 2, 1, 3, 4)
        .reshape(shard_width, 3 * experts * hidden)
    )
    expert_full = lax.all_gather(expert_local, "fsdp", axis=0, tiled=True)

    span_pos = shard_rank * span + jnp.arange(span, dtype=jnp.int32)
    row_pos = shard_rank * span + tensor_rank * rows + jnp.arange(rows, dtype=jnp.int32)
    cos_row, sin_row = rope_tables(span_pos)
    info = jnp.concatenate([jnp.reshape(shard_rank, (1,)).astype(jnp.int32), lengths])
    valid = (row_pos[None, :] < lengths[:, None]).astype(f32)[:, :, None]
    grad_out = cotangent.astype(f32) * valid
    grad_mixed = gather_tp(grad_out.astype(bf16)).reshape(total_rows, width)

    x_all = gather_tp(inputs)
    normed_all, query, kv = project_qkv(x_all, gain_attn[None, :], qkv_full, cos_row, sin_row)
    kv_all = lax.all_gather(kv, "fsdp", axis=0, tiled=False)
    attended, log_total = attend(info, query, kv_all)
    attended_rows = attended.reshape(total_rows, -1)
    attn_part = dot_nt(attended_rows, out_full).astype(bf16).reshape(tensor_count, micro, rows, width)
    residual = inputs.astype(f32)
    middle = residual + scatter_tp(attn_part).astype(f32)
    inverse_moe = norm_scale(middle)
    normed_moe = (middle * inverse_moe * gain_moe).astype(bf16)
    moe_all = gather_tp(normed_moe).reshape(total_rows, width)

    expert_ids = jnp.arange(experts, dtype=jnp.int32)
    picked = jnp.any(routes[:, :, :, None] == expert_ids, axis=2)
    picked_all = picked.reshape(micro, tensor_count, rows, experts).transpose(1, 0, 2, 3).reshape(total_rows, experts)
    logits = dot_nn(moe_all, router_full)
    gates = gates_of(logits, picked_all)
    gates_wide = jnp.pad(gates, ((0, 0), (0, LANES - experts)))
    mixed_part, gin_part, expert_grad = experts_both(moe_all, grad_mixed, gates_wide, expert_full)
    expert_sum = lax.psum_scatter(expert_grad, "fsdp", scatter_dimension=0, tiled=True)

    gin_own = scatter_tp(gin_part.reshape(tensor_count, micro, rows, width + LANES)).astype(f32)
    mixed = scatter_tp(mixed_part.reshape(tensor_count, micro, rows, width)).astype(f32)
    outputs = ((middle + mixed) * valid).astype(bf16)

    gates_own = lax.dynamic_index_in_dim(gates.reshape(tensor_count, micro * rows, experts), tensor_rank, 0, False)
    gate_grads = gin_own[..., width : width + experts].reshape(micro * rows, experts)
    grad_logits = gates_own * (gate_grads - jnp.sum(gates_own * gate_grads, axis=-1, keepdims=True))
    grad_logits = grad_logits.astype(bf16)
    moe_rows = normed_moe.reshape(micro * rows, width)
    router_grad = lax.dot_general(moe_rows, grad_logits, (((0,), (0,)), ((), ())), preferred_element_type=f32)
    grad_moe = gin_own[..., :width] + dot_nt(grad_logits, router_full).reshape(micro, rows, width)
    grad_norm, gain_moe_part = norm_back(middle, inverse_moe, gain_moe, grad_moe)
    grad_middle = grad_out + grad_norm
    grad_attn = gather_tp(grad_middle.astype(bf16)).reshape(total_rows, width)
    grad_attended = dot_nn(grad_attn, out_full).astype(bf16).reshape(query.shape)
    out_grad = lax.dot_general(grad_attn, attended_rows, (((0,), (0,)), ((), ())), preferred_element_type=f32)
    dq, dkv = attend_back(info, query, kv_all, attended, log_total, grad_attended, cos_row, sin_row)
    dkv_own = lax.psum_scatter(dkv, "fsdp", scatter_dimension=0, tiled=False)
    half = HD // 2
    dk = dkv_own[..., :LANES].astype(f32)
    dk_swapped = dk.reshape(dk.shape[:-1] + (2, 2, half))[..., ::-1, :].reshape(dk.shape)
    table = lambda t: t.reshape(tensor_count, 1, rows, LANES)
    dk = (dk * table(cos_row) - dk_swapped * table(sin_row)).astype(bf16)
    grads = jnp.concatenate([dq, dk, dkv_own[..., LANES:]], axis=-1).reshape(total_rows, qkv_cols)
    qkv_grad = lax.dot_general(
        normed_all.reshape(total_rows, width), grads, (((0,), (0,)), ((), ())), preferred_element_type=f32
    )
    normed_part = dot_nt(grads, qkv_full).astype(bf16).reshape(tensor_count, micro, rows, width)
    grad_normed = scatter_tp(normed_part).astype(f32)
    inverse_attn = norm_scale(residual)
    grad_residual, gain_attn_part = norm_back(residual, inverse_attn, gain_attn, grad_normed)
    input_grad = grad_middle + grad_residual

    attn_grad = jnp.concatenate([qkv_grad.astype(bf16), out_grad.astype(bf16)], axis=1)
    attn_sum = lax.psum_scatter(attn_grad, "fsdp", scatter_dimension=0, tiled=True).astype(f32)
    small_part = jnp.concatenate([gain_attn_part[:, None], gain_moe_part[:, None], router_grad], axis=1)
    small_sum = lax.psum_scatter(small_part, ("fsdp", "tp"), scatter_dimension=0, tiled=True)
    split = (
        expert_sum.reshape(shard_width, experts // PAIR, 3, PAIR, hidden)
        .transpose(2, 1, 3, 0, 4)
        .reshape(3, experts, shard_width, hidden)
    )
    q_cols, k_cols = query_weight.shape[1], key_weight.shape[1]
    return (
        outputs,
        input_grad,
        small_sum[:, 0],
        small_sum[:, 1],
        small_sum[:, 2:],
        attn_sum[:, :q_cols],
        attn_sum[:, q_cols : q_cols + k_cols],
        attn_sum[:, q_cols + k_cols : qkv_cols],
        attn_sum[:, qkv_cols:].T,
        split[0].astype(f32),
        split[1].astype(f32),
        split[2].transpose(0, 2, 1).astype(f32),
    )


def solution(mesh):
    rows_spec = P(None, ("fsdp", "tp"), None)
    small_specs = (P(("fsdp", "tp")), P(("fsdp", "tp")), P(("fsdp", "tp"), None))
    weight_specs = (
        P("fsdp", "tp"),
        P("fsdp", "tp"),
        P("fsdp", "tp"),
        P("tp", "fsdp"),
        P(None, "fsdp", "tp"),
        P(None, "fsdp", "tp"),
        P(None, "tp", "fsdp"),
    )
    in_specs = (rows_spec, rows_spec, P(), P(None, "fsdp", None)) + small_specs + weight_specs
    out_specs = (rows_spec, rows_spec) + small_specs + weight_specs
    return jax.shard_map(local, mesh=mesh, in_specs=in_specs, out_specs=out_specs, check_vma=False)
```

```python
import functools

import jax
import jax.numpy as jnp
from jax import lax
from jax.experimental import pallas as pl
from jax.experimental.pallas import tpu as pltpu
from jax.sharding import PartitionSpec as P

HD = 64
LANES = 128
PAIR = 2
EPS = 1e-06
FILL = -1e30
THETA = 10000.0
VMEM_CAP = 60 * 1024 * 1024
f32 = jnp.float32
bf16 = jnp.bfloat16


def dot_nn(a, b):
    return lax.dot_general(a, b, (((1,), (0,)), ((), ())), preferred_element_type=f32)


def dot_nt(a, b):
    return lax.dot_general(a, b, (((1,), (1,)), ((), ())), preferred_element_type=f32)


def swap_halves(values):
    lane = lax.broadcasted_iota(jnp.int32, values.shape, values.ndim - 1)
    ahead = pltpu.roll(values, values.shape[-1] - HD // 2, values.ndim - 1)
    back = pltpu.roll(values, HD // 2, values.ndim - 1)
    return jnp.where(lane % HD < HD // 2, ahead, back)


def rope_tables(positions):
    half = HD // 2
    freqs = THETA ** (-jnp.arange(half, dtype=f32) * 2.0 / HD)
    angles = positions.astype(f32)[:, None] * freqs[None, :]
    cosine, sine = jnp.cos(angles), jnp.sin(angles)
    cos_row = jnp.concatenate([cosine] * 4, axis=1)
    sin_row = jnp.concatenate([-sine, sine] * 2, axis=1)
    return cos_row, sin_row


def head_rows(values, head):
    key_head, member = head // 2, head % 2
    pair = values[:, key_head * LANES : (key_head + 1) * LANES]
    if member != key_head:
        pair = pltpu.roll(pair, HD, 1)
    lane = lax.broadcasted_iota(jnp.int32, pair.shape, 1)
    return jnp.where(lane // HD == key_head, pair, jnp.zeros_like(pair))


def join_heads(first, second, key_head):
    if key_head == 0:
        second = pltpu.roll(second, HD, 1)
    else:
        first = pltpu.roll(first, HD, 1)
    lane = lax.broadcasted_iota(jnp.int32, first.shape, 1)
    return jnp.where(lane < HD, first, second)


def cost(microseconds):
    return pl.CostEstimate(flops=int(microseconds * 9e8), bytes_accessed=1024, transcendentals=0)


def params():
    return pltpu.CompilerParams(vmem_limit_bytes=VMEM_CAP)


def shape(dims, kind):
    return jax.ShapeDtypeStruct(dims, kind)


def normalised(x, gain):
    inverse = lax.rsqrt(jnp.mean(x * x, axis=-1, keepdims=True) + EPS)
    unit = x * inverse
    return inverse, unit, unit * gain


def qkv_kernel(*refs):
    x_refs = refs[:-6]
    gain_ref, w_ref, cos_ref, sin_ref, q_ref, kv_ref = refs[-6:]
    rows = x_refs[0].shape[0]
    for slot, x_ref in enumerate(x_refs):
        here = slice(slot * rows, (slot + 1) * rows)
        cos_row, sin_row = cos_ref[here, :], sin_ref[here, :]
        _, _, normed = normalised(x_ref[...].astype(f32), gain_ref[...])
        pre = dot_nn(normed.astype(bf16), w_ref[...])
        for part in range(3):
            cols = pre[:, part * LANES : (part + 1) * LANES]
            turned = cols * cos_row + swap_halves(cols) * sin_row
            if part < 2:
                q_ref[here, part * LANES : (part + 1) * LANES] = (turned * HD ** (-0.5)).astype(bf16)
            else:
                kv_ref[here, 0:LANES] = turned.astype(bf16)
        kv_ref[here, LANES : 2 * LANES] = pre[:, 3 * LANES : 4 * LANES].astype(bf16)


def project_qkv(x_slots, gain, weight, cos_row, sin_row):
    span = cos_row.shape[0]
    return pl.pallas_call(
        qkv_kernel,
        out_shape=[shape((span, 2 * LANES), bf16), shape((span, 2 * LANES), bf16)],
        compiler_params=params(),
        cost_estimate=cost(3),
        name="project_qkv",
    )(*x_slots, gain, weight, cos_row, sin_row)


def reversed_bits(index, count):
    result, bit = 0, 1
    while bit < count:
        result = result + ((index // bit) % 2) * (count // (2 * bit))
        bit *= 2
    return result


def places(rank, rows, dims, axis):
    index = lax.broadcasted_iota(jnp.int32, dims, axis)
    return (rank ^ (index // rows)) * rows + index % rows


def allowed_keys(rank, rows, span, key_start, query_start, length):
    key_pos = key_start + places(rank, rows, (span, span), 0)
    query_pos = query_start + places(rank, rows, (span, span), 1)
    return (key_pos <= query_pos) & (key_pos < length)


def block_kind(info_ref, j, span, count):
    mine, length = info_ref[0], info_ref[2]
    other = mine ^ reversed_bits(j, count)
    wanted = (other <= mine) & (mine * span < length) & (other * span < length)
    edge = (other == mine) | ((other + 1) * span > length)
    return other, wanted, edge


def attend_kernel(info_ref, q_ref, kv_ref, *refs):
    heads, best, total, accum = refs[-4:]
    out_refs, log_ref = refs[:-5], refs[-5]
    j = pl.program_id(0)
    count = pl.num_programs(0)
    mine, rank, length = info_ref[0], info_ref[1], info_ref[2]
    rows = out_refs[0].shape[0]
    span = q_ref.shape[0]
    other, wanted, edge = block_kind(info_ref, j, span, BLOCKS[0])

    @pl.when(j == 0)
    def _():
        values = q_ref[...].astype(f32)
        for head in range(4):
            heads[head] = head_rows(values, head).astype(bf16)
        best[...] = jnp.full(best.shape, FILL, f32)
        total[...] = jnp.zeros(total.shape, f32)
        accum[...] = jnp.zeros(accum.shape, f32)

    def block(masked):
        keys = kv_ref[0, :, :LANES]
        values_t = kv_ref[0, :, LANES:].astype(f32).T.astype(bf16)
        if masked:
            allowed = allowed_keys(rank, rows, span, other * span, mine * span, length)
        for head in range(4):
            scores = dot_nt(keys, heads[head])
            if masked:
                scores = jnp.where(allowed, scores, FILL)
            old = best[head : head + 1]
            new = jnp.maximum(old, jnp.max(scores, axis=0, keepdims=True))
            factor = jnp.exp(old - new)
            weights = jnp.exp(scores - new)
            if masked:
                weights = jnp.where(allowed, weights, 0.0)
            best[head : head + 1] = new
            total[head : head + 1] = total[head : head + 1] * factor + jnp.sum(weights, axis=0, keepdims=True)
            accum[head] = accum[head] * factor + dot_nn(values_t, weights.astype(bf16))

    @pl.when(wanted & edge)
    def _():
        block(True)

    @pl.when(wanted & jnp.logical_not(edge))
    def _():
        block(False)

    @pl.when(j == count - 1)
    def _():
        live = mine * span < length
        for key_head in range(2):
            pair = []
            for member in range(2):
                head = key_head * 2 + member
                sums = jnp.where(live, total[head : head + 1], 1.0)
                log_ref[head : head + 1] = best[head : head + 1] + jnp.log(sums)
                pair.append((accum[head] * (1.0 / sums)).T)
            joined = join_heads(pair[0], pair[1], key_head).astype(bf16)
            for slot, out_ref in enumerate(out_refs):
                out_ref[:, key_head * LANES : (key_head + 1) * LANES] = joined[slot * rows : (slot + 1) * rows]


BLOCKS = [0]


def attend(info, query, kv_all, rows):
    span, cols = query.shape
    blocks = kv_all.shape[0]
    slots = span // rows
    BLOCKS[0] = blocks
    return pl.pallas_call(
        attend_kernel,
        grid_spec=pltpu.PrefetchScalarGridSpec(
            num_scalar_prefetch=1,
            grid=(blocks,),
            in_specs=[
                pl.BlockSpec((span, cols), lambda j, info_ref: (0, 0)),
                pl.BlockSpec((1, span, 2 * LANES), lambda j, info_ref: (j, 0, 0)),
            ],
            out_specs=[pl.BlockSpec((rows, cols), lambda j, info_ref: (0, 0))] * slots
            + [pl.BlockSpec((8, span), lambda j, info_ref: (0, 0))],
            scratch_shapes=[
                pltpu.VMEM((4, span, LANES), bf16),
                pltpu.VMEM((8, span), f32),
                pltpu.VMEM((8, span), f32),
                pltpu.VMEM((4, LANES, span), f32),
            ],
        ),
        out_shape=[shape((rows, cols), bf16)] * slots + [shape((8, span), f32)],
        compiler_params=params(),
        cost_estimate=cost(12),
        name="attend",
    )(info, query, kv_all)


def attend_back_kernel(slots, info_ref, q_ref, kv_ref, log_ref, cos_ref, sin_ref, *refs):
    out_refs, grad_refs = refs[:slots], refs[slots : 2 * slots]
    dq_ref, keep_ref, send_ref, heads, grads, delta, accum, dkv = refs[2 * slots :]
    j = pl.program_id(0)
    count = pl.num_programs(0)
    mine, rank, length = info_ref[0], info_ref[1], info_ref[2]
    span, cols = q_ref.shape
    rows = span // slots
    other, wanted, edge = block_kind(info_ref, j, span, BLOCKS[0])

    @pl.when(j == 0)
    def _():
        values = q_ref[...].astype(f32)
        attended = jnp.concatenate([ref[...] for ref in out_refs], axis=0).astype(f32)
        grad = jnp.concatenate([ref[...] for ref in grad_refs], axis=0).astype(f32)
        product = grad * attended
        for head in range(4):
            heads[head] = head_rows(values, head).astype(bf16)
            grads[head] = head_rows(grad, head).astype(bf16)
            delta[head : head + 1] = jnp.sum(head_rows(product, head).T, axis=0, keepdims=True)
        accum[...] = jnp.zeros(accum.shape, f32)

    def block(masked):
        keys = kv_ref[0, :, :LANES]
        values = kv_ref[0, :, LANES:]
        keys_t = keys.astype(f32).T.astype(bf16)
        if masked:
            allowed = allowed_keys(rank, rows, span, other * span, mine * span, length)
        grad_keys = jnp.zeros((span, LANES), f32)
        grad_values = jnp.zeros((span, LANES), f32)
        for head in range(4):
            scores = dot_nt(keys, heads[head])
            probs = jnp.exp(scores - log_ref[head : head + 1])
            if masked:
                probs = jnp.where(allowed, probs, 0.0)
            grad_probs = dot_nt(values, grads[head])
            grad_scores = (probs * (grad_probs - delta[head : head + 1])).astype(bf16)
            grad_values = grad_values + dot_nn(probs.astype(bf16), grads[head])
            grad_keys = grad_keys + dot_nn(grad_scores, heads[head])
            accum[head] = accum[head] + dot_nn(keys_t, grad_scores)
        dkv[:, 0:LANES] = grad_keys.astype(bf16)
        dkv[:, LANES : 2 * LANES] = grad_values.astype(bf16)

    @pl.when(wanted & edge)
    def _():
        block(True)

    @pl.when(wanted & jnp.logical_not(edge))
    def _():
        block(False)

    @pl.when(jnp.logical_not(wanted))
    def _():
        dkv[...] = jnp.zeros(dkv.shape, bf16)

    @pl.when(j < count // 2)
    def _():
        keep_ref[0] = dkv[...]

    @pl.when(j >= count // 2)
    def _():
        send_ref[0] = dkv[...]

    @pl.when(j == count - 1)
    def _():
        for key_head in range(2):
            pair = [accum[key_head * 2 + member].T for member in range(2)]
            joined = join_heads(pair[0], pair[1], key_head) * HD ** (-0.5)
            turned = joined * cos_ref[...] - swap_halves(joined) * sin_ref[...]
            dq_ref[:, key_head * LANES : (key_head + 1) * LANES] = turned.astype(bf16)


def attend_back(info, query, kv_all, log_total, cos_row, sin_row, att_slots, grad_slots):
    span, cols = query.shape
    blocks, slots = kv_all.shape[0], len(att_slots)
    rows, half = span // slots, blocks // 2
    BLOCKS[0] = blocks
    fixed = lambda *dims: pl.BlockSpec(dims, lambda j, info_ref: (0,) * len(dims))
    return pl.pallas_call(
        functools.partial(attend_back_kernel, slots),
        grid_spec=pltpu.PrefetchScalarGridSpec(
            num_scalar_prefetch=1,
            grid=(blocks,),
            in_specs=[
                fixed(span, cols),
                pl.BlockSpec((1, span, 2 * LANES), lambda j, info_ref: (j, 0, 0)),
                fixed(8, span),
                fixed(span, LANES),
                fixed(span, LANES),
            ]
            + [fixed(rows, cols)] * (2 * slots),
            out_specs=[
                fixed(span, cols),
                pl.BlockSpec((1, span, 2 * LANES), lambda j, info_ref: (jnp.minimum(j, half - 1), 0, 0)),
                pl.BlockSpec((1, span, 2 * LANES), lambda j, info_ref: (jnp.maximum(j - half, 0), 0, 0)),
            ],
            scratch_shapes=[
                pltpu.VMEM((4, span, LANES), bf16),
                pltpu.VMEM((4, span, LANES), bf16),
                pltpu.VMEM((8, span), f32),
                pltpu.VMEM((4, LANES, span), f32),
                pltpu.VMEM((span, 2 * LANES), bf16),
            ],
        ),
        out_shape=[shape((span, cols), bf16)] + [shape((half, span, 2 * LANES), bf16)] * 2,
        compiler_params=params(),
        cost_estimate=cost(18),
        name="attend_back",
    )(info, query, kv_all, log_total, cos_row, sin_row, *att_slots, *grad_slots)


def middle_kernel(x_ref, gain_ref, w_ref, *refs):
    att_refs, (att_all, middle_ref, normed_ref) = refs[:-3], refs[-3:]
    cols = att_refs[0].shape[1]
    for slot, att_ref in enumerate(att_refs):
        att_all[:, slot * cols : (slot + 1) * cols] = att_ref[...]
    middle = x_ref[...].astype(f32) + dot_nt(att_all[...], w_ref[...])
    middle_ref[...] = middle
    normed_ref[...] = normalised(middle, gain_ref[...])[2].astype(bf16)


def close_attention(x, gain, weight, att_slots):
    rows, width = x.shape
    return pl.pallas_call(
        middle_kernel,
        out_shape=[shape((rows, weight.shape[1]), bf16), shape((rows, width), f32), shape((rows, width), bf16)],
        compiler_params=params(),
        cost_estimate=cost(2),
        name="middle",
    )(x, gain, weight, *att_slots)


def expert_kernel(slots, info_ref, routes_ref, router_ref, w_ref, *refs):
    x_refs, gm_refs = refs[:slots], refs[slots : 2 * slots]
    gin_refs, mixed_refs = refs[2 * slots : 3 * slots], refs[3 * slots : 4 * slots]
    gates_ref, low_g, low_h, x_all, gm_all, gates, mixed, gin, gate_sums = refs[4 * slots :]
    step = pl.program_id(0)
    last = pl.num_programs(0) - 1
    span, width = x_all.shape
    rows = span // slots
    wide = PAIR * LANES
    chunk = 256
    rank = info_ref[1]

    @pl.when(step == 0)
    def _():
        lane = lax.broadcasted_iota(jnp.int32, (rows, LANES), 1)
        for slot in range(slots):
            here = slice(slot * rows, (slot + 1) * rows)
            x_all[here, :] = x_refs[slot][...]
            gm_all[here, :] = gm_refs[slot][...]
            named = routes_ref[pl.ds(pl.multiple_of((rank ^ slot) * rows, rows), rows), :]
            picked = lane == named[:, 0:1]
            for k in range(1, named.shape[1]):
                picked = picked | (lane == named[:, k : k + 1])
            logits = jnp.where(picked, dot_nn(x_refs[slot][...], router_ref[...]), FILL)
            peak = jnp.max(logits, axis=1, keepdims=True)
            exps = jnp.where(picked, jnp.exp(logits - peak), 0.0)
            gates[here, :] = exps / jnp.sum(exps, axis=1, keepdims=True)
        gates_ref[...] = gates[0:rows, :]
        mixed[...] = jnp.zeros(mixed.shape, f32)
        gin[...] = jnp.zeros(gin.shape, f32)
        gate_sums[...] = jnp.zeros(gate_sums.shape, f32)

    def rows_step(i, _):
        here = pl.ds(pl.multiple_of(i * chunk, chunk), chunk)
        pre = dot_nn(x_all[here, :], w_ref[:, : 2 * wide])
        gate_pre, up_pre = pre[:, :wide], pre[:, wide:]
        back = dot_nn(gm_all[here, :], w_ref[:, 2 * wide :])
        sig = 1.0 / (1.0 + jnp.exp(-gate_pre))
        silu = gate_pre * sig
        hidden = silu * up_pre
        lane = lax.broadcasted_iota(jnp.int32, (chunk, LANES), 1)
        product = hidden * back
        spread = []
        sums = gate_sums[here, :]
        for member in range(PAIR):
            hit = lane == step * PAIR + member
            gate = jnp.sum(jnp.where(hit, gates[here, :], 0.0), axis=1, keepdims=True)
            spread.append(jnp.broadcast_to(gate, (chunk, LANES)))
            amount = jnp.sum(product[:, member * LANES : (member + 1) * LANES], axis=1, keepdims=True)
            sums = sums + jnp.where(hit, amount, 0.0)
        gate_sums[here, :] = sums
        factor = jnp.concatenate(spread, axis=1)
        grad_hidden = factor * back
        low_hidden = (factor * hidden).astype(bf16)
        grad_up = (grad_hidden * silu).astype(bf16)
        grad_gate = (grad_hidden * up_pre * (sig * (1.0 + gate_pre * (1.0 - sig)))).astype(bf16)
        low_h[here, :] = low_hidden
        low_g[here, 0:wide] = grad_gate
        low_g[here, wide : 2 * wide] = grad_up
        mixed[here, :] += dot_nt(low_hidden, w_ref[:, 2 * wide :])
        gin[here, :] += dot_nt(low_g[here, :], w_ref[:, : 2 * wide])
        return 0

    lax.fori_loop(0, span // chunk, rows_step, 0)

    @pl.when(step == last)
    def _():
        for slot in range(slots):
            here = slice(slot * rows, (slot + 1) * rows)
            mixed_refs[slot][...] = mixed[here, :].astype(bf16)
            gin_refs[slot][:, 0:width] = gin[here, :].astype(bf16)
            gin_refs[slot][:, width : width + LANES] = gate_sums[here, :].astype(bf16)


def experts_both(info, routes, router, weight, x_slots, gm_slots):
    rows, width = x_slots[0].shape
    slots = len(x_slots)
    span = rows * slots
    wide = PAIR * LANES
    steps = weight.shape[1] // (3 * wide)
    fixed = lambda *dims: pl.BlockSpec(dims, lambda i, info_ref: (0,) * len(dims))
    moving = lambda height, cols: pl.BlockSpec((height, cols), lambda i, info_ref: (0, i))
    return pl.pallas_call(
        functools.partial(expert_kernel, slots),
        grid_spec=pltpu.PrefetchScalarGridSpec(
            num_scalar_prefetch=1,
            grid=(steps,),
            in_specs=[fixed(*routes.shape), fixed(*router.shape), moving(width, 3 * wide)]
            + [fixed(rows, width)] * (2 * slots),
            out_specs=[fixed(rows, width + LANES)] * slots
            + [fixed(rows, width)] * slots
            + [fixed(rows, LANES), moving(span, 2 * wide), moving(span, wide)],
            scratch_shapes=[
                pltpu.VMEM((span, width), bf16),
                pltpu.VMEM((span, width), bf16),
                pltpu.VMEM((span, LANES), f32),
                pltpu.VMEM((span, width), f32),
                pltpu.VMEM((span, width), f32),
                pltpu.VMEM((span, LANES), f32),
            ],
        ),
        out_shape=[shape((rows, width + LANES), bf16)] * slots
        + [shape((rows, width), bf16)] * slots
        + [shape((rows, LANES), f32), shape((span, steps * 2 * wide), bf16), shape((span, steps * wide), bf16)],
        compiler_params=params(),
        cost_estimate=cost(24),
        name="experts",
    )(info, routes, router, weight, *x_slots, *gm_slots)


def expert_grad_kernel(micro, slots, *refs):
    count = micro * slots
    x_refs, gm_refs = refs[:count], refs[count : 2 * count]
    g_refs, h_refs = refs[2 * count : 2 * count + micro], refs[2 * count + micro : 2 * count + 2 * micro]
    dw_ref, x_t, gm_t = refs[2 * count + 2 * micro :]
    rows = x_refs[0].shape[0]
    width = x_t.shape[0]
    wide = PAIR * LANES
    chunk = 256

    @pl.when(pl.program_id(0) == 0)
    def _():
        for i in range(count):
            x_t[:, i * rows : (i + 1) * rows] = x_refs[i][...].T
            gm_t[:, i * rows : (i + 1) * rows] = gm_refs[i][...].T

    def weight_step(i, _):
        here = pl.ds(pl.multiple_of(i * chunk, chunk), chunk)
        g_sum, h_sum = 0.0, 0.0
        for m in range(micro):
            part = slice(m * slots * rows, (m + 1) * slots * rows)
            g_sum = g_sum + dot_nn(x_t[here, part], g_refs[m][...])
            h_sum = h_sum + dot_nn(gm_t[here, part], h_refs[m][...])
        dw_ref[here, 0 : 2 * wide] = g_sum.astype(bf16)
        dw_ref[here, 2 * wide : 3 * wide] = h_sum.astype(bf16)
        return 0

    lax.fori_loop(0, width // chunk, weight_step, 0)


def expert_grads(x_slots, gm_slots, lows_g, lows_h):
    micro, slots = len(x_slots), len(x_slots[0])
    rows, width = x_slots[0][0].shape
    span = rows * slots
    wide = PAIR * LANES
    steps = lows_h[0].shape[1] // wide
    fixed = pl.BlockSpec((rows, width), lambda i: (0, 0))
    moving = lambda height, cols: pl.BlockSpec((height, cols), lambda i: (0, i))
    flat = [block for part in x_slots for block in part] + [block for part in gm_slots for block in part]
    return pl.pallas_call(
        functools.partial(expert_grad_kernel, micro, slots),
        grid=(steps,),
        in_specs=[fixed] * len(flat) + [moving(span, 2 * wide)] * micro + [moving(span, wide)] * micro,
        out_specs=moving(width, 3 * wide),
        out_shape=shape((width, steps * 3 * wide), bf16),
        scratch_shapes=[pltpu.VMEM((width, micro * span), bf16), pltpu.VMEM((width, micro * span), bf16)],
        compiler_params=params(),
        cost_estimate=cost(22),
        name="expert_grads",
    )(*flat, *lows_g, *lows_h)


def moe_back_kernel(
    slots, info_ref, p0, p1, p2, gates_ref, router_ref, middle_ref, normed_ref, gain_ref, cot_ref, w_ref, *refs
):
    grad_middle_ref, grad_attn_ref, sums_ref = refs[:3]
    out_refs = refs[3:]
    rows, width = middle_ref.shape
    gate = lambda ref: ref[:, width : width + LANES].astype(f32)
    gates = gates_ref[...]
    gate_grads = gate(p0) + gate(p1) + gate(p2)
    grad_logits = gates * (gate_grads - jnp.sum(gates * gate_grads, axis=1, keepdims=True))
    grad_logits = grad_logits.astype(bf16)
    main = lambda ref: ref[:, 0:width].astype(f32)
    grad_moe = main(p0) + main(p1) + main(p2) + dot_nt(grad_logits, router_ref[...])
    middle, gain = middle_ref[...], gain_ref[...]
    inverse, unit, _ = normalised(middle, gain)
    weighted = grad_moe * gain
    inner = jnp.mean(weighted * middle, axis=-1, keepdims=True)
    grad_norm = inverse * weighted - middle * (inverse * inverse * inverse) * inner
    start = info_ref[0] * rows * slots + info_ref[1] * rows
    row_pos = start + lax.broadcasted_iota(jnp.int32, (rows, width), 0)
    grad_out = jnp.where(row_pos < info_ref[2], cot_ref[...].astype(f32), 0.0)
    grad_middle = grad_out + grad_norm
    grad_middle_ref[...] = grad_middle
    low = grad_middle.astype(bf16)
    grad_attn_ref[...] = low
    router_part = dot_nn(grad_logits.astype(f32).T.astype(bf16), normed_ref[...])
    gain_part = jnp.sum(grad_moe * unit, axis=0, keepdims=True)
    first = lax.broadcasted_iota(jnp.int32, (8, width), 0) == 0
    sums_ref[0:8, :] = jnp.where(first, jnp.broadcast_to(gain_part, (8, width)), 0.0)
    sums_ref[8:24, :] = router_part[0:16, :]
    grads = dot_nn(low, w_ref[...]).astype(bf16)
    cols = grads.shape[1] // slots
    for slot in range(slots):
        out_refs[slot][...] = grads[:, slot * cols : (slot + 1) * cols]


def moe_back(info, parts, gates, router, middle, normed, gain, cot, weight, slots):
    rows, width = middle.shape
    fixed = lambda value: pl.BlockSpec(value.shape, lambda i, info_ref: (0, 0))
    outs = [shape((rows, width), f32), shape((rows, width), bf16), shape((24, width), f32)]
    outs = outs + [shape((rows, weight.shape[1] // slots), bf16)] * slots
    operands = [*parts, gates, router, middle, normed, gain, cot, weight]
    return pl.pallas_call(
        functools.partial(moe_back_kernel, slots),
        grid_spec=pltpu.PrefetchScalarGridSpec(
            num_scalar_prefetch=1, grid=(1,), in_specs=[fixed(v) for v in operands], out_specs=[fixed(v) for v in outs]
        ),
        out_shape=outs,
        compiler_params=params(),
        cost_estimate=cost(3),
        name="moe_back",
    )(info, *operands)


def qkv_back_kernel(slots, dq_ref, dkv_ref, cos_ref, sin_ref, gain_ref, w_ref, *refs):
    x_refs, part_refs = refs[:slots], refs[slots : 2 * slots]
    grads_ref, normed_ref, sums_ref = refs[2 * slots :]
    rows = x_refs[0].shape[0]
    width = w_ref.shape[0]
    cols = dq_ref.shape[1]
    dk = dkv_ref[:, 0:LANES].astype(f32)
    turned = dk * cos_ref[...] - swap_halves(dk) * sin_ref[...]
    grads_ref[:, 0:cols] = dq_ref[...]
    grads_ref[:, cols : cols + LANES] = turned.astype(bf16)
    grads_ref[:, cols + LANES : cols + 2 * LANES] = dkv_ref[:, LANES : 2 * LANES].astype(bf16)
    total = jnp.zeros((1, width), f32)
    for slot in range(slots):
        here = slice(slot * rows, (slot + 1) * rows)
        _, unit, normed = normalised(x_refs[slot][...].astype(f32), gain_ref[...])
        normed_ref[here, :] = normed.astype(bf16)
        part = dot_nt(grads_ref[here, :], w_ref[...])
        part_refs[slot][...] = part.astype(bf16)
        total = total + jnp.sum(part * unit, axis=0, keepdims=True)
    first = lax.broadcasted_iota(jnp.int32, (8, width), 0) == 0
    sums_ref[...] = jnp.where(first, jnp.broadcast_to(total, (8, width)), 0.0)


def qkv_back(dq, dkv, cos_row, sin_row, gain, weight, x_slots):
    slots = len(x_slots)
    rows, width = x_slots[0].shape
    span = rows * slots
    return pl.pallas_call(
        functools.partial(qkv_back_kernel, slots),
        out_shape=[shape((rows, width), bf16)] * slots
        + [shape((span, weight.shape[1]), bf16), shape((span, width), bf16), shape((8, width), f32)],
        compiler_params=params(),
        cost_estimate=cost(4),
        name="qkv_back",
    )(dq, dkv, cos_row, sin_row, gain, weight, *x_slots)


def input_grad_kernel(p0, p1, p2, x_ref, gain_ref, grad_middle_ref, out_ref):
    grad_normed = p0[...].astype(f32) + p1[...].astype(f32) + p2[...].astype(f32)
    x = x_ref[...].astype(f32)
    inverse, _, _ = normalised(x, gain_ref[...])
    weighted = grad_normed * gain_ref[...]
    inner = jnp.mean(weighted * x, axis=-1, keepdims=True)
    out_ref[...] = grad_middle_ref[...] + inverse * weighted - x * (inverse * inverse * inverse) * inner


def close_input_grad(parts, x, gain, grad_middle):
    return pl.pallas_call(
        input_grad_kernel,
        out_shape=shape(x.shape, f32),
        compiler_params=params(),
        cost_estimate=cost(1),
        name="input_grad",
    )(*parts, x, gain, grad_middle)


def exchange(values, axis, bit):
    count = lax.axis_size(axis)
    return lax.ppermute(values, axis, [(i, i ^ bit) for i in range(count)])


def gather_slots(values, axis):
    count = lax.axis_size(axis)
    slots = {0: values}
    bit = count // 2
    while bit:
        for slot in sorted(slots):
            slots[slot | bit] = exchange(slots[slot], axis, bit)
        bit //= 2
    return [slots[slot] for slot in range(count)]


def trade_slots(blocks, axis):
    return [blocks[0]] + [exchange(blocks[slot], axis, slot) for slot in range(1, len(blocks))]


def scatter_slots(blocks):
    if len(blocks) == 2:
        return [blocks[0], exchange(blocks[1], "tp", 1), jnp.zeros_like(blocks[0])]
    met = exchange(blocks[3], "tp", 1)
    near = exchange(blocks[1], "tp", 1)
    joined = (blocks[2].astype(f32) + met.astype(f32)).astype(bf16)
    return [blocks[0], near, exchange(joined, "tp", 2)]


def scatter_spans(keep, send):
    bit = 1
    while True:
        came = exchange(send, "fsdp", bit)
        half = keep.shape[0] // 2
        if half == 0:
            return keep[0].astype(f32) + came[0].astype(f32)
        send = (keep[half:].astype(f32) + came[half:].astype(f32)).astype(bf16)
        keep = (keep[:half].astype(f32) + came[:half].astype(f32)).astype(bf16)
        bit *= 2


def scatter_columns(values):
    for axis in ("fsdp", "tp"):
        rank = lax.axis_index(axis)
        bit = lax.axis_size(axis) // 2
        while bit:
            half = values.shape[1] // 2
            upper = (rank // bit) % 2 == 1
            low, high = values[:, :half], values[:, half:]
            came = exchange(jnp.where(upper, low, high), axis, bit)
            values = jnp.where(upper, high, low) + came
            bit //= 2
    return values


def after(value, *others):
    return lax.optimization_barrier((value, *others))[0]


def local(
    inputs,
    cotangent,
    lengths,
    routes,
    attn_gain,
    moe_gain,
    router_weight,
    query_weight,
    key_weight,
    value_weight,
    output_weight,
    gate_weight,
    up_weight,
    down_weight,
):
    tensor_count = lax.axis_size("tp")
    tensor_rank = lax.axis_index("tp")
    shard_rank = lax.axis_index("fsdp")
    micro, rows, width = inputs.shape
    span = rows * tensor_count
    experts, shard_width, hidden = gate_weight.shape
    steps = range(micro)
    slot_ranks = [tensor_rank ^ slot for slot in range(tensor_count)]

    small = jnp.concatenate([router_weight, attn_gain[:, None], moe_gain[:, None]], axis=1)
    small_slots = jnp.stack(gather_slots(small, "tp"))
    order = jnp.arange(tensor_count) ^ tensor_rank
    small_block = small_slots[order].reshape(shard_width, small.shape[1])
    small_block = jnp.pad(small_block, ((0, 0), (0, LANES - small.shape[1])))
    qkv_local = jnp.concatenate([query_weight, key_weight, value_weight, small_block], axis=1)
    qkv_cols = qkv_local.shape[1] - LANES
    qkv_gathered = lax.all_gather(qkv_local, "fsdp", axis=0, tiled=True)
    qkv_full, router_full = qkv_gathered[:, :qkv_cols], qkv_gathered[:, qkv_cols:]
    gains = router_full[:, experts : experts + 2].T.astype(f32)
    gain_attn, gain_moe = gains[0:1], gains[1:2]

    x_slots = [gather_slots(inputs[0], "tp")]
    for m in range(1, micro):
        x_slots.append(gather_slots(after(inputs[m], x_slots[m - 1][-1]), "tp"))

    out_local = jnp.concatenate(gather_slots(output_weight.T, "tp"), axis=1)
    out_full = lax.all_gather(out_local, "fsdp", axis=0, tiled=True)
    stacked = jnp.stack(
        [gate_weight.transpose(1, 0, 2), up_weight.transpose(1, 0, 2), down_weight.transpose(2, 0, 1)], axis=1
    )
    expert_local = (
        stacked.reshape(shard_width, 3, experts // PAIR, PAIR, hidden)
        .transpose(0, 2, 1, 3, 4)
        .reshape(shard_width, 3 * experts * hidden)
    )
    expert_full = lax.all_gather(expert_local, "fsdp", axis=0, tiled=True)

    row_place = jnp.arange(rows, dtype=jnp.int32)
    span_pos = jnp.concatenate([shard_rank * span + rank * rows + row_place for rank in slot_ranks])
    cos_row, sin_row = rope_tables(span_pos)
    row_pos = shard_rank * span + tensor_rank * rows + row_place
    infos = [jnp.stack([shard_rank, tensor_rank, lengths[m]]).astype(jnp.int32) for m in steps]
    valid = [(row_pos < lengths[m])[:, None] for m in steps]
    previous = x_slots[-1][-1]
    gm_slots = []
    for m in steps:
        own = after(jnp.where(valid[m], cotangent[m], jnp.zeros_like(cotangent[m])), previous)
        gm_slots.append(gather_slots(own, "tp"))
        previous = gm_slots[m][-1]

    forward = []
    for m in steps:
        query, kv = project_qkv(x_slots[m], gain_attn, qkv_full, cos_row, sin_row)
        kv_slots = gather_slots(kv, "fsdp")
        kv_all = jnp.stack([kv_slots[reversed_bits(j, len(kv_slots))] for j in range(len(kv_slots))])
        *att_slots, log_total = attend(infos[m], query, kv_all, rows)
        att_own, middle, normed = close_attention(inputs[m], gain_moe, out_full, trade_slots(att_slots, "tp"))
        forward.append((query, kv_all, att_slots, log_total, att_own, middle, normed))

    moe_slots, expert_outs = [], []
    for m in steps:
        moe_slots.append(gather_slots(forward[m][6], "tp"))
        results = experts_both(infos[m], routes[m], router_full, expert_full, moe_slots[m], gm_slots[m])
        expert_outs.append(results)
    slots = tensor_count
    expert_grad = expert_grads(
        moe_slots,
        gm_slots,
        [results[2 * slots + 1] for results in expert_outs],
        [results[2 * slots + 2] for results in expert_outs],
    )
    expert_sum = lax.psum_scatter(expert_grad, "fsdp", scatter_dimension=0, tiled=True)

    output_list, input_list, sums, qkv_grad, out_grad = [], [], 0.0, 0.0, 0.0
    backward = []
    for m in steps:
        query, kv_all, att_slots, log_total, att_own, middle, normed = forward[m]
        results = expert_outs[m]
        parts = scatter_slots(results[:slots])
        grad_middle, grad_attn, sums_moe, *grad_slots = moe_back(
            infos[m], parts, results[2 * slots], router_full, middle, normed, gain_moe, cotangent[m], out_full, slots
        )
        out_grad = out_grad + lax.dot_general(
            grad_attn, att_own, (((0,), (0,)), ((), ())), preferred_element_type=f32
        )
        sums = sums + sums_moe
        dq, keep, send = attend_back(
            infos[m], query, kv_all, log_total, cos_row, sin_row, att_slots, trade_slots(grad_slots, "tp")
        )
        backward.append((grad_middle, dq, keep, send))
    for m in steps:
        grad_middle, dq, keep, send = backward[m]
        dkv = scatter_spans(keep, send)
        *normed_parts, grads, normed_attn, sums_attn = qkv_back(
            dq, dkv, cos_row, sin_row, gain_attn, qkv_full, x_slots[m]
        )
        qkv_grad = qkv_grad + lax.dot_general(
            normed_attn, grads, (((0,), (0,)), ((), ())), preferred_element_type=f32
        )
        sums = sums + jnp.pad(sums_attn[0:1], ((1, 22), (0, 0)))
        input_list.append(close_input_grad(scatter_slots(normed_parts), inputs[m], gain_attn, grad_middle))
    for m in steps:
        mixed = sum(part.astype(f32) for part in scatter_slots(expert_outs[m][slots : 2 * slots]))
        output_list.append(jnp.where(valid[m], forward[m][5] + mixed, 0.0).astype(bf16))

    qkv_sum = lax.psum_scatter(qkv_grad.astype(bf16), "fsdp", scatter_dimension=0, tiled=True).astype(f32)
    out_sum = lax.psum_scatter(out_grad.astype(bf16), "fsdp", scatter_dimension=0, tiled=True)
    head_cols = output_weight.shape[0]
    out_parts = [out_sum[:, slot * head_cols : (slot + 1) * head_cols] for slot in range(slots)]
    out_final = sum(part.astype(f32) for part in scatter_slots(out_parts))
    small_sum = scatter_columns(sums)
    split = (
        expert_sum.reshape(shard_width, experts // PAIR, 3, PAIR, hidden)
        .transpose(2, 1, 3, 0, 4)
        .reshape(3, experts, shard_width, hidden)
    )
    q_cols, k_cols = query_weight.shape[1], key_weight.shape[1]
    return (
        jnp.stack(output_list),
        jnp.stack(input_list),
        small_sum[1],
        small_sum[0],
        small_sum[8 : 8 + experts].T,
        qkv_sum[:, :q_cols],
        qkv_sum[:, q_cols : q_cols + k_cols],
        qkv_sum[:, q_cols + k_cols : qkv_cols],
        out_final.T,
        split[0].astype(f32),
        split[1].astype(f32),
        split[2].transpose(0, 2, 1).astype(f32),
    )


def solution(mesh):
    rows_spec = P(None, ("fsdp", "tp"), None)
    small_specs = (P(("fsdp", "tp")), P(("fsdp", "tp")), P(("fsdp", "tp"), None))
    weight_specs = (
        P("fsdp", "tp"),
        P("fsdp", "tp"),
        P("fsdp", "tp"),
        P("tp", "fsdp"),
        P(None, "fsdp", "tp"),
        P(None, "fsdp", "tp"),
        P(None, "tp", "fsdp"),
    )
    in_specs = (rows_spec, rows_spec, P(), P(None, "fsdp", None)) + small_specs + weight_specs
    out_specs = (rows_spec, rows_spec) + small_specs + weight_specs
    return jax.shard_map(local, mesh=mesh, in_specs=in_specs, out_specs=out_specs, check_vma=False)
```

```python
import functools

import jax
import jax.numpy as jnp
from jax import lax
from jax.experimental import pallas as pl
from jax.experimental.pallas import tpu as pltpu
from jax.sharding import PartitionSpec as P

HD = 64
LANES = 128
PAIR = 2
EPS = 1e-06
FILL = -1e30
THETA = 10000.0
VMEM_CAP = 60 * 1024 * 1024
f32 = jnp.float32
bf16 = jnp.bfloat16


def dot_nn(a, b):
    return lax.dot_general(a, b, (((1,), (0,)), ((), ())), preferred_element_type=f32)


def dot_nt(a, b):
    return lax.dot_general(a, b, (((1,), (1,)), ((), ())), preferred_element_type=f32)


def swap_halves(values):
    lane = lax.broadcasted_iota(jnp.int32, values.shape, values.ndim - 1)
    ahead = pltpu.roll(values, values.shape[-1] - HD // 2, values.ndim - 1)
    back = pltpu.roll(values, HD // 2, values.ndim - 1)
    return jnp.where(lane % HD < HD // 2, ahead, back)


def rope_tables(positions):
    half = HD // 2
    freqs = THETA ** (-jnp.arange(half, dtype=f32) * 2.0 / HD)
    angles = positions.astype(f32)[:, None] * freqs[None, :]
    cosine, sine = jnp.cos(angles), jnp.sin(angles)
    cos_row = jnp.concatenate([cosine] * 4, axis=1)
    sin_row = jnp.concatenate([-sine, sine] * 2, axis=1)
    return cos_row, sin_row


def head_rows(values, head):
    key_head, member = head // 2, head % 2
    pair = values[:, key_head * LANES : (key_head + 1) * LANES]
    if member != key_head:
        pair = pltpu.roll(pair, HD, 1)
    lane = lax.broadcasted_iota(jnp.int32, pair.shape, 1)
    return jnp.where(lane // HD == key_head, pair, jnp.zeros_like(pair))


def join_heads(first, second, key_head):
    if key_head == 0:
        second = pltpu.roll(second, HD, 1)
    else:
        first = pltpu.roll(first, HD, 1)
    lane = lax.broadcasted_iota(jnp.int32, first.shape, 1)
    return jnp.where(lane < HD, first, second)


def cost(microseconds):
    return pl.CostEstimate(flops=int(microseconds * 9e8), bytes_accessed=1024, transcendentals=0)


def params():
    return pltpu.CompilerParams(vmem_limit_bytes=VMEM_CAP)


def shape(dims, kind):
    return jax.ShapeDtypeStruct(dims, kind)


def normalised(x, gain):
    inverse = lax.rsqrt(jnp.mean(x * x, axis=-1, keepdims=True) + EPS)
    unit = x * inverse
    return inverse, unit, unit * gain


def qkv_kernel(*refs):
    x_refs = refs[:-6]
    gain_ref, w_ref, cos_ref, sin_ref, q_ref, kv_ref = refs[-6:]
    rows = x_refs[0].shape[0]
    for slot, x_ref in enumerate(x_refs):
        here = slice(slot * rows, (slot + 1) * rows)
        cos_row, sin_row = cos_ref[here, :], sin_ref[here, :]
        _, _, normed = normalised(x_ref[...].astype(f32), gain_ref[...])
        pre = dot_nn(normed.astype(bf16), w_ref[...])
        for part in range(3):
            cols = pre[:, part * LANES : (part + 1) * LANES]
            turned = cols * cos_row + swap_halves(cols) * sin_row
            if part < 2:
                q_ref[here, part * LANES : (part + 1) * LANES] = (turned * HD ** (-0.5)).astype(bf16)
            else:
                kv_ref[here, 0:LANES] = turned.astype(bf16)
        kv_ref[here, LANES : 2 * LANES] = pre[:, 3 * LANES : 4 * LANES].astype(bf16)


def project_qkv(x_slots, gain, weight, cos_row, sin_row):
    span = cos_row.shape[0]
    return pl.pallas_call(
        qkv_kernel,
        out_shape=[shape((span, 2 * LANES), bf16), shape((span, 2 * LANES), bf16)],
        compiler_params=params(),
        cost_estimate=cost(3),
        name="project_qkv",
    )(*x_slots, gain, weight, cos_row, sin_row)


def reversed_bits(index, count):
    result, bit = 0, 1
    while bit < count:
        result = result + ((index // bit) % 2) * (count // (2 * bit))
        bit *= 2
    return result


def places(rank, rows, dims, axis):
    index = lax.broadcasted_iota(jnp.int32, dims, axis)
    return (rank ^ (index // rows)) * rows + index % rows


def allowed_keys(rank, rows, span, key_start, query_start, length):
    key_pos = key_start + places(rank, rows, (span, span), 0)
    query_pos = query_start + places(rank, rows, (span, span), 1)
    return (key_pos <= query_pos) & (key_pos < length)


def block_kind(info_ref, j, span, count):
    mine, length = info_ref[0], info_ref[2]
    other = mine ^ reversed_bits(j, count)
    wanted = (other <= mine) & (mine * span < length) & (other * span < length)
    edge = (other == mine) | ((other + 1) * span > length)
    return other, wanted, edge


def attend_kernel(info_ref, q_ref, kv_ref, *refs):
    heads, best, total, accum = refs[-4:]
    out_refs, log_ref = refs[:-5], refs[-5]
    j = pl.program_id(0)
    count = pl.num_programs(0)
    mine, rank, length = info_ref[0], info_ref[1], info_ref[2]
    rows = out_refs[0].shape[0]
    span = q_ref.shape[0]
    other, wanted, edge = block_kind(info_ref, j, span, BLOCKS[0])

    @pl.when(j == 0)
    def _():
        values = q_ref[...].astype(f32)
        for head in range(4):
            heads[head] = head_rows(values, head).astype(bf16)
        best[...] = jnp.full(best.shape, FILL, f32)
        total[...] = jnp.zeros(total.shape, f32)
        accum[...] = jnp.zeros(accum.shape, f32)

    def block(masked):
        keys = kv_ref[0, :, :LANES]
        values_t = kv_ref[0, :, LANES:].astype(f32).T.astype(bf16)
        if masked:
            allowed = allowed_keys(rank, rows, span, other * span, mine * span, length)
        for head in range(4):
            scores = dot_nt(keys, heads[head])
            if masked:
                scores = jnp.where(allowed, scores, FILL)
            old = best[head : head + 1]
            new = jnp.maximum(old, jnp.max(scores, axis=0, keepdims=True))
            factor = jnp.exp(old - new)
            weights = jnp.exp(scores - new)
            if masked:
                weights = jnp.where(allowed, weights, 0.0)
            best[head : head + 1] = new
            total[head : head + 1] = total[head : head + 1] * factor + jnp.sum(weights, axis=0, keepdims=True)
            accum[head] = accum[head] * factor + dot_nn(values_t, weights.astype(bf16))

    @pl.when(wanted & edge)
    def _():
        block(True)

    @pl.when(wanted & jnp.logical_not(edge))
    def _():
        block(False)

    @pl.when(j == count - 1)
    def _():
        live = mine * span < length
        for key_head in range(2):
            pair = []
            for member in range(2):
                head = key_head * 2 + member
                sums = jnp.where(live, total[head : head + 1], 1.0)
                log_ref[head : head + 1] = best[head : head + 1] + jnp.log(sums)
                pair.append((accum[head] * (1.0 / sums)).T)
            joined = join_heads(pair[0], pair[1], key_head).astype(bf16)
            for slot, out_ref in enumerate(out_refs):
                out_ref[:, key_head * LANES : (key_head + 1) * LANES] = joined[slot * rows : (slot + 1) * rows]


BLOCKS = [0]


def attend(info, query, kv_all, rows):
    span, cols = query.shape
    blocks = kv_all.shape[0]
    slots = span // rows
    BLOCKS[0] = blocks
    return pl.pallas_call(
        attend_kernel,
        grid_spec=pltpu.PrefetchScalarGridSpec(
            num_scalar_prefetch=1,
            grid=(blocks,),
            in_specs=[
                pl.BlockSpec((span, cols), lambda j, info_ref: (0, 0)),
                pl.BlockSpec((1, span, 2 * LANES), lambda j, info_ref: (j, 0, 0)),
            ],
            out_specs=[pl.BlockSpec((rows, cols), lambda j, info_ref: (0, 0))] * slots
            + [pl.BlockSpec((8, span), lambda j, info_ref: (0, 0))],
            scratch_shapes=[
                pltpu.VMEM((4, span, LANES), bf16),
                pltpu.VMEM((8, span), f32),
                pltpu.VMEM((8, span), f32),
                pltpu.VMEM((4, LANES, span), f32),
            ],
        ),
        out_shape=[shape((rows, cols), bf16)] * slots + [shape((8, span), f32)],
        compiler_params=params(),
        cost_estimate=cost(12),
        name="attend",
    )(info, query, kv_all)


def attend_back_kernel(slots, info_ref, q_ref, kv_ref, log_ref, cos_ref, sin_ref, *refs):
    out_refs, grad_refs = refs[:slots], refs[slots : 2 * slots]
    dq_ref, keep_ref, send_ref, heads, grads, delta, accum, dkv = refs[2 * slots :]
    j = pl.program_id(0)
    count = pl.num_programs(0)
    mine, rank, length = info_ref[0], info_ref[1], info_ref[2]
    span, cols = q_ref.shape
    rows = span // slots
    other, wanted, edge = block_kind(info_ref, j, span, BLOCKS[0])

    @pl.when(j == 0)
    def _():
        values = q_ref[...].astype(f32)
        attended = jnp.concatenate([ref[...] for ref in out_refs], axis=0).astype(f32)
        grad = jnp.concatenate([ref[...] for ref in grad_refs], axis=0).astype(f32)
        product = grad * attended
        for head in range(4):
            heads[head] = head_rows(values, head).astype(bf16)
            grads[head] = head_rows(grad, head).astype(bf16)
            delta[head : head + 1] = jnp.sum(head_rows(product, head).T, axis=0, keepdims=True)
        accum[...] = jnp.zeros(accum.shape, f32)

    def block(masked):
        keys = kv_ref[0, :, :LANES]
        values = kv_ref[0, :, LANES:]
        keys_t = keys.astype(f32).T.astype(bf16)
        if masked:
            allowed = allowed_keys(rank, rows, span, other * span, mine * span, length)
        grad_keys = jnp.zeros((span, LANES), f32)
        grad_values = jnp.zeros((span, LANES), f32)
        for head in range(4):
            scores = dot_nt(keys, heads[head])
            probs = jnp.exp(scores - log_ref[head : head + 1])
            if masked:
                probs = jnp.where(allowed, probs, 0.0)
            grad_probs = dot_nt(values, grads[head])
            grad_scores = (probs * (grad_probs - delta[head : head + 1])).astype(bf16)
            grad_values = grad_values + dot_nn(probs.astype(bf16), grads[head])
            grad_keys = grad_keys + dot_nn(grad_scores, heads[head])
            accum[head] = accum[head] + dot_nn(keys_t, grad_scores)
        dkv[:, 0:LANES] = grad_keys.astype(bf16)
        dkv[:, LANES : 2 * LANES] = grad_values.astype(bf16)

    @pl.when(wanted & edge)
    def _():
        block(True)

    @pl.when(wanted & jnp.logical_not(edge))
    def _():
        block(False)

    @pl.when(jnp.logical_not(wanted))
    def _():
        dkv[...] = jnp.zeros(dkv.shape, bf16)

    @pl.when(j < count // 2)
    def _():
        keep_ref[0] = dkv[...]

    @pl.when(j >= count // 2)
    def _():
        send_ref[0] = dkv[...]

    @pl.when(j == count - 1)
    def _():
        for key_head in range(2):
            pair = [accum[key_head * 2 + member].T for member in range(2)]
            joined = join_heads(pair[0], pair[1], key_head) * HD ** (-0.5)
            turned = joined * cos_ref[...] - swap_halves(joined) * sin_ref[...]
            dq_ref[:, key_head * LANES : (key_head + 1) * LANES] = turned.astype(bf16)


def attend_back(info, query, kv_all, log_total, cos_row, sin_row, att_slots, grad_slots):
    span, cols = query.shape
    blocks, slots = kv_all.shape[0], len(att_slots)
    rows, half = span // slots, blocks // 2
    BLOCKS[0] = blocks
    fixed = lambda *dims: pl.BlockSpec(dims, lambda j, info_ref: (0,) * len(dims))
    return pl.pallas_call(
        functools.partial(attend_back_kernel, slots),
        grid_spec=pltpu.PrefetchScalarGridSpec(
            num_scalar_prefetch=1,
            grid=(blocks,),
            in_specs=[
                fixed(span, cols),
                pl.BlockSpec((1, span, 2 * LANES), lambda j, info_ref: (j, 0, 0)),
                fixed(8, span),
                fixed(span, LANES),
                fixed(span, LANES),
            ]
            + [fixed(rows, cols)] * (2 * slots),
            out_specs=[
                fixed(span, cols),
                pl.BlockSpec((1, span, 2 * LANES), lambda j, info_ref: (jnp.minimum(j, half - 1), 0, 0)),
                pl.BlockSpec((1, span, 2 * LANES), lambda j, info_ref: (jnp.maximum(j - half, 0), 0, 0)),
            ],
            scratch_shapes=[
                pltpu.VMEM((4, span, LANES), bf16),
                pltpu.VMEM((4, span, LANES), bf16),
                pltpu.VMEM((8, span), f32),
                pltpu.VMEM((4, LANES, span), f32),
                pltpu.VMEM((span, 2 * LANES), bf16),
            ],
        ),
        out_shape=[shape((span, cols), bf16)] + [shape((half, span, 2 * LANES), bf16)] * 2,
        compiler_params=params(),
        cost_estimate=cost(18),
        name="attend_back",
    )(info, query, kv_all, log_total, cos_row, sin_row, *att_slots, *grad_slots)


def middle_kernel(x_ref, gain_ref, w_ref, *refs):
    att_refs, (att_all, middle_ref, normed_ref) = refs[:-3], refs[-3:]
    cols = att_refs[0].shape[1]
    for slot, att_ref in enumerate(att_refs):
        att_all[:, slot * cols : (slot + 1) * cols] = att_ref[...]
    middle = x_ref[...].astype(f32) + dot_nt(att_all[...], w_ref[...])
    middle_ref[...] = middle
    normed_ref[...] = normalised(middle, gain_ref[...])[2].astype(bf16)


def close_attention(x, gain, weight, att_slots):
    rows, width = x.shape
    return pl.pallas_call(
        middle_kernel,
        out_shape=[shape((rows, weight.shape[1]), bf16), shape((rows, width), f32), shape((rows, width), bf16)],
        compiler_params=params(),
        cost_estimate=cost(2),
        name="middle",
    )(x, gain, weight, *att_slots)


def expert_kernel(slots, info_ref, routes_ref, router_ref, w_ref, *refs):
    x_refs, gm_refs = refs[:slots], refs[slots : 2 * slots]
    gin_refs, mixed_refs = refs[2 * slots : 3 * slots], refs[3 * slots : 4 * slots]
    gates_ref, low_g, low_h, x_all, gm_all, gates, mixed, gin, gate_sums = refs[4 * slots :]
    step = pl.program_id(0)
    last = pl.num_programs(0) - 1
    span, width = x_all.shape
    rows = span // slots
    wide = PAIR * LANES
    chunk = 256
    rank = info_ref[1]

    @pl.when(step == 0)
    def _():
        lane = lax.broadcasted_iota(jnp.int32, (rows, LANES), 1)
        for slot in range(slots):
            here = slice(slot * rows, (slot + 1) * rows)
            x_all[here, :] = x_refs[slot][...]
            gm_all[here, :] = gm_refs[slot][...]
            named = routes_ref[pl.ds(pl.multiple_of((rank ^ slot) * rows, rows), rows), :]
            picked = lane == named[:, 0:1]
            for k in range(1, named.shape[1]):
                picked = picked | (lane == named[:, k : k + 1])
            logits = jnp.where(picked, dot_nn(x_refs[slot][...], router_ref[...]), FILL)
            peak = jnp.max(logits, axis=1, keepdims=True)
            exps = jnp.where(picked, jnp.exp(logits - peak), 0.0)
            gates[here, :] = exps / jnp.sum(exps, axis=1, keepdims=True)
        gates_ref[...] = gates[0:rows, :]
        mixed[...] = jnp.zeros(mixed.shape, f32)
        gin[...] = jnp.zeros(gin.shape, f32)
        gate_sums[...] = jnp.zeros(gate_sums.shape, f32)

    def rows_step(i, _):
        here = pl.ds(pl.multiple_of(i * chunk, chunk), chunk)
        pre = dot_nn(x_all[here, :], w_ref[:, : 2 * wide])
        gate_pre, up_pre = pre[:, :wide], pre[:, wide:]
        back = dot_nn(gm_all[here, :], w_ref[:, 2 * wide :])
        sig = 1.0 / (1.0 + jnp.exp(-gate_pre))
        silu = gate_pre * sig
        hidden = silu * up_pre
        lane = lax.broadcasted_iota(jnp.int32, (chunk, LANES), 1)
        product = hidden * back
        spread = []
        sums = gate_sums[here, :]
        for member in range(PAIR):
            hit = lane == step * PAIR + member
            gate = jnp.sum(jnp.where(hit, gates[here, :], 0.0), axis=1, keepdims=True)
            spread.append(jnp.broadcast_to(gate, (chunk, LANES)))
            amount = jnp.sum(product[:, member * LANES : (member + 1) * LANES], axis=1, keepdims=True)
            sums = sums + jnp.where(hit, amount, 0.0)
        gate_sums[here, :] = sums
        factor = jnp.concatenate(spread, axis=1)
        grad_hidden = factor * back
        low_hidden = (factor * hidden).astype(bf16)
        grad_up = (grad_hidden * silu).astype(bf16)
        grad_gate = (grad_hidden * up_pre * (sig * (1.0 + gate_pre * (1.0 - sig)))).astype(bf16)
        low_h[here, :] = low_hidden
        low_g[here, 0:wide] = grad_gate
        low_g[here, wide : 2 * wide] = grad_up
        mixed[here, :] += dot_nt(low_hidden, w_ref[:, 2 * wide :])
        gin[here, :] += dot_nt(low_g[here, :], w_ref[:, : 2 * wide])
        return 0

    lax.fori_loop(0, span // chunk, rows_step, 0)

    @pl.when(step == last)
    def _():
        for slot in range(slots):
            here = slice(slot * rows, (slot + 1) * rows)
            mixed_refs[slot][...] = mixed[here, :].astype(bf16)
            gin_refs[slot][:, 0:width] = gin[here, :].astype(bf16)
            gin_refs[slot][:, width : width + LANES] = gate_sums[here, :].astype(bf16)


def experts_both(info, routes, router, weight, x_slots, gm_slots):
    rows, width = x_slots[0].shape
    slots = len(x_slots)
    span = rows * slots
    wide = PAIR * LANES
    steps = weight.shape[1] // (3 * wide)
    fixed = lambda *dims: pl.BlockSpec(dims, lambda i, info_ref: (0,) * len(dims))
    moving = lambda height, cols: pl.BlockSpec((height, cols), lambda i, info_ref: (0, i))
    return pl.pallas_call(
        functools.partial(expert_kernel, slots),
        grid_spec=pltpu.PrefetchScalarGridSpec(
            num_scalar_prefetch=1,
            grid=(steps,),
            in_specs=[fixed(*routes.shape), fixed(*router.shape), moving(width, 3 * wide)]
            + [fixed(rows, width)] * (2 * slots),
            out_specs=[fixed(rows, width + LANES)] * slots
            + [fixed(rows, width)] * slots
            + [fixed(rows, LANES), moving(span, 2 * wide), moving(span, wide)],
            scratch_shapes=[
                pltpu.VMEM((span, width), bf16),
                pltpu.VMEM((span, width), bf16),
                pltpu.VMEM((span, LANES), f32),
                pltpu.VMEM((span, width), f32),
                pltpu.VMEM((span, width), f32),
                pltpu.VMEM((span, LANES), f32),
            ],
        ),
        out_shape=[shape((rows, width + LANES), bf16)] * slots
        + [shape((rows, width), bf16)] * slots
        + [shape((rows, LANES), f32), shape((span, steps * 2 * wide), bf16), shape((span, steps * wide), bf16)],
        compiler_params=params(),
        cost_estimate=cost(24),
        name="experts",
    )(info, routes, router, weight, *x_slots, *gm_slots)


def expert_grad_kernel(micro, slots, *refs):
    count = micro * slots
    x_refs, gm_refs = refs[:count], refs[count : 2 * count]
    g_refs, h_refs = refs[2 * count : 2 * count + micro], refs[2 * count + micro : 2 * count + 2 * micro]
    dw_ref, x_t, gm_t = refs[2 * count + 2 * micro :]
    rows = x_refs[0].shape[0]
    width = x_t.shape[0]
    wide = PAIR * LANES
    chunk = 256

    @pl.when(pl.program_id(0) == 0)
    def _():
        for i in range(count):
            x_t[:, i * rows : (i + 1) * rows] = x_refs[i][...].T
            gm_t[:, i * rows : (i + 1) * rows] = gm_refs[i][...].T

    def weight_step(i, _):
        here = pl.ds(pl.multiple_of(i * chunk, chunk), chunk)
        g_sum, h_sum = 0.0, 0.0
        for m in range(micro):
            part = slice(m * slots * rows, (m + 1) * slots * rows)
            g_sum = g_sum + dot_nn(x_t[here, part], g_refs[m][...])
            h_sum = h_sum + dot_nn(gm_t[here, part], h_refs[m][...])
        dw_ref[here, 0 : 2 * wide] = g_sum.astype(bf16)
        dw_ref[here, 2 * wide : 3 * wide] = h_sum.astype(bf16)
        return 0

    lax.fori_loop(0, width // chunk, weight_step, 0)


def expert_grads(x_slots, gm_slots, lows_g, lows_h, part, parts):
    micro, slots = len(x_slots), len(x_slots[0])
    rows, width = x_slots[0][0].shape
    span = rows * slots
    wide = PAIR * LANES
    steps = lows_h[0].shape[1] // wide // parts
    first = part * steps
    fixed = pl.BlockSpec((rows, width), lambda i: (0, 0))
    moving = lambda height, cols: pl.BlockSpec((height, cols), lambda i: (0, first + i))
    flat = [block for part in x_slots for block in part] + [block for part in gm_slots for block in part]
    return pl.pallas_call(
        functools.partial(expert_grad_kernel, micro, slots),
        grid=(steps,),
        in_specs=[fixed] * len(flat) + [moving(span, 2 * wide)] * micro + [moving(span, wide)] * micro,
        out_specs=pl.BlockSpec((width, 3 * wide), lambda i: (0, i)),
        out_shape=shape((width, steps * 3 * wide), bf16),
        scratch_shapes=[pltpu.VMEM((width, micro * span), bf16), pltpu.VMEM((width, micro * span), bf16)],
        compiler_params=params(),
        cost_estimate=cost(12),
        name="expert_grads",
    )(*flat, *lows_g, *lows_h)


def moe_back_kernel(
    slots, info_ref, p0, p1, p2, gates_ref, router_ref, middle_ref, normed_ref, gain_ref, cot_ref, w_ref, *refs
):
    grad_middle_ref, grad_attn_ref, sums_ref = refs[:3]
    out_refs = refs[3:]
    rows, width = middle_ref.shape
    gate = lambda ref: ref[:, width : width + LANES].astype(f32)
    gates = gates_ref[...]
    gate_grads = gate(p0) + gate(p1) + gate(p2)
    grad_logits = gates * (gate_grads - jnp.sum(gates * gate_grads, axis=1, keepdims=True))
    grad_logits = grad_logits.astype(bf16)
    main = lambda ref: ref[:, 0:width].astype(f32)
    grad_moe = main(p0) + main(p1) + main(p2) + dot_nt(grad_logits, router_ref[...])
    middle, gain = middle_ref[...], gain_ref[...]
    inverse, unit, _ = normalised(middle, gain)
    weighted = grad_moe * gain
    inner = jnp.mean(weighted * middle, axis=-1, keepdims=True)
    grad_norm = inverse * weighted - middle * (inverse * inverse * inverse) * inner
    start = info_ref[0] * rows * slots + info_ref[1] * rows
    row_pos = start + lax.broadcasted_iota(jnp.int32, (rows, width), 0)
    grad_out = jnp.where(row_pos < info_ref[2], cot_ref[...].astype(f32), 0.0)
    grad_middle = grad_out + grad_norm
    grad_middle_ref[...] = grad_middle
    low = grad_middle.astype(bf16)
    grad_attn_ref[...] = low
    router_part = dot_nn(grad_logits.astype(f32).T.astype(bf16), normed_ref[...])
    gain_part = jnp.sum(grad_moe * unit, axis=0, keepdims=True)
    first = lax.broadcasted_iota(jnp.int32, (8, width), 0) == 0
    sums_ref[0:8, :] = jnp.where(first, jnp.broadcast_to(gain_part, (8, width)), 0.0)
    sums_ref[8:24, :] = router_part[0:16, :]
    grads = dot_nn(low, w_ref[...]).astype(bf16)
    cols = grads.shape[1] // slots
    for slot in range(slots):
        out_refs[slot][...] = grads[:, slot * cols : (slot + 1) * cols]


def moe_back(info, parts, gates, router, middle, normed, gain, cot, weight, slots):
    rows, width = middle.shape
    fixed = lambda value: pl.BlockSpec(value.shape, lambda i, info_ref: (0, 0))
    outs = [shape((rows, width), f32), shape((rows, width), bf16), shape((24, width), f32)]
    outs = outs + [shape((rows, weight.shape[1] // slots), bf16)] * slots
    operands = [*parts, gates, router, middle, normed, gain, cot, weight]
    return pl.pallas_call(
        functools.partial(moe_back_kernel, slots),
        grid_spec=pltpu.PrefetchScalarGridSpec(
            num_scalar_prefetch=1, grid=(1,), in_specs=[fixed(v) for v in operands], out_specs=[fixed(v) for v in outs]
        ),
        out_shape=outs,
        compiler_params=params(),
        cost_estimate=cost(3),
        name="moe_back",
    )(info, *operands)


def qkv_back_kernel(slots, dq_ref, dkv_ref, cos_ref, sin_ref, gain_ref, w_ref, *refs):
    x_refs, part_refs = refs[:slots], refs[slots : 2 * slots]
    grads_ref, normed_ref, sums_ref = refs[2 * slots :]
    rows = x_refs[0].shape[0]
    width = w_ref.shape[0]
    cols = dq_ref.shape[1]
    dk = dkv_ref[:, 0:LANES].astype(f32)
    turned = dk * cos_ref[...] - swap_halves(dk) * sin_ref[...]
    grads_ref[:, 0:cols] = dq_ref[...]
    grads_ref[:, cols : cols + LANES] = turned.astype(bf16)
    grads_ref[:, cols + LANES : cols + 2 * LANES] = dkv_ref[:, LANES : 2 * LANES].astype(bf16)
    total = jnp.zeros((1, width), f32)
    for slot in range(slots):
        here = slice(slot * rows, (slot + 1) * rows)
        _, unit, normed = normalised(x_refs[slot][...].astype(f32), gain_ref[...])
        normed_ref[here, :] = normed.astype(bf16)
        part = dot_nt(grads_ref[here, :], w_ref[...])
        part_refs[slot][...] = part.astype(bf16)
        total = total + jnp.sum(part * unit, axis=0, keepdims=True)
    first = lax.broadcasted_iota(jnp.int32, (8, width), 0) == 0
    sums_ref[...] = jnp.where(first, jnp.broadcast_to(total, (8, width)), 0.0)


def qkv_back(dq, dkv, cos_row, sin_row, gain, weight, x_slots):
    slots = len(x_slots)
    rows, width = x_slots[0].shape
    span = rows * slots
    return pl.pallas_call(
        functools.partial(qkv_back_kernel, slots),
        out_shape=[shape((rows, width), bf16)] * slots
        + [shape((span, weight.shape[1]), bf16), shape((span, width), bf16), shape((8, width), f32)],
        compiler_params=params(),
        cost_estimate=cost(4),
        name="qkv_back",
    )(dq, dkv, cos_row, sin_row, gain, weight, *x_slots)


def input_grad_kernel(micro, *refs):
    part_refs, middle_refs = refs[: 3 * micro], refs[3 * micro : 4 * micro]
    x_ref, gain_ref, out_ref = refs[4 * micro :]
    for m in range(micro):
        p0, p1, p2 = (ref[...].astype(f32) for ref in part_refs[3 * m : 3 * m + 3])
        grad_normed = p0 + p1 + p2
        x = x_ref[m].astype(f32)
        inverse, _, _ = normalised(x, gain_ref[...])
        weighted = grad_normed * gain_ref[...]
        inner = jnp.mean(weighted * x, axis=-1, keepdims=True)
        out_ref[m] = middle_refs[m][...] + inverse * weighted - x * (inverse * inverse * inverse) * inner


def close_input_grad(parts, grad_middles, x, gain):
    micro = x.shape[0]
    return pl.pallas_call(
        functools.partial(input_grad_kernel, micro),
        out_shape=shape(x.shape, f32),
        compiler_params=params(),
        cost_estimate=cost(2),
        name="input_grad",
    )(*[part for group in parts for part in group], *grad_middles, x, gain)


def outputs_kernel(micro, slots, info_ref, *refs):
    part_refs, middle_refs, out_ref = refs[: 3 * micro], refs[3 * micro : 4 * micro], refs[4 * micro]
    rows, width = middle_refs[0].shape
    start = info_ref[0] * rows * slots + info_ref[1] * rows
    row_pos = start + lax.broadcasted_iota(jnp.int32, (rows, width), 0)
    for m in range(micro):
        p0, p1, p2 = (ref[...].astype(f32) for ref in part_refs[3 * m : 3 * m + 3])
        total = middle_refs[m][...] + (p0 + p1 + p2)
        out_ref[m] = jnp.where(row_pos < info_ref[2 + m], total, 0.0).astype(bf16)


def close_outputs(info, parts, middles, slots):
    micro = len(middles)
    rows, width = middles[0].shape
    operands = [part for group in parts for part in group] + middles
    fixed = pl.BlockSpec((rows, width), lambda i, info_ref: (0, 0))
    return pl.pallas_call(
        functools.partial(outputs_kernel, micro, slots),
        grid_spec=pltpu.PrefetchScalarGridSpec(
            num_scalar_prefetch=1,
            grid=(1,),
            in_specs=[fixed] * len(operands),
            out_specs=pl.BlockSpec((micro, rows, width), lambda i, info_ref: (0, 0, 0)),
        ),
        out_shape=shape((micro, rows, width), bf16),
        compiler_params=params(),
        cost_estimate=cost(2),
        name="outputs",
    )(info, *operands)


def weights_kernel(first, info_ref, all_ref, small_ref, weight_ref, router_ref, gains_ref, table):
    blocks, rows, _ = all_ref.shape
    slots, few = small_ref.shape[1:3]
    for j in range(blocks):
        place = info_ref[0] ^ reversed_bits(j, blocks)
        weight_ref[pl.ds(pl.multiple_of(place * rows, rows), rows), :] = all_ref[j]
        for slot in range(slots):
            start = place * rows + (info_ref[1] ^ slot) * few
            table[pl.ds(pl.multiple_of(start, few), few), :] = small_ref[j, slot]
    router_ref[...] = table[...].astype(bf16)
    gains_ref[...] = table[...].T[first : first + 8, :]


def place_weights(info, weight_all, small_all, first):
    blocks, rows, cols = weight_all.shape
    whole = lambda dims: pl.BlockSpec(dims, lambda i, info_ref: (0,) * len(dims))
    outs = [shape((blocks * rows, cols), bf16), shape((blocks * rows, LANES), bf16), shape((8, blocks * rows), f32)]
    return pl.pallas_call(
        functools.partial(weights_kernel, first),
        grid_spec=pltpu.PrefetchScalarGridSpec(
            num_scalar_prefetch=1,
            grid=(1,),
            in_specs=[whole(weight_all.shape), whole(small_all.shape)],
            out_specs=[whole(out.shape) for out in outs],
            scratch_shapes=[pltpu.VMEM((blocks * rows, LANES), f32)],
        ),
        out_shape=outs,
        compiler_params=params(),
        cost_estimate=cost(3),
        name="place_weights",
    )(info, weight_all, small_all)


def output_weight_kernel(info_ref, all_ref, weight_ref):
    blocks, slots, rows, cols = all_ref.shape
    for j in range(blocks):
        place = info_ref[0] ^ reversed_bits(j, blocks)
        here = pl.ds(pl.multiple_of(place * rows, rows), rows)
        for slot in range(slots):
            weight_ref[here, slot * cols : (slot + 1) * cols] = all_ref[j, slot]


def place_output_weight(info, weight_all):
    blocks, slots, rows, cols = weight_all.shape
    out = shape((blocks * rows, slots * cols), bf16)
    return pl.pallas_call(
        output_weight_kernel,
        grid_spec=pltpu.PrefetchScalarGridSpec(
            num_scalar_prefetch=1,
            grid=(1,),
            in_specs=[pl.BlockSpec(weight_all.shape, lambda i, info_ref: (0, 0, 0, 0))],
            out_specs=pl.BlockSpec(out.shape, lambda i, info_ref: (0, 0)),
        ),
        out_shape=out,
        compiler_params=params(),
        cost_estimate=cost(3),
        name="place_output_weight",
    )(info, weight_all)


def weight_grad_kernel(micro, blocks, info_ref, *refs):
    left_refs, right_refs = refs[:micro], refs[micro : 2 * micro]
    keep_ref, send_ref = refs[2 * micro : 2 * micro + 2]
    flipped = refs[2 * micro + 2 :]
    half, high, _ = keep_ref.shape
    for m in range(micro):
        flipped[m][...] = left_refs[m][...].T

    for j in range(blocks):
        place = info_ref[0] ^ reversed_bits(j, blocks)
        here = pl.ds(pl.multiple_of(place * high, high), high)
        total = dot_nn(flipped[0][here, :], right_refs[0][...])
        for m in range(1, micro):
            total = total + dot_nn(flipped[m][here, :], right_refs[m][...])
        if j < half:
            keep_ref[j] = total.astype(bf16)
        else:
            send_ref[j - half] = total.astype(bf16)


def weight_grad(info, lefts, rights, blocks):
    micro, half = len(lefts), blocks // 2
    rows, width = lefts[0].shape
    cols = rights[0].shape[1]
    whole = lambda dims: pl.BlockSpec(dims, lambda j, info_ref: (0,) * len(dims))
    out = (half, width // blocks, cols)
    return pl.pallas_call(
        functools.partial(weight_grad_kernel, micro, blocks),
        grid_spec=pltpu.PrefetchScalarGridSpec(
            num_scalar_prefetch=1,
            grid=(1,),
            in_specs=[whole(value.shape) for value in [*lefts, *rights]],
            out_specs=[whole(out)] * 2,
            scratch_shapes=[pltpu.VMEM((width, rows), bf16)] * micro,
        ),
        out_shape=[shape(out, bf16)] * 2,
        compiler_params=params(),
        cost_estimate=cost(4),
        name="weight_grad",
    )(info, *lefts, *rights)


def unpack_kernel(half, low_ref, high_ref, gate_ref, up_ref, down_ref):
    i = pl.program_id(0)

    def place(ref):
        for member in range(PAIR):
            cut = lambda kind: ref[:, (kind * PAIR + member) * LANES : (kind * PAIR + member + 1) * LANES].astype(f32)
            gate_ref[member] = cut(0)
            up_ref[member] = cut(1)
            down_ref[member] = cut(2).T

    @pl.when(i < half)
    def _():
        place(low_ref)

    @pl.when(i >= half)
    def _():
        place(high_ref)


def unpack_experts(halves):
    rows, cols = halves[0].shape
    part = 3 * PAIR * LANES
    half = cols // part
    experts = 2 * half * PAIR
    return pl.pallas_call(
        functools.partial(unpack_kernel, half),
        grid=(2 * half,),
        in_specs=[
            pl.BlockSpec((rows, part), lambda i: (0, jnp.minimum(i, half - 1))),
            pl.BlockSpec((rows, part), lambda i: (0, jnp.maximum(i - half, 0))),
        ],
        out_specs=[
            pl.BlockSpec((PAIR, rows, LANES), lambda i: (i, 0, 0)),
            pl.BlockSpec((PAIR, rows, LANES), lambda i: (i, 0, 0)),
            pl.BlockSpec((PAIR, LANES, rows), lambda i: (i, 0, 0)),
        ],
        out_shape=[
            shape((experts, rows, LANES), f32),
            shape((experts, rows, LANES), f32),
            shape((experts, LANES, rows), f32),
        ],
        compiler_params=params(),
        cost_estimate=cost(3),
        name="unpack",
    )(*halves)


def exchange(values, axis, bit):
    count = lax.axis_size(axis)
    return lax.ppermute(values, axis, [(i, i ^ bit) for i in range(count)])


def gather_slots(values, axis):
    count = lax.axis_size(axis)
    slots = {0: values}
    bit = count // 2
    while bit:
        for slot in sorted(slots):
            slots[slot | bit] = exchange(slots[slot], axis, bit)
        bit //= 2
    return [slots[slot] for slot in range(count)]


class Moves:
    def __init__(self):
        self.inputs, self.outputs, self.steps = [], [], []

    def take(self, value):
        self.inputs.append(value)
        return ("in", len(self.inputs) - 1)

    def make(self, dims, kind):
        self.outputs.append(shape(dims, kind))
        return ("out", len(self.outputs) - 1)

    def copy(self, source, target, place, needs, size):
        ready = max([self.steps[need][5] for need in needs], default=0.0)
        rate = 45e3 if place and place[1] != 1 or place and place[0] == "tp" else 150e3
        finish = ready + 1.0 + size / rate
        self.steps.append((source, target, place, needs, ready, finish))
        return len(self.steps) - 1

    def gather_tp(self, value, pieces=2):
        count = lax.axis_size("tp")
        rows, size = value.shape[0] // pieces, value.size * 2 // pieces
        arrays = [self.take(value)] + [self.make(value.shape, value.dtype) for _ in range(count - 1)]
        for piece in range(pieces):
            index = (pl.ds(piece * rows, rows),)
            came, bit = {0: []}, count // 2
            while bit:
                for slot in sorted(came):
                    step = self.copy(
                        (arrays[slot], index), (arrays[slot | bit], index), ("tp", bit), came[slot], size * (1 + bit // 2)
                    )
                    came[slot | bit] = [step]
                bit //= 2
        return arrays[1:]

    def trade_tp(self, blocks):
        made = []
        for slot in range(1, len(blocks)):
            made.append(self.make(blocks[slot].shape, blocks[slot].dtype))
            self.copy((self.take(blocks[slot]), ()), (made[-1], ()), ("tp", slot), [], blocks[slot].size * 4)
        return made

    def spread(self, source, target, rows, size, pieces, needs):
        count = lax.axis_size("fsdp")
        bits = []
        while count >> (len(bits) + 1):
            bits.append(count >> (len(bits) + 1))
        upper = bits[:-1]
        turned = upper[len(upper) // 2 :] + upper[: len(upper) // 2]
        orders = [upper + [1], turned + [1]]
        for piece in range(pieces):
            inner = (pl.ds(piece * (rows // pieces), rows // pieces),) if pieces > 1 else ()
            came = {0: list(needs)}
            for bit in orders[piece % 2]:
                for slot in sorted(came):
                    origin = source(inner) if slot == 0 else (target, (reversed_bits(slot, count),) + inner)
                    goal = (target, (reversed_bits(slot | bit, count),) + inner)
                    came[slot | bit] = [self.copy(origin, goal, ("fsdp", bit), came[slot], size // pieces)]

    def gather_fsdp(self, value, pieces=2):
        count = lax.axis_size("fsdp")
        held, target = self.take(value), self.make((count,) + value.shape, value.dtype)
        self.spread(lambda inner: (held, inner), target, value.shape[0], value.size * 2, pieces, [])
        self.copy((held, ()), (target, (0,)), None, [], value.size)
        return target

    def gather_both(self, value):
        count, slots = lax.axis_size("fsdp"), lax.axis_size("tp")
        held, target = self.take(value), self.make((count, slots) + value.shape, value.dtype)
        needs = [self.copy((held, ()), (target, (0, 0)), None, [], value.size)]
        for slot in range(1, slots):
            needs.append(self.copy((held, ()), (target, (0, slot)), ("tp", slot), [], value.size * 2))
        self.spread(lambda inner: (target, (0,) + inner), target, slots, value.size * 2 * slots, 1, needs)
        return target

    def kernel(self, *refs):
        ins, outs = refs[: len(self.inputs)], refs[len(self.inputs) : len(self.inputs) + len(self.outputs)]
        send, recv = refs[-2:]
        ranks = {axis: lax.axis_index(axis) for axis in ("fsdp", "tp")}
        partner = lambda place: {place[0]: ranks[place[0]] ^ place[1]}
        barrier = pltpu.get_barrier_semaphore()
        places = sorted({step[2] for step in self.steps if step[2]})
        for place in places:
            pl.semaphore_signal(barrier, inc=1, device_id=partner(place), device_id_type=pl.DeviceIdType.MESH)
        pl.semaphore_wait(barrier, len(places))

        def view(spot):
            (kind, number), index = spot
            ref = (ins if kind == "in" else outs)[number]
            return ref.at[index] if index else ref

        started, arrived = {}, set()

        def arrive(number):
            if number not in arrived:
                arrived.add(number)
                copy, place = started[number]
                if place:
                    copy.wait_recv()
                else:
                    copy.wait()

        for number in sorted(range(len(self.steps)), key=lambda i: self.steps[i][4]):
            source, target, place, needs, _, _ = self.steps[number]
            for need in needs:
                arrive(need)
            if place:
                copy = pltpu.make_async_remote_copy(
                    src_ref=view(source),
                    dst_ref=view(target),
                    send_sem=send.at[number],
                    recv_sem=recv.at[number],
                    device_id=partner(place),
                    device_id_type=pl.DeviceIdType.MESH,
                )
            else:
                copy = pltpu.make_async_copy(view(source), view(target), send.at[number])
            copy.start()
            started[number] = (copy, place)
        for number in sorted(range(len(self.steps)), key=lambda i: self.steps[i][5]):
            arrive(number)
            if self.steps[number][2]:
                started[number][0].wait_send()

    def run(self, number, time, name):
        count = len(self.steps)
        anywhere = pl.BlockSpec(memory_space=pl.ANY)
        made = pl.pallas_call(
            self.kernel,
            out_shape=self.outputs,
            in_specs=[anywhere] * len(self.inputs),
            out_specs=[anywhere] * len(self.outputs),
            scratch_shapes=[pltpu.SemaphoreType.DMA((count,)), pltpu.SemaphoreType.DMA((count,))],
            compiler_params=pltpu.CompilerParams(collective_id=number, has_side_effects=True),
            cost_estimate=cost(time),
            name=name,
        )(*self.inputs)
        self.made = list(made)

    def get(self, spot):
        return [self.made[part[1]] for part in spot] if isinstance(spot, list) else self.made[spot[1]]


def trade_slots(blocks, axis):
    return [blocks[0]] + [exchange(blocks[slot], axis, slot) for slot in range(1, len(blocks))]


def scatter_slots(blocks):
    if len(blocks) == 2:
        return [blocks[0], exchange(blocks[1], "tp", 1), jnp.zeros_like(blocks[0])]
    met = exchange(blocks[3], "tp", 1)
    near = exchange(blocks[1], "tp", 1)
    joined = (blocks[2].astype(f32) + met.astype(f32)).astype(bf16)
    return [blocks[0], near, exchange(joined, "tp", 2)]


def scatter_spans(keep, send):
    bit = 1
    while True:
        came = exchange(send, "fsdp", bit)
        half = keep.shape[0] // 2
        if half == 0:
            return keep[0].astype(f32) + came[0].astype(f32)
        send = (keep[half:].astype(f32) + came[half:].astype(f32)).astype(bf16)
        keep = (keep[:half].astype(f32) + came[:half].astype(f32)).astype(bf16)
        bit *= 2


def scatter_columns(values):
    for axis in ("fsdp", "tp"):
        rank = lax.axis_index(axis)
        bit = lax.axis_size(axis) // 2
        while bit:
            half = values.shape[1] // 2
            upper = (rank // bit) % 2 == 1
            low, high = values[:, :half], values[:, half:]
            came = exchange(jnp.where(upper, low, high), axis, bit)
            values = jnp.where(upper, high, low) + came
            bit //= 2
    return values


def after(value, *others):
    return lax.optimization_barrier((value, *others))[0]


def local(
    inputs,
    cotangent,
    lengths,
    routes,
    attn_gain,
    moe_gain,
    router_weight,
    query_weight,
    key_weight,
    value_weight,
    output_weight,
    gate_weight,
    up_weight,
    down_weight,
):
    tensor_count = lax.axis_size("tp")
    tensor_rank = lax.axis_index("tp")
    shard_rank = lax.axis_index("fsdp")
    micro, rows, width = inputs.shape
    span = rows * tensor_count
    experts, shard_width, hidden = gate_weight.shape
    steps = range(micro)
    slots, blocks = tensor_count, lax.axis_size("fsdp")
    slot_ranks = [tensor_rank ^ slot for slot in range(slots)]
    odd, upper = tensor_rank % 2 == 1, tensor_rank // 2 % 2 == 1
    info_all = jnp.concatenate([jnp.stack([shard_rank, tensor_rank]).astype(jnp.int32), lengths])
    infos = [jnp.stack([info_all[0], info_all[1], info_all[2 + m]]) for m in steps]

    small = jnp.concatenate([router_weight, attn_gain[:, None], moe_gain[:, None]], axis=1).astype(f32)
    small = jnp.pad(small, ((0, 0), (0, LANES - small.shape[1])))
    qkv_local = jnp.concatenate([query_weight, key_weight, value_weight], axis=1)
    qkv_cols = qkv_local.shape[1]

    stacked = jnp.stack(
        [gate_weight.transpose(1, 0, 2), up_weight.transpose(1, 0, 2), down_weight.transpose(2, 0, 1)], axis=1
    )
    expert_local = (
        stacked.reshape(shard_width, 3, experts // PAIR, PAIR, hidden)
        .transpose(0, 2, 1, 3, 4)
        .reshape(shard_width, 3 * experts * hidden)
    )
    expert_full = lax.all_gather(expert_local, "fsdp", axis=0, tiled=True)

    row_place = jnp.arange(rows, dtype=jnp.int32)
    span_pos = jnp.concatenate([shard_rank * span + rank * rows + row_place for rank in slot_ranks])
    cos_row, sin_row = rope_tables(span_pos)
    row_pos = shard_rank * span + tensor_rank * rows + row_place
    valid = row_pos[None, :] < lengths[:, None]
    own_grads = jnp.where(valid[:, :, None], cotangent, jnp.zeros_like(cotangent))

    x_slots, queries, kvs, kv_alls, gm_slots = [], [], [], [], []
    for m in range(micro + 1):
        moves = Moves()
        wanted = {}
        if m < micro:
            wanted["x"] = moves.gather_tp(after(inputs[m], kvs[-1]) if m else inputs[m])
        if m:
            wanted["kv"] = moves.gather_fsdp(kvs[m - 1])
        if m == 0:
            wanted["weights"] = moves.gather_fsdp(qkv_local)
            wanted["small"] = moves.gather_both(small)
        if m == micro:
            wanted["gm"] = moves.gather_tp(own_grads[0])
            wanted["out"] = moves.gather_both(output_weight.T)
        moves.run(m, 25, "open")
        if m == 0:
            qkv_full, router_full, gains = place_weights(
                info_all, moves.get(wanted["weights"]), moves.get(wanted["small"]), experts
            )
            gain_attn, gain_moe = gains[0:1], gains[1:2]
        if m:
            kv_alls.append(moves.get(wanted["kv"]))
        if m < micro:
            x_slots.append([inputs[m]] + moves.get(wanted["x"]))
            query, kv = project_qkv(x_slots[m], gain_attn, qkv_full, cos_row, sin_row)
            queries.append(query)
            kvs.append(kv)
        else:
            gm_slots.append([own_grads[0]] + moves.get(wanted["gm"]))
            out_all = moves.get(wanted["out"])
    for m in range(1, micro):
        gm_slots.append(gather_slots(after(own_grads[m], gm_slots[m - 1][-1]), "tp"))

    order = kv_alls[-1]
    attended, logs, att_owns, middles, normeds, moe_slots = [], [], [], [], [], []
    for m in steps:
        *att_slots, log_total = attend(after(infos[m], order), queries[m], kv_alls[m], rows)
        if m == 0:
            out_full = place_output_weight(after(info_all, log_total), out_all)
        moves = Moves()
        traded = moves.trade_tp(att_slots)
        moves.run(micro + 1 + m, 8, "trade")
        att_own, middle, normed = close_attention(
            inputs[m], gain_moe, out_full, [att_slots[0]] + moves.get(traded)
        )
        order = middle
        attended.append(att_slots)
        logs.append(log_total)
        att_owns.append(att_own)
        middles.append(middle)
        normeds.append(normed)
        moe_slots.append(gather_slots(normed, "tp"))

    expert_outs, gin_parts = [], []
    for m in steps:
        results = experts_both(
            after(infos[m], order), routes[m], router_full, expert_full, moe_slots[m], gm_slots[m]
        )
        expert_outs.append(results)
        gin_parts.append(scatter_slots(results[:slots]))
        order = results[2 * slots]
    lows_g = [results[2 * slots + 1] for results in expert_outs]
    lows_h = [results[2 * slots + 2] for results in expert_outs]

    sums = 0.0
    grad_middles, grad_attns, grad_slots = [], [], []
    expert_sums = []
    pieces = 2
    for m in range(max(pieces, micro)):
        if m < pieces:
            some_grad = expert_grads(
                [[after(moe_slots[0][0], order)] + moe_slots[0][1:]] + moe_slots[1:], gm_slots, lows_g, lows_h, m, pieces
            )
            expert_sums.append(lax.psum_scatter(some_grad, "fsdp", scatter_dimension=0, tiled=True))
            order = some_grad
        if m < micro:
            grad_middle, grad_attn, sums_moe, *grads = moe_back(
                after(infos[m], order),
                gin_parts[m],
                expert_outs[m][2 * slots],
                router_full,
                middles[m],
                normeds[m],
                gain_moe,
                cotangent[m],
                out_full,
                slots,
            )
            order = sums_moe
            sums = sums + sums_moe
            grad_middles.append(grad_middle)
            grad_attns.append(grad_attn)
            grad_slots.append(trade_slots(grads, "tp"))
    out_keep, out_send = weight_grad(after(info_all, order), grad_attns, att_owns, blocks)
    order = out_keep

    dqs, dkvs, mixed_parts = [], [], []
    for m in steps:
        dq, keep, send = attend_back(
            after(infos[m], order), queries[m], kv_alls[m], logs[m], cos_row, sin_row, attended[m], grad_slots[m]
        )
        mixed_parts.append(scatter_slots([after(part, order) for part in expert_outs[m][slots : 2 * slots]]))
        order = dq
        dqs.append(dq)
        dkvs.append(scatter_spans(keep, send))

    normed_all, qkv_grads, normed_parts = [], [], []
    for m in steps:
        *parts, grads, normed_attn, sums_attn = qkv_back(
            dqs[m], dkvs[m], cos_row, sin_row, after(gain_attn, order), qkv_full, x_slots[m]
        )
        order = sums_attn
        sums = sums + jnp.pad(sums_attn[0:1], ((1, 22), (0, 0)))
        normed_all.append(normed_attn)
        qkv_grads.append(grads)
        normed_parts.append(scatter_slots(parts))
    qkv_keep, qkv_send = weight_grad(after(info_all, order), normed_all, qkv_grads, blocks)
    qkv_sum = scatter_spans(qkv_keep, qkv_send)
    small_sum = scatter_columns(sums)
    out_sum = scatter_spans(out_keep, out_send).astype(bf16)
    head_cols = output_weight.shape[0]
    out_parts = [out_sum[:, slot * head_cols : (slot + 1) * head_cols] for slot in range(slots)]
    out_final = sum(part.astype(f32) for part in scatter_slots(out_parts))
    outputs = close_outputs(after(info_all, qkv_keep), mixed_parts, middles, slots)
    expert_sums[0] = after(expert_sums[0], outputs)
    gate_sum, up_sum, down_sum = unpack_experts(expert_sums)
    input_grad = close_input_grad(normed_parts, grad_middles, inputs, after(gain_attn, gate_sum))
    q_cols, k_cols = query_weight.shape[1], key_weight.shape[1]
    return (
        outputs,
        input_grad,
        small_sum[1],
        small_sum[0],
        small_sum[8 : 8 + experts].T,
        qkv_sum[:, :q_cols],
        qkv_sum[:, q_cols : q_cols + k_cols],
        qkv_sum[:, q_cols + k_cols : qkv_cols],
        out_final.T,
        gate_sum,
        up_sum,
        down_sum,
    )


def solution(mesh):
    rows_spec = P(None, ("fsdp", "tp"), None)
    small_specs = (P(("fsdp", "tp")), P(("fsdp", "tp")), P(("fsdp", "tp"), None))
    weight_specs = (
        P("fsdp", "tp"),
        P("fsdp", "tp"),
        P("fsdp", "tp"),
        P("tp", "fsdp"),
        P(None, "fsdp", "tp"),
        P(None, "fsdp", "tp"),
        P(None, "tp", "fsdp"),
    )
    in_specs = (rows_spec, rows_spec, P(), P(None, "fsdp", None)) + small_specs + weight_specs
    out_specs = (rows_spec, rows_spec) + small_specs + weight_specs
    return jax.shard_map(local, mesh=mesh, in_specs=in_specs, out_specs=out_specs, check_vma=False)
```

```python
import functools

import jax
import jax.numpy as jnp
from jax import lax
from jax.experimental import pallas as pl
from jax.experimental.pallas import tpu as pltpu
from jax.sharding import PartitionSpec as P

HD = 64
LANES = 128
PAIR = 2
EPS = 1e-06
FILL = -1e30
THETA = 10000.0
VMEM_CAP = 60 * 1024 * 1024
f32 = jnp.float32
bf16 = jnp.bfloat16


def dot_nn(a, b):
    return lax.dot_general(a, b, (((1,), (0,)), ((), ())), preferred_element_type=f32)


def dot_nt(a, b):
    return lax.dot_general(a, b, (((1,), (1,)), ((), ())), preferred_element_type=f32)


def swap_halves(values):
    lane = lax.broadcasted_iota(jnp.int32, values.shape, values.ndim - 1)
    ahead = pltpu.roll(values, values.shape[-1] - HD // 2, values.ndim - 1)
    back = pltpu.roll(values, HD // 2, values.ndim - 1)
    return jnp.where(lane % HD < HD // 2, ahead, back)


def rope_tables(positions):
    half = HD // 2
    freqs = THETA ** (-jnp.arange(half, dtype=f32) * 2.0 / HD)
    angles = positions.astype(f32)[:, None] * freqs[None, :]
    cosine, sine = jnp.cos(angles), jnp.sin(angles)
    cos_row = jnp.concatenate([cosine] * 4, axis=1)
    sin_row = jnp.concatenate([-sine, sine] * 2, axis=1)
    return cos_row, sin_row


def head_rows(values, head):
    key_head, member = head // 2, head % 2
    pair = values[:, key_head * LANES : (key_head + 1) * LANES]
    if member != key_head:
        pair = pltpu.roll(pair, HD, 1)
    lane = lax.broadcasted_iota(jnp.int32, pair.shape, 1)
    return jnp.where(lane // HD == key_head, pair, jnp.zeros_like(pair))


def join_heads(first, second, key_head):
    if key_head == 0:
        second = pltpu.roll(second, HD, 1)
    else:
        first = pltpu.roll(first, HD, 1)
    lane = lax.broadcasted_iota(jnp.int32, first.shape, 1)
    return jnp.where(lane < HD, first, second)


def cost(microseconds):
    return pl.CostEstimate(flops=int(microseconds * 6e7), bytes_accessed=1024, transcendentals=0)


def params():
    return pltpu.CompilerParams(vmem_limit_bytes=VMEM_CAP)


def riding(number):
    return pltpu.CompilerParams(vmem_limit_bytes=VMEM_CAP, collective_id=number, has_side_effects=True)


def shape(dims, kind):
    return jax.ShapeDtypeStruct(dims, kind)


def normalised(x, gain):
    inverse = lax.rsqrt(jnp.mean(x * x, axis=-1, keepdims=True) + EPS)
    unit = x * inverse
    return inverse, unit, unit * gain


def qkv_kernel(*refs):
    x_refs = refs[:-6]
    gain_ref, w_ref, cos_ref, sin_ref, q_ref, kv_ref = refs[-6:]
    rows = x_refs[0].shape[0]
    for slot, x_ref in enumerate(x_refs):
        here = slice(slot * rows, (slot + 1) * rows)
        cos_row, sin_row = cos_ref[here, :], sin_ref[here, :]
        _, _, normed = normalised(x_ref[...].astype(f32), gain_ref[...])
        pre = dot_nn(normed.astype(bf16), w_ref[...])
        for part in range(3):
            cols = pre[:, part * LANES : (part + 1) * LANES]
            turned = cols * cos_row + swap_halves(cols) * sin_row
            if part < 2:
                q_ref[here, part * LANES : (part + 1) * LANES] = (turned * HD ** (-0.5)).astype(bf16)
            else:
                kv_ref[here, 0:LANES] = turned.astype(bf16)
        kv_ref[here, LANES : 2 * LANES] = pre[:, 3 * LANES : 4 * LANES].astype(bf16)


def project_qkv(x_slots, gain, weight, cos_row, sin_row):
    span = cos_row.shape[0]
    return pl.pallas_call(
        qkv_kernel,
        out_shape=[shape((span, 2 * LANES), bf16), shape((span, 2 * LANES), bf16)],
        compiler_params=params(),
        cost_estimate=cost(3),
        name="project_qkv",
    )(*x_slots, gain, weight, cos_row, sin_row)


def reversed_bits(index, count):
    result, bit = 0, 1
    while bit < count:
        result = result + ((index // bit) % 2) * (count // (2 * bit))
        bit *= 2
    return result


def places(rank, rows, dims, axis):
    index = lax.broadcasted_iota(jnp.int32, dims, axis)
    return (rank ^ (index // rows)) * rows + index % rows


def allowed_keys(rank, rows, span, key_start, query_start, length):
    key_pos = key_start + places(rank, rows, (span, span), 0)
    query_pos = query_start + places(rank, rows, (span, span), 1)
    return (key_pos <= query_pos) & (key_pos < length)


def block_kind(info_ref, j, span, count):
    mine, length = info_ref[0], info_ref[2]
    other = mine ^ reversed_bits(j, count)
    wanted = (other <= mine) & (mine * span < length) & (other * span < length)
    edge = (other == mine) | ((other + 1) * span > length)
    return other, wanted, edge


def attend_kernel(info_ref, q_ref, kv_ref, *refs):
    heads, best, total, accum = refs[-4:]
    out_refs, log_ref = refs[:-5], refs[-5]
    j = pl.program_id(0)
    count = pl.num_programs(0)
    mine, rank, length = info_ref[0], info_ref[1], info_ref[2]
    rows = out_refs[0].shape[0]
    span = q_ref.shape[0]
    other, wanted, edge = block_kind(info_ref, j, span, BLOCKS[0])

    @pl.when(j == 0)
    def _():
        values = q_ref[...].astype(f32)
        for head in range(4):
            heads[head] = head_rows(values, head).astype(bf16)
        best[...] = jnp.full(best.shape, FILL, f32)
        total[...] = jnp.zeros(total.shape, f32)
        accum[...] = jnp.zeros(accum.shape, f32)

    def block(masked):
        keys = kv_ref[0, :, :LANES]
        values_t = kv_ref[0, :, LANES:].astype(f32).T.astype(bf16)
        if masked:
            allowed = allowed_keys(rank, rows, span, other * span, mine * span, length)
        for head in range(4):
            scores = dot_nt(keys, heads[head])
            if masked:
                scores = jnp.where(allowed, scores, FILL)
            old = best[head : head + 1]
            new = jnp.maximum(old, jnp.max(scores, axis=0, keepdims=True))
            factor = jnp.exp(old - new)
            weights = jnp.exp(scores - new)
            if masked:
                weights = jnp.where(allowed, weights, 0.0)
            best[head : head + 1] = new
            total[head : head + 1] = total[head : head + 1] * factor + jnp.sum(weights, axis=0, keepdims=True)
            accum[head] = accum[head] * factor + dot_nn(values_t, weights.astype(bf16))

    @pl.when(wanted & edge)
    def _():
        block(True)

    @pl.when(wanted & jnp.logical_not(edge))
    def _():
        block(False)

    @pl.when(j == count - 1)
    def _():
        live = mine * span < length
        for key_head in range(2):
            pair = []
            for member in range(2):
                head = key_head * 2 + member
                sums = jnp.where(live, total[head : head + 1], 1.0)
                log_ref[head : head + 1] = best[head : head + 1] + jnp.log(sums)
                pair.append((accum[head] * (1.0 / sums)).T)
            joined = join_heads(pair[0], pair[1], key_head).astype(bf16)
            for slot, out_ref in enumerate(out_refs):
                out_ref[:, key_head * LANES : (key_head + 1) * LANES] = joined[slot * rows : (slot + 1) * rows]


BLOCKS = [0]


def attend(info, query, kv_all, rows):
    span, cols = query.shape
    blocks = kv_all.shape[0]
    slots = span // rows
    BLOCKS[0] = blocks
    return pl.pallas_call(
        attend_kernel,
        grid_spec=pltpu.PrefetchScalarGridSpec(
            num_scalar_prefetch=1,
            grid=(blocks,),
            in_specs=[
                pl.BlockSpec((span, cols), lambda j, info_ref: (0, 0)),
                pl.BlockSpec((1, span, 2 * LANES), lambda j, info_ref: (j, 0, 0)),
            ],
            out_specs=[pl.BlockSpec((rows, cols), lambda j, info_ref: (0, 0))] * slots
            + [pl.BlockSpec((8, span), lambda j, info_ref: (0, 0))],
            scratch_shapes=[
                pltpu.VMEM((4, span, LANES), bf16),
                pltpu.VMEM((8, span), f32),
                pltpu.VMEM((8, span), f32),
                pltpu.VMEM((4, LANES, span), f32),
            ],
        ),
        out_shape=[shape((rows, cols), bf16)] * slots + [shape((8, span), f32)],
        compiler_params=params(),
        cost_estimate=cost(12),
        name="attend",
    )(info, query, kv_all)


def attend_back_kernel(slots, info_ref, q_ref, kv_ref, log_ref, cos_ref, sin_ref, *refs):
    out_refs, grad_refs = refs[:slots], refs[slots : 2 * slots]
    blocks = BLOCKS[0]
    dq_ref, dkv_refs = refs[2 * slots], refs[2 * slots + 1 : 2 * slots + 1 + blocks]
    heads, grads, delta, accum, dkv = refs[2 * slots + 1 + blocks :]
    j = pl.program_id(0)
    count = pl.num_programs(0)
    mine, rank, length = info_ref[0], info_ref[1], info_ref[2]
    span, cols = q_ref.shape
    rows = span // slots
    other, wanted, edge = block_kind(info_ref, j, span, BLOCKS[0])

    @pl.when(j == 0)
    def _():
        values = q_ref[...].astype(f32)
        attended = jnp.concatenate([ref[...] for ref in out_refs], axis=0).astype(f32)
        grad = jnp.concatenate([ref[...] for ref in grad_refs], axis=0).astype(f32)
        product = grad * attended
        for head in range(4):
            heads[head] = head_rows(values, head).astype(bf16)
            grads[head] = head_rows(grad, head).astype(bf16)
            delta[head : head + 1] = jnp.sum(head_rows(product, head).T, axis=0, keepdims=True)
        accum[...] = jnp.zeros(accum.shape, f32)

    def block(masked):
        keys = kv_ref[0, :, :LANES]
        values = kv_ref[0, :, LANES:]
        keys_t = keys.astype(f32).T.astype(bf16)
        if masked:
            allowed = allowed_keys(rank, rows, span, other * span, mine * span, length)
        grad_keys = jnp.zeros((span, LANES), f32)
        grad_values = jnp.zeros((span, LANES), f32)
        for head in range(4):
            scores = dot_nt(keys, heads[head])
            probs = jnp.exp(scores - log_ref[head : head + 1])
            if masked:
                probs = jnp.where(allowed, probs, 0.0)
            grad_probs = dot_nt(values, grads[head])
            grad_scores = (probs * (grad_probs - delta[head : head + 1])).astype(bf16)
            grad_values = grad_values + dot_nn(probs.astype(bf16), grads[head])
            grad_keys = grad_keys + dot_nn(grad_scores, heads[head])
            accum[head] = accum[head] + dot_nn(keys_t, grad_scores)
        dkv[:, 0:LANES] = grad_keys.astype(bf16)
        dkv[:, LANES : 2 * LANES] = grad_values.astype(bf16)

    @pl.when(wanted & edge)
    def _():
        block(True)

    @pl.when(wanted & jnp.logical_not(edge))
    def _():
        block(False)

    @pl.when(jnp.logical_not(wanted))
    def _():
        dkv[...] = jnp.zeros(dkv.shape, bf16)

    for place in range(blocks):

        @pl.when(j == place)
        def _():
            dkv_refs[place][...] = dkv[...]

    @pl.when(j == count - 1)
    def _():
        for key_head in range(2):
            pair = [accum[key_head * 2 + member].T for member in range(2)]
            joined = join_heads(pair[0], pair[1], key_head) * HD ** (-0.5)
            turned = joined * cos_ref[...] - swap_halves(joined) * sin_ref[...]
            dq_ref[:, key_head * LANES : (key_head + 1) * LANES] = turned.astype(bf16)


def attend_back(info, query, kv_all, log_total, cos_row, sin_row, att_slots, grad_slots):
    span, cols = query.shape
    blocks, slots = kv_all.shape[0], len(att_slots)
    rows = span // slots
    BLOCKS[0] = blocks
    fixed = lambda *dims: pl.BlockSpec(dims, lambda j, info_ref: (0,) * len(dims))
    return pl.pallas_call(
        functools.partial(attend_back_kernel, slots),
        grid_spec=pltpu.PrefetchScalarGridSpec(
            num_scalar_prefetch=1,
            grid=(blocks,),
            in_specs=[
                fixed(span, cols),
                pl.BlockSpec((1, span, 2 * LANES), lambda j, info_ref: (j, 0, 0)),
                fixed(8, span),
                fixed(span, LANES),
                fixed(span, LANES),
            ]
            + [fixed(rows, cols)] * (2 * slots),
            out_specs=[fixed(span, cols)] + [fixed(span, 2 * LANES)] * blocks,
            scratch_shapes=[
                pltpu.VMEM((4, span, LANES), bf16),
                pltpu.VMEM((4, span, LANES), bf16),
                pltpu.VMEM((8, span), f32),
                pltpu.VMEM((4, LANES, span), f32),
                pltpu.VMEM((span, 2 * LANES), bf16),
            ],
        ),
        out_shape=[shape((span, cols), bf16)] + [shape((span, 2 * LANES), bf16)] * blocks,
        compiler_params=params(),
        cost_estimate=cost(18),
        name="attend_back",
    )(info, query, kv_all, log_total, cos_row, sin_row, *att_slots, *grad_slots)


def middle_kernel(x_ref, gain_ref, w_ref, *refs):
    att_refs, (att_all, middle_ref, normed_ref) = refs[:-3], refs[-3:]
    cols = att_refs[0].shape[1]
    for slot, att_ref in enumerate(att_refs):
        att_all[:, slot * cols : (slot + 1) * cols] = att_ref[...]
    middle = x_ref[...].astype(f32) + dot_nt(att_all[...], w_ref[...])
    middle_ref[...] = middle
    normed_ref[...] = normalised(middle, gain_ref[...])[2].astype(bf16)


def close_attention(x, gain, weight, att_slots):
    rows, width = x.shape
    return pl.pallas_call(
        middle_kernel,
        out_shape=[shape((rows, weight.shape[1]), bf16), shape((rows, width), f32), shape((rows, width), bf16)],
        compiler_params=params(),
        cost_estimate=cost(2),
        name="middle",
    )(x, gain, weight, *att_slots)


def expert_kernel(slots, ride, info_ref, routes_ref, router_ref, w_ref, *refs):
    x_refs, gm_refs = refs[:slots], refs[slots : 2 * slots]
    ride_in, refs = refs[2 * slots : 2 * slots + len(ride.inputs)], refs[2 * slots + len(ride.inputs) :]
    gin_refs, mixed_refs, refs = refs[:slots], refs[slots : 2 * slots], refs[2 * slots :]
    gates_ref, low_g, low_h = refs[:3]
    ride_out, refs = refs[3 : 3 + len(ride.outputs)], refs[3 + len(ride.outputs) :]
    x_all, gm_all, gates, mixed, gin, gate_sums, send, recv = refs
    step = pl.program_id(0)
    last = pl.num_programs(0) - 1
    span, width = x_all.shape
    rows = span // slots
    wide = PAIR * LANES
    chunk = 256
    rank = lax.axis_index("tp")

    @pl.when(step == 0)
    def _():
        ride.begin(ride_in, ride_out, send, recv)
        lane = lax.broadcasted_iota(jnp.int32, (rows, LANES), 1)
        for slot in range(slots):
            here = slice(slot * rows, (slot + 1) * rows)
            x_all[here, :] = x_refs[slot][...]
            gm_all[here, :] = gm_refs[slot][...]
            named = routes_ref[pl.ds(pl.multiple_of((rank ^ slot) * rows, rows), rows), :]
            picked = lane == named[:, 0:1]
            for k in range(1, named.shape[1]):
                picked = picked | (lane == named[:, k : k + 1])
            logits = jnp.where(picked, dot_nn(x_refs[slot][...], router_ref[...]), FILL)
            peak = jnp.max(logits, axis=1, keepdims=True)
            exps = jnp.where(picked, jnp.exp(logits - peak), 0.0)
            gates[here, :] = exps / jnp.sum(exps, axis=1, keepdims=True)
        gates_ref[...] = gates[0:rows, :]
        mixed[...] = jnp.zeros(mixed.shape, f32)
        gin[...] = jnp.zeros(gin.shape, f32)
        gate_sums[...] = jnp.zeros(gate_sums.shape, f32)

    def rows_step(i, _):
        here = pl.ds(pl.multiple_of(i * chunk, chunk), chunk)
        pre = dot_nn(x_all[here, :], w_ref[:, : 2 * wide])
        gate_pre, up_pre = pre[:, :wide], pre[:, wide:]
        back = dot_nn(gm_all[here, :], w_ref[:, 2 * wide :])
        sig = 1.0 / (1.0 + jnp.exp(-gate_pre))
        silu = gate_pre * sig
        hidden = silu * up_pre
        lane = lax.broadcasted_iota(jnp.int32, (chunk, LANES), 1)
        product = hidden * back
        spread = []
        sums = gate_sums[here, :]
        for member in range(PAIR):
            hit = lane == step * PAIR + member
            gate = jnp.sum(jnp.where(hit, gates[here, :], 0.0), axis=1, keepdims=True)
            spread.append(jnp.broadcast_to(gate, (chunk, LANES)))
            amount = jnp.sum(product[:, member * LANES : (member + 1) * LANES], axis=1, keepdims=True)
            sums = sums + jnp.where(hit, amount, 0.0)
        gate_sums[here, :] = sums
        factor = jnp.concatenate(spread, axis=1)
        grad_hidden = factor * back
        low_hidden = (factor * hidden).astype(bf16)
        grad_up = (grad_hidden * silu).astype(bf16)
        grad_gate = (grad_hidden * up_pre * (sig * (1.0 + gate_pre * (1.0 - sig)))).astype(bf16)
        low_h[here, :] = low_hidden
        low_g[here, 0:wide] = grad_gate
        low_g[here, wide : 2 * wide] = grad_up
        mixed[here, :] += dot_nt(low_hidden, w_ref[:, 2 * wide :])
        gin[here, :] += dot_nt(low_g[here, :], w_ref[:, : 2 * wide])
        return 0

    lax.fori_loop(0, span // chunk, rows_step, 0)

    @pl.when(step == last)
    def _():
        for slot in range(slots):
            here = slice(slot * rows, (slot + 1) * rows)
            mixed_refs[slot][...] = mixed[here, :].astype(bf16)
            gin_refs[slot][:, 0:width] = gin[here, :].astype(bf16)
            gin_refs[slot][:, width : width + LANES] = gate_sums[here, :].astype(bf16)
        ride.finish(ride_in, ride_out, send, recv)


def experts_both(info, routes, router, weight, x_slots, gm_slots, ride, number):
    rows, width = x_slots[0].shape
    slots = len(x_slots)
    span = rows * slots
    wide = PAIR * LANES
    steps = weight.shape[1] // (3 * wide)
    fixed = lambda *dims: pl.BlockSpec(dims, lambda i, info_ref: (0,) * len(dims))
    moving = lambda height, cols: pl.BlockSpec((height, cols), lambda i, info_ref: (0, i))
    anywhere = pl.BlockSpec(memory_space=pl.ANY)
    results = pl.pallas_call(
        functools.partial(expert_kernel, slots, ride),
        grid_spec=pltpu.PrefetchScalarGridSpec(
            num_scalar_prefetch=1,
            grid=(steps,),
            in_specs=[fixed(*routes.shape), fixed(*router.shape), moving(width, 3 * wide)]
            + [fixed(rows, width)] * (2 * slots)
            + [anywhere] * len(ride.inputs),
            out_specs=[fixed(rows, width + LANES)] * slots
            + [fixed(rows, width)] * slots
            + [fixed(rows, LANES), moving(span, 2 * wide), moving(span, wide)]
            + [anywhere] * len(ride.outputs),
            scratch_shapes=[
                pltpu.VMEM((span, width), bf16),
                pltpu.VMEM((span, width), bf16),
                pltpu.VMEM((span, LANES), f32),
                pltpu.VMEM((span, width), f32),
                pltpu.VMEM((span, width), f32),
                pltpu.VMEM((span, LANES), f32),
            ]
            + ride.semaphores(),
        ),
        out_shape=[shape((rows, width + LANES), bf16)] * slots
        + [shape((rows, width), bf16)] * slots
        + [shape((rows, LANES), f32), shape((span, steps * 2 * wide), bf16), shape((span, steps * wide), bf16)]
        + ride.outputs,
        compiler_params=riding(number),
        cost_estimate=cost(24),
        name="experts",
    )(info, routes, router, weight, *x_slots, *gm_slots, *ride.inputs)
    ride.made = list(results[2 * slots + 3 :])
    return results[: 2 * slots + 3]


def expert_grad_kernel(micro, slots, ride, *refs):
    count = micro * slots
    send, recv = refs[-2:]
    given = 2 * count + 2 * micro
    ride_in = refs[given : given + len(ride.inputs)]
    ride_out = refs[given + len(ride.inputs) + 1 : given + len(ride.inputs) + 1 + len(ride.outputs)]
    x_refs, gm_refs = refs[:count], refs[count : 2 * count]
    g_refs, h_refs = refs[2 * count : 2 * count + micro], refs[2 * count + micro : 2 * count + 2 * micro]
    dw_ref, (x_t, gm_t) = refs[given + len(ride.inputs)], refs[-4:-2]
    rows = x_refs[0].shape[0]
    width = x_t.shape[0]
    wide = PAIR * LANES
    chunk = 256

    @pl.when(pl.program_id(0) == 0)
    def _():
        ride.begin(ride_in, ride_out, send, recv)
        for i in range(count):
            x_t[:, i * rows : (i + 1) * rows] = x_refs[i][...].T
            gm_t[:, i * rows : (i + 1) * rows] = gm_refs[i][...].T

    def weight_step(i, _):
        here = pl.ds(pl.multiple_of(i * chunk, chunk), chunk)
        g_sum, h_sum = 0.0, 0.0
        for m in range(micro):
            part = slice(m * slots * rows, (m + 1) * slots * rows)
            g_sum = g_sum + dot_nn(x_t[here, part], g_refs[m][...])
            h_sum = h_sum + dot_nn(gm_t[here, part], h_refs[m][...])
        dw_ref[here, 0 : 2 * wide] = g_sum.astype(bf16)
        dw_ref[here, 2 * wide : 3 * wide] = h_sum.astype(bf16)
        return 0

    lax.fori_loop(0, width // chunk, weight_step, 0)

    @pl.when(pl.program_id(0) == pl.num_programs(0) - 1)
    def _():
        ride.finish(ride_in, ride_out, send, recv)


def expert_grads(x_slots, gm_slots, lows_g, lows_h, ride, number):
    micro, slots = len(x_slots), len(x_slots[0])
    rows, width = x_slots[0][0].shape
    span = rows * slots
    wide = PAIR * LANES
    steps = lows_h[0].shape[1] // wide
    fixed = pl.BlockSpec((rows, width), lambda i: (0, 0))
    moving = lambda height, cols: pl.BlockSpec((height, cols), lambda i: (0, i))
    flat = [block for part in x_slots for block in part] + [block for part in gm_slots for block in part]
    anywhere = pl.BlockSpec(memory_space=pl.ANY)
    summed, *ride.made = pl.pallas_call(
        functools.partial(expert_grad_kernel, micro, slots, ride),
        grid=(steps,),
        in_specs=[fixed] * len(flat) + [moving(span, 2 * wide)] * micro + [moving(span, wide)] * micro
        + [anywhere] * len(ride.inputs),
        out_specs=[pl.BlockSpec((width, 3 * wide), lambda i: (0, i))] + [anywhere] * len(ride.outputs),
        out_shape=[shape((width, steps * 3 * wide), bf16)] + ride.outputs,
        scratch_shapes=[pltpu.VMEM((width, micro * span), bf16), pltpu.VMEM((width, micro * span), bf16)]
        + ride.semaphores(),
        compiler_params=riding(number),
        cost_estimate=cost(12),
        name="expert_grads",
    )(*flat, *lows_g, *lows_h, *ride.inputs)
    return summed


def moe_back_kernel(
    slots, info_ref, *refs
):
    parts, refs = refs[:slots], refs[slots:]
    gates_ref, router_ref, middle_ref, normed_ref, gain_ref, cot_ref, w_ref = refs[:7]
    refs = refs[7:]
    grad_middle_ref, grad_attn_ref, sums_ref = refs[:3]
    out_refs = refs[3:]
    rows, width = middle_ref.shape
    gate = lambda ref: ref[:, width : width + LANES].astype(f32)
    gates = gates_ref[...]
    gate_grads = sum(gate(part) for part in parts)
    grad_logits = gates * (gate_grads - jnp.sum(gates * gate_grads, axis=1, keepdims=True))
    grad_logits = grad_logits.astype(bf16)
    main = lambda ref: ref[:, 0:width].astype(f32)
    grad_moe = sum(main(part) for part in parts) + dot_nt(grad_logits, router_ref[...])
    middle, gain = middle_ref[...], gain_ref[...]
    inverse, unit, _ = normalised(middle, gain)
    weighted = grad_moe * gain
    inner = jnp.mean(weighted * middle, axis=-1, keepdims=True)
    grad_norm = inverse * weighted - middle * (inverse * inverse * inverse) * inner
    start = info_ref[0] * rows * slots + info_ref[1] * rows
    row_pos = start + lax.broadcasted_iota(jnp.int32, (rows, width), 0)
    grad_out = jnp.where(row_pos < info_ref[2], cot_ref[...].astype(f32), 0.0)
    grad_middle = grad_out + grad_norm
    grad_middle_ref[...] = grad_middle
    low = grad_middle.astype(bf16)
    grad_attn_ref[...] = low
    router_part = dot_nn(grad_logits.astype(f32).T.astype(bf16), normed_ref[...])
    gain_part = jnp.sum(grad_moe * unit, axis=0, keepdims=True)
    first = lax.broadcasted_iota(jnp.int32, (8, width), 0) == 0
    sums_ref[0:8, :] = jnp.where(first, jnp.broadcast_to(gain_part, (8, width)), 0.0)
    sums_ref[8:24, :] = router_part[0:16, :]
    grads = dot_nn(low, w_ref[...]).astype(bf16)
    cols = grads.shape[1] // slots
    for slot in range(slots):
        out_refs[slot][...] = grads[:, slot * cols : (slot + 1) * cols]


def moe_back(info, parts, gates, router, middle, normed, gain, cot, weight, slots):
    rows, width = middle.shape
    fixed = lambda value: pl.BlockSpec(value.shape, lambda i, info_ref: (0, 0))
    outs = [shape((rows, width), f32), shape((rows, width), bf16), shape((24, width), f32)]
    outs = outs + [shape((rows, weight.shape[1] // slots), bf16)] * slots
    operands = [*parts, gates, router, middle, normed, gain, cot, weight]
    return pl.pallas_call(
        functools.partial(moe_back_kernel, slots),
        grid_spec=pltpu.PrefetchScalarGridSpec(
            num_scalar_prefetch=1, grid=(1,), in_specs=[fixed(v) for v in operands], out_specs=[fixed(v) for v in outs]
        ),
        out_shape=outs,
        compiler_params=params(),
        cost_estimate=cost(3),
        name="moe_back",
    )(info, *operands)


def qkv_back_kernel(slots, blocks, dq_ref, cos_ref, sin_ref, gain_ref, w_ref, *refs):
    dkv_refs, refs = refs[:blocks], refs[blocks:]
    dkv = sum(ref[...].astype(f32) for ref in dkv_refs)
    x_refs, part_refs = refs[:slots], refs[slots : 2 * slots]
    grads_ref, normed_ref, sums_ref = refs[2 * slots :]
    rows = x_refs[0].shape[0]
    width = w_ref.shape[0]
    cols = dq_ref.shape[1]
    dk = dkv[:, 0:LANES]
    turned = dk * cos_ref[...] - swap_halves(dk) * sin_ref[...]
    grads_ref[:, 0:cols] = dq_ref[...]
    grads_ref[:, cols : cols + LANES] = turned.astype(bf16)
    grads_ref[:, cols + LANES : cols + 2 * LANES] = dkv[:, LANES : 2 * LANES].astype(bf16)
    total = jnp.zeros((1, width), f32)
    for slot in range(slots):
        here = slice(slot * rows, (slot + 1) * rows)
        _, unit, normed = normalised(x_refs[slot][...].astype(f32), gain_ref[...])
        normed_ref[here, :] = normed.astype(bf16)
        part = dot_nt(grads_ref[here, :], w_ref[...])
        part_refs[slot][...] = part.astype(bf16)
        total = total + jnp.sum(part * unit, axis=0, keepdims=True)
    first = lax.broadcasted_iota(jnp.int32, (8, width), 0) == 0
    sums_ref[...] = jnp.where(first, jnp.broadcast_to(total, (8, width)), 0.0)


def qkv_back(dq, dkv_parts, cos_row, sin_row, gain, weight, x_slots):
    slots = len(x_slots)
    rows, width = x_slots[0].shape
    span = rows * slots
    return pl.pallas_call(
        functools.partial(qkv_back_kernel, slots, len(dkv_parts)),
        out_shape=[shape((rows, width), bf16)] * slots
        + [shape((span, weight.shape[1]), bf16), shape((span, width), bf16), shape((8, width), f32)],
        compiler_params=params(),
        cost_estimate=cost(4),
        name="qkv_back",
    )(dq, cos_row, sin_row, gain, weight, *dkv_parts, *x_slots)


def input_grad_kernel(micro, slots, *refs):
    part_refs, middle_refs = refs[: slots * micro], refs[slots * micro : (slots + 1) * micro]
    x_ref, gain_ref, out_ref = refs[(slots + 1) * micro :]
    for m in range(micro):
        grad_normed = sum(ref[...].astype(f32) for ref in part_refs[slots * m : slots * (m + 1)])
        x = x_ref[m].astype(f32)
        inverse, _, _ = normalised(x, gain_ref[...])
        weighted = grad_normed * gain_ref[...]
        inner = jnp.mean(weighted * x, axis=-1, keepdims=True)
        out_ref[m] = middle_refs[m][...] + inverse * weighted - x * (inverse * inverse * inverse) * inner


def close_input_grad(parts, grad_middles, x, gain):
    micro = x.shape[0]
    return pl.pallas_call(
        functools.partial(input_grad_kernel, micro, len(parts[0])),
        out_shape=shape(x.shape, f32),
        compiler_params=params(),
        cost_estimate=cost(2),
        name="input_grad",
    )(*[part for group in parts for part in group], *grad_middles, x, gain)


def outputs_kernel(micro, slots, info_ref, *refs):
    part_refs, middle_refs, out_ref = refs[: slots * micro], refs[slots * micro : -1], refs[-1]
    rows, width = middle_refs[0].shape
    start = info_ref[0] * rows * slots + info_ref[1] * rows
    row_pos = start + lax.broadcasted_iota(jnp.int32, (rows, width), 0)
    for m in range(micro):
        mixed = sum(ref[...].astype(f32) for ref in part_refs[slots * m : slots * (m + 1)])
        total = middle_refs[m][...] + mixed
        out_ref[m] = jnp.where(row_pos < info_ref[2 + m], total, 0.0).astype(bf16)


def close_outputs(info, parts, middles, slots):
    micro = len(middles)
    rows, width = middles[0].shape
    operands = [part for group in parts for part in group] + middles
    fixed = pl.BlockSpec((rows, width), lambda i, info_ref: (0, 0))
    return pl.pallas_call(
        functools.partial(outputs_kernel, micro, slots),
        grid_spec=pltpu.PrefetchScalarGridSpec(
            num_scalar_prefetch=1,
            grid=(1,),
            in_specs=[fixed] * len(operands),
            out_specs=pl.BlockSpec((micro, rows, width), lambda i, info_ref: (0, 0, 0)),
        ),
        out_shape=shape((micro, rows, width), bf16),
        compiler_params=params(),
        cost_estimate=cost(2),
        name="outputs",
    )(info, *operands)


def weights_kernel(first, info_ref, all_ref, small_ref, weight_ref, router_ref, gains_ref, table):
    blocks, rows, _ = all_ref.shape
    slots, few = small_ref.shape[1:3]
    for j in range(blocks):
        place = info_ref[0] ^ reversed_bits(j, blocks)
        weight_ref[pl.ds(pl.multiple_of(place * rows, rows), rows), :] = all_ref[j]
        for slot in range(slots):
            start = place * rows + (info_ref[1] ^ slot) * few
            table[pl.ds(pl.multiple_of(start, few), few), :] = small_ref[j, slot]
    router_ref[...] = table[...].astype(bf16)
    gains_ref[...] = table[...].T[first : first + 8, :]


def place_weights(info, weight_all, small_all, first):
    blocks, rows, cols = weight_all.shape
    whole = lambda dims: pl.BlockSpec(dims, lambda i, info_ref: (0,) * len(dims))
    outs = [shape((blocks * rows, cols), bf16), shape((blocks * rows, LANES), bf16), shape((8, blocks * rows), f32)]
    return pl.pallas_call(
        functools.partial(weights_kernel, first),
        grid_spec=pltpu.PrefetchScalarGridSpec(
            num_scalar_prefetch=1,
            grid=(1,),
            in_specs=[whole(weight_all.shape), whole(small_all.shape)],
            out_specs=[whole(out.shape) for out in outs],
            scratch_shapes=[pltpu.VMEM((blocks * rows, LANES), f32)],
        ),
        out_shape=outs,
        compiler_params=params(),
        cost_estimate=cost(3),
        name="place_weights",
    )(info, weight_all, small_all)


def output_weight_kernel(info_ref, all_ref, weight_ref):
    blocks, slots, rows, cols = all_ref.shape
    for j in range(blocks):
        place = info_ref[0] ^ reversed_bits(j, blocks)
        here = pl.ds(pl.multiple_of(place * rows, rows), rows)
        for slot in range(slots):
            weight_ref[here, slot * cols : (slot + 1) * cols] = all_ref[j, slot]


def place_output_weight(info, weight_all):
    blocks, slots, rows, cols = weight_all.shape
    out = shape((blocks * rows, slots * cols), bf16)
    return pl.pallas_call(
        output_weight_kernel,
        grid_spec=pltpu.PrefetchScalarGridSpec(
            num_scalar_prefetch=1,
            grid=(1,),
            in_specs=[pl.BlockSpec(weight_all.shape, lambda i, info_ref: (0, 0, 0, 0))],
            out_specs=pl.BlockSpec(out.shape, lambda i, info_ref: (0, 0)),
        ),
        out_shape=out,
        compiler_params=params(),
        cost_estimate=cost(3),
        name="place_output_weight",
    )(info, weight_all)


def weight_grad_kernel(micro, blocks, info_ref, *refs):
    left_refs, right_refs = refs[:micro], refs[micro : 2 * micro]
    keep_ref, send_ref = refs[2 * micro : 2 * micro + 2]
    flipped = refs[2 * micro + 2 :]
    half, high, _ = keep_ref.shape
    for m in range(micro):
        flipped[m][...] = left_refs[m][...].T

    for j in range(blocks):
        place = info_ref[0] ^ reversed_bits(j, blocks)
        here = pl.ds(pl.multiple_of(place * high, high), high)
        total = dot_nn(flipped[0][here, :], right_refs[0][...])
        for m in range(1, micro):
            total = total + dot_nn(flipped[m][here, :], right_refs[m][...])
        if j < half:
            keep_ref[j] = total.astype(bf16)
        else:
            send_ref[j - half] = total.astype(bf16)


def weight_grad(info, lefts, rights, blocks):
    micro, half = len(lefts), blocks // 2
    rows, width = lefts[0].shape
    cols = rights[0].shape[1]
    whole = lambda dims: pl.BlockSpec(dims, lambda j, info_ref: (0,) * len(dims))
    out = (half, width // blocks, cols)
    return pl.pallas_call(
        functools.partial(weight_grad_kernel, micro, blocks),
        grid_spec=pltpu.PrefetchScalarGridSpec(
            num_scalar_prefetch=1,
            grid=(1,),
            in_specs=[whole(value.shape) for value in [*lefts, *rights]],
            out_specs=[whole(out)] * 2,
            scratch_shapes=[pltpu.VMEM((width, rows), bf16)] * micro,
        ),
        out_shape=[shape(out, bf16)] * 2,
        compiler_params=params(),
        cost_estimate=cost(4),
        name="weight_grad",
    )(info, *lefts, *rights)


def unpack_kernel(sum_ref, gate_ref, up_ref, down_ref):
    for member in range(PAIR):
        cut = lambda kind: sum_ref[:, (kind * PAIR + member) * LANES : (kind * PAIR + member + 1) * LANES].astype(f32)
        gate_ref[member] = cut(0)
        up_ref[member] = cut(1)
        down_ref[member] = cut(2).T


def unpack_experts(summed):
    rows, cols = summed.shape
    part = 3 * PAIR * LANES
    count = cols // part
    experts = count * PAIR
    return pl.pallas_call(
        unpack_kernel,
        grid=(count,),
        in_specs=[pl.BlockSpec((rows, part), lambda i: (0, i))],
        out_specs=[
            pl.BlockSpec((PAIR, rows, LANES), lambda i: (i, 0, 0)),
            pl.BlockSpec((PAIR, rows, LANES), lambda i: (i, 0, 0)),
            pl.BlockSpec((PAIR, LANES, rows), lambda i: (i, 0, 0)),
        ],
        out_shape=[
            shape((experts, rows, LANES), f32),
            shape((experts, rows, LANES), f32),
            shape((experts, LANES, rows), f32),
        ],
        compiler_params=params(),
        cost_estimate=cost(5),
        name="unpack",
    )(summed)


def exchange(values, axis, bit):
    count = lax.axis_size(axis)
    return lax.ppermute(values, axis, [(i, i ^ bit) for i in range(count)])


class Moves:
    def __init__(self):
        self.inputs, self.outputs, self.steps = [], [], []

    def take(self, value):
        self.inputs.append(value)
        return ("in", len(self.inputs) - 1)

    def make(self, dims, kind):
        self.outputs.append(shape(dims, kind))
        return ("out", len(self.outputs) - 1)

    def copy(self, source, target, place, needs, size):
        ready = max([self.steps[need][5] for need in needs], default=0.0)
        rate = 45e3 if place and place[1] != 1 or place and place[0] == "tp" else 150e3
        finish = ready + 1.0 + size / rate
        self.steps.append((source, target, place, needs, ready, finish))
        return len(self.steps) - 1

    def gather_tp(self, value, pieces=2):
        count = lax.axis_size("tp")
        rows, size = value.shape[0] // pieces, value.size * 2 // pieces
        arrays = [self.take(value)] + [self.make(value.shape, value.dtype) for _ in range(count - 1)]
        for piece in range(pieces):
            index = (pl.ds(piece * rows, rows),)
            came, bit = {0: []}, count // 2
            while bit:
                for slot in sorted(came):
                    step = self.copy(
                        (arrays[slot], index), (arrays[slot | bit], index), ("tp", bit), came[slot], size * (1 + bit // 2)
                    )
                    came[slot | bit] = [step]
                bit //= 2
        return arrays[1:]

    def trade_tp(self, blocks):
        made = []
        for slot in range(1, len(blocks)):
            made.append(self.make(blocks[slot].shape, blocks[slot].dtype))
            self.copy((self.take(blocks[slot]), ()), (made[-1], ()), ("tp", slot), [], blocks[slot].size * 4)
        return made

    def share_tp(self, value):
        held, made = self.take(value), []
        for slot in range(1, lax.axis_size("tp")):
            made.append(self.make(value.shape, value.dtype))
            self.copy((held, ()), (made[-1], ()), ("tp", slot), [], value.size * 4)
        return made

    def trade_fsdp(self, blocks):
        made = []
        for place in range(1, len(blocks)):
            made.append(self.make(blocks[place].shape, blocks[place].dtype))
            slot = reversed_bits(place, len(blocks))
            self.copy((self.take(blocks[place]), ()), (made[-1], ()), ("fsdp", slot), [], blocks[place].size * 4)
        return made

    def trade_stack(self, value, first, count):
        skip = int(first == 0)
        held, target = self.take(value), self.make((value.shape[0] - skip,) + value.shape[1:], value.dtype)
        for j in range(skip, value.shape[0]):
            slot = reversed_bits(first + j, count)
            self.copy((held, (j,)), (target, (j - skip,)), ("fsdp", slot), [], value[0].size * 4)
        return target

    def trade_rows(self, value, count):
        rows = value.shape[0] // count
        held, target = self.take(value), self.make((count - 1, rows) + value.shape[1:], value.dtype)
        for slot in range(1, count):
            source = lambda ranks, slot=slot: (pl.ds(pl.multiple_of((ranks["fsdp"] ^ slot) * rows, rows), rows),)
            self.copy((held, source), (target, (slot - 1,)), ("fsdp", slot), [], rows * 512)
        return target

    def spread(self, source, target, rows, size, pieces, needs):
        count = lax.axis_size("fsdp")
        bits = []
        while count >> (len(bits) + 1):
            bits.append(count >> (len(bits) + 1))
        upper = bits[:-1]
        turned = upper[len(upper) // 2 :] + upper[: len(upper) // 2]
        orders = [upper + [1], turned + [1]]
        for piece in range(pieces):
            inner = (pl.ds(piece * (rows // pieces), rows // pieces),) if pieces > 1 else ()
            came = {0: list(needs)}
            for bit in orders[piece % 2]:
                for slot in sorted(came):
                    origin = source(inner) if slot == 0 else (target, (reversed_bits(slot, count),) + inner)
                    goal = (target, (reversed_bits(slot | bit, count),) + inner)
                    came[slot | bit] = [self.copy(origin, goal, ("fsdp", bit), came[slot], size // pieces)]

    def gather_fsdp(self, value, pieces=2):
        count = lax.axis_size("fsdp")
        held, target = self.take(value), self.make((count,) + value.shape, value.dtype)
        self.spread(lambda inner: (held, inner), target, value.shape[0], value.size * 2, pieces, [])
        self.copy((held, ()), (target, (0,)), None, [], value.size)
        return target

    def gather_both(self, value):
        count, slots = lax.axis_size("fsdp"), lax.axis_size("tp")
        held, target = self.take(value), self.make((count, slots) + value.shape, value.dtype)
        needs = [self.copy((held, ()), (target, (0, 0)), None, [], value.size)]
        for slot in range(1, slots):
            needs.append(self.copy((held, ()), (target, (0, slot)), ("tp", slot), [], value.size * 2))
        self.spread(lambda inner: (target, (0,) + inner), target, slots, value.size * 2 * slots, 2, needs)
        return target

    def meet(self):
        ranks = {axis: lax.axis_index(axis) for axis in ("fsdp", "tp")}
        barrier = pltpu.get_barrier_semaphore()
        places = sorted({step[2] for step in self.steps if step[2]})
        for axis, bit in places:
            pl.semaphore_signal(
                barrier, inc=1, device_id={axis: ranks[axis] ^ bit}, device_id_type=pl.DeviceIdType.MESH
            )
        pl.semaphore_wait(barrier, len(places))

    def describe(self, number, ins, outs, send, recv):
        ranks = {axis: lax.axis_index(axis) for axis in ("fsdp", "tp")}

        def view(spot):
            (kind, which), index = spot
            ref = (ins if kind == "in" else outs)[which]
            index = index(ranks) if callable(index) else index
            return ref.at[index] if index else ref

        source, target, place = self.steps[number][:3]
        if place is None:
            return pltpu.make_async_copy(view(source), view(target), send.at[number])
        axis, bit = place
        return pltpu.make_async_remote_copy(
            src_ref=view(source),
            dst_ref=view(target),
            send_sem=send.at[number],
            recv_sem=recv.at[number],
            device_id={axis: ranks[axis] ^ bit},
            device_id_type=pl.DeviceIdType.MESH,
        )

    def begin(self, ins, outs, send, recv):
        self.meet()
        for number in range(len(self.steps)):
            self.describe(number, ins, outs, send, recv).start()

    def finish(self, ins, outs, send, recv):
        for number in range(len(self.steps)):
            self.describe(number, ins, outs, send, recv).wait()

    def kernel(self, *refs):
        ins, outs = refs[: len(self.inputs)], refs[len(self.inputs) : len(self.inputs) + len(self.outputs)]
        send, recv = refs[-2:]
        self.meet()
        started, arrived = {}, set()

        def arrive(number):
            if number not in arrived:
                arrived.add(number)
                if self.steps[number][2]:
                    started[number].wait_recv()
                else:
                    started[number].wait()

        for number in sorted(range(len(self.steps)), key=lambda i: self.steps[i][4]):
            for need in self.steps[number][3]:
                arrive(need)
            started[number] = self.describe(number, ins, outs, send, recv)
            started[number].start()
        for number in sorted(range(len(self.steps)), key=lambda i: self.steps[i][5]):
            arrive(number)
            if self.steps[number][2]:
                started[number].wait_send()

    def semaphores(self):
        return [pltpu.SemaphoreType.DMA((len(self.steps),)), pltpu.SemaphoreType.DMA((len(self.steps),))]

    def run(self, number, time, name):
        count = len(self.steps)
        anywhere = pl.BlockSpec(memory_space=pl.ANY)
        made = pl.pallas_call(
            self.kernel,
            out_shape=self.outputs,
            in_specs=[anywhere] * len(self.inputs),
            out_specs=[anywhere] * len(self.outputs),
            scratch_shapes=[pltpu.SemaphoreType.DMA((count,)), pltpu.SemaphoreType.DMA((count,))],
            compiler_params=pltpu.CompilerParams(collective_id=number, has_side_effects=True),
            cost_estimate=cost(time),
            name=name,
        )(*self.inputs)
        self.made = list(made)

    def get(self, spot):
        return [self.made[part[1]] for part in spot] if isinstance(spot, list) else self.made[spot[1]]


def trade_slots(blocks, axis):
    return [blocks[0]] + [exchange(blocks[slot], axis, slot) for slot in range(1, len(blocks))]


def after(value, *others):
    return lax.optimization_barrier((value, *others))[0]


def local(
    inputs,
    cotangent,
    lengths,
    routes,
    attn_gain,
    moe_gain,
    router_weight,
    query_weight,
    key_weight,
    value_weight,
    output_weight,
    gate_weight,
    up_weight,
    down_weight,
):
    tensor_count = lax.axis_size("tp")
    tensor_rank = lax.axis_index("tp")
    shard_rank = lax.axis_index("fsdp")
    micro, rows, width = inputs.shape
    span = rows * tensor_count
    experts, shard_width, hidden = gate_weight.shape
    steps = range(micro)
    slots, blocks = tensor_count, lax.axis_size("fsdp")
    slot_ranks = [tensor_rank ^ slot for slot in range(slots)]
    odd, upper = tensor_rank % 2 == 1, tensor_rank // 2 % 2 == 1
    info_all = jnp.concatenate([jnp.stack([shard_rank, tensor_rank]).astype(jnp.int32), lengths])
    infos = [jnp.stack([info_all[0], info_all[1], info_all[2 + m]]) for m in steps]

    small = jnp.concatenate([router_weight, attn_gain[:, None], moe_gain[:, None]], axis=1).astype(f32)
    small = jnp.pad(small, ((0, 0), (0, LANES - small.shape[1])))
    qkv_local = jnp.concatenate([query_weight, key_weight, value_weight], axis=1)
    qkv_cols = qkv_local.shape[1]

    stacked = jnp.stack(
        [gate_weight.transpose(1, 0, 2), up_weight.transpose(1, 0, 2), down_weight.transpose(2, 0, 1)], axis=1
    )
    expert_local = (
        stacked.reshape(shard_width, 3, experts // PAIR, PAIR, hidden)
        .transpose(0, 2, 1, 3, 4)
        .reshape(shard_width, 3 * experts * hidden)
    )

    row_place = jnp.arange(rows, dtype=jnp.int32)
    span_pos = jnp.concatenate([shard_rank * span + rank * rows + row_place for rank in slot_ranks])
    cos_row, sin_row = rope_tables(span_pos)
    row_pos = shard_rank * span + tensor_rank * rows + row_place
    valid = row_pos[None, :] < lengths[:, None]
    own_grads = jnp.where(valid[:, :, None], cotangent, jnp.zeros_like(cotangent))

    x_slots, queries, kvs, kv_alls, gm_slots = [], [], [], [], []
    for m in range(micro + 1):
        moves = Moves()
        wanted = {}
        if m < micro:
            wanted["x"] = moves.gather_tp(after(inputs[m], kvs[-1]) if m else inputs[m])
        if m:
            wanted["kv"] = moves.gather_fsdp(kvs[m - 1])
        if m == 0:
            wanted["weights"] = moves.gather_fsdp(qkv_local)
            wanted["small"] = moves.gather_both(small)
            wanted["out"] = moves.gather_both(output_weight.T)
        if m == micro:
            wanted["gm"] = moves.gather_tp(own_grads[0])
        moves.run(m, 25, "open")
        if m == 0:
            qkv_full, router_full, gains = place_weights(
                info_all, moves.get(wanted["weights"]), moves.get(wanted["small"]), experts
            )
            gain_attn, gain_moe = gains[0:1], gains[1:2]
            out_all = moves.get(wanted["out"])
        if m:
            kv_alls.append(moves.get(wanted["kv"]))
        if m < micro:
            x_slots.append([inputs[m]] + moves.get(wanted["x"]))
            query, kv = project_qkv(x_slots[m], gain_attn, qkv_full, cos_row, sin_row)
            queries.append(query)
            kvs.append(kv)
        else:
            gm_slots.append([own_grads[0]] + moves.get(wanted["gm"]))
    for m in range(1, micro):
        gm_slots.append(trade_slots([after(own_grads[m], gm_slots[m - 1][-1])] * slots, "tp"))

    expert_full = lax.all_gather(after(expert_local, kv_alls[-1]), "fsdp", axis=0, tiled=True)
    order = kv_alls[-1]
    attended, logs, att_owns, middles, normeds, moe_slots = [], [], [], [], [], []
    for m in steps:
        *att_slots, log_total = attend(after(infos[m], order), queries[m], kv_alls[m], rows)
        if m == 0:
            out_full = place_output_weight(after(info_all, log_total), out_all)
        moves = Moves()
        traded = moves.trade_tp(att_slots)
        moves.run(micro + 1 + m, 8, "trade")
        att_own, middle, normed = close_attention(
            inputs[m], gain_moe, out_full, [att_slots[0]] + moves.get(traded)
        )
        order = middle
        attended.append(att_slots)
        logs.append(log_total)
        att_owns.append(att_own)
        middles.append(middle)
        normeds.append(normed)
        if m == 0:
            moe_slots.append(trade_slots([normed] * slots, "tp"))

    expert_outs, gin_parts = [], []
    for m in steps:
        ride = Moves()
        ahead = ride.share_tp(normeds[m + 1]) if m + 1 < micro else None
        behind = ride.trade_tp(expert_outs[m - 1][:slots]) if m else None
        results = experts_both(
            after(infos[m], order),
            routes[m],
            router_full,
            expert_full,
            moe_slots[m],
            gm_slots[m],
            ride,
            2 * micro + 4 + m,
        )
        expert_outs.append(results)
        if ahead:
            moe_slots.append([normeds[m + 1]] + ride.get(ahead))
        if behind:
            gin_parts.append([expert_outs[m - 1][0]] + ride.get(behind))
        order = results[2 * slots]
    lows_g = [results[2 * slots + 1] for results in expert_outs]
    lows_h = [results[2 * slots + 2] for results in expert_outs]
    ride = Moves()
    behind = ride.trade_tp(expert_outs[-1][:slots])
    expert_grad = expert_grads(moe_slots, gm_slots, lows_g, lows_h, ride, 3 * micro + 4)
    gin_parts.append([expert_outs[-1][0]] + ride.get(behind))
    expert_sum = lax.psum_scatter(expert_grad, "fsdp", scatter_dimension=0, tiled=True)

    sums = 0.0
    order = expert_grad
    grad_middles, grad_attns, grad_slots = [], [], []
    moves = Moves()
    for m in steps:
        grad_middle, grad_attn, sums_moe, *grads = moe_back(
            after(infos[m], order),
            gin_parts[m],
            expert_outs[m][2 * slots],
            router_full,
            middles[m],
            normeds[m],
            gain_moe,
            cotangent[m],
            out_full,
            slots,
        )
        order = sums_moe
        sums = sums + sums_moe
        grad_middles.append(grad_middle)
        grad_attns.append(grad_attn)
        grad_slots.append((grads[0], moves.trade_tp(grads)))
    moves.run(3 * micro + 5, 12, "trade_back")
    grad_slots = [[own] + moves.get(spots) for own, spots in grad_slots]
    out_keep, out_send = weight_grad(after(info_all, order), grad_attns, att_owns, blocks)
    order = out_keep

    out_met = exchange(out_send, "fsdp", 1)
    out_stack = (out_keep.astype(f32) + out_met.astype(f32)).astype(bf16)

    dqs, dkvs, mixed_parts = [], [], []
    for m in steps:
        dq, *dkv = attend_back(
            after(infos[m], order), queries[m], kv_alls[m], logs[m], cos_row, sin_row, attended[m], grad_slots[m]
        )
        mixed = expert_outs[m][slots : 2 * slots]
        mixed_parts.append(trade_slots([mixed[0]] + [after(part, order) for part in mixed[1:]], "tp"))
        order = dq
        dqs.append(dq)
        if m + 1 < micro:
            dkv = [dkv[0]] + [exchange(dkv[j], "fsdp", reversed_bits(j, blocks)) for j in range(1, blocks)]
        dkvs.append(dkv)

    normed_all, qkv_grads, normed_parts = [], [], []
    for m in steps:
        if m + 1 == micro:
            moves = Moves()
            came = moves.trade_fsdp(dkvs[m])
            met = [moves.trade_tp(parts) for parts in normed_parts]
            moves.run(2 * micro + 1, 24, "close_keys")
            dkvs[m] = [dkvs[m][0]] + moves.get(came)
            normed_parts = [[parts[0]] + moves.get(spots) for parts, spots in zip(normed_parts, met)]
        *parts, grads, normed_attn, sums_attn = qkv_back(
            dqs[m], dkvs[m], cos_row, sin_row, after(gain_attn, order), qkv_full, x_slots[m]
        )
        order = sums_attn
        sums = sums + jnp.pad(sums_attn[0:1], ((1, 22), (0, 0)))
        normed_all.append(normed_attn)
        qkv_grads.append(grads)
        normed_parts.append(parts)
    qkv_keep, qkv_send = weight_grad(after(info_all, order), normed_all, qkv_grads, blocks)
    table = jnp.pad(sums, ((0, LANES - sums.shape[0]), (0, 0))).T

    moves = Moves()
    met = moves.trade_tp(normed_parts[-1])
    near, far = moves.trade_stack(qkv_keep, 0, blocks), moves.trade_stack(qkv_send, blocks // 2, blocks)
    out_spot = moves.trade_stack(out_stack, 0, blocks)
    table_spot = moves.trade_rows(table, blocks)
    moves.run(2 * micro + 2, 24, "close_weights")
    normed_parts[-1] = [normed_parts[-1][0]] + moves.get(met)
    total = lambda first, *stacks: first.astype(f32) + sum(jnp.sum(stack.astype(f32), axis=0) for stack in stacks)
    out_sum = total(out_stack[0], moves.get(out_spot)).astype(bf16)
    own_rows = lax.dynamic_slice_in_dim(table, shard_rank * shard_width, shard_width, 0)
    table_sum = total(own_rows, moves.get(table_spot))
    qkv_sum = total(qkv_keep[0], moves.get(near), moves.get(far))
    head_cols, few = output_weight.shape[0], small.shape[0]
    out_parts = [out_sum[:, slot * head_cols : (slot + 1) * head_cols] for slot in range(slots)]
    table_parts = [lax.dynamic_slice_in_dim(table_sum, rank * few, few, 0) for rank in slot_ranks]
    moves = Moves()
    out_spots, table_spots = moves.trade_tp(out_parts), moves.trade_tp(table_parts)
    moves.run(2 * micro + 3, 6, "close_small")
    out_final = sum(part.astype(f32) for part in [out_parts[0]] + moves.get(out_spots))
    small_sum = sum([table_parts[0]] + moves.get(table_spots))

    outputs = close_outputs(after(info_all, normed_parts[-1][-1]), mixed_parts, middles, slots)
    gate_sum, up_sum, down_sum = unpack_experts(expert_sum)
    input_grad = close_input_grad(normed_parts, grad_middles, inputs, gain_attn)
    q_cols, k_cols = query_weight.shape[1], key_weight.shape[1]
    return (
        outputs,
        input_grad,
        small_sum[:, 1],
        small_sum[:, 0],
        small_sum[:, 8 : 8 + experts],
        qkv_sum[:, :q_cols],
        qkv_sum[:, q_cols : q_cols + k_cols],
        qkv_sum[:, q_cols + k_cols : qkv_cols],
        out_final.T,
        gate_sum,
        up_sum,
        down_sum,
    )


def solution(mesh):
    rows_spec = P(None, ("fsdp", "tp"), None)
    small_specs = (P(("fsdp", "tp")), P(("fsdp", "tp")), P(("fsdp", "tp"), None))
    weight_specs = (
        P("fsdp", "tp"),
        P("fsdp", "tp"),
        P("fsdp", "tp"),
        P("tp", "fsdp"),
        P(None, "fsdp", "tp"),
        P(None, "fsdp", "tp"),
        P(None, "tp", "fsdp"),
    )
    in_specs = (rows_spec, rows_spec, P(), P(None, "fsdp", None)) + small_specs + weight_specs
    out_specs = (rows_spec, rows_spec) + small_specs + weight_specs
    return jax.shard_map(local, mesh=mesh, in_specs=in_specs, out_specs=out_specs, check_vma=False)
```

```python
import functools

import jax
import jax.numpy as jnp
from jax import lax
from jax.experimental import pallas as pl
from jax.experimental.pallas import tpu as pltpu
from jax.sharding import PartitionSpec as P

HD = 64
LANES = 128
PAIR = 2
EPS = 1e-06
FILL = -1e30
THETA = 10000.0
VMEM_CAP = 60 * 1024 * 1024
f32 = jnp.float32
bf16 = jnp.bfloat16


def dot_nn(a, b):
    return lax.dot_general(a, b, (((1,), (0,)), ((), ())), preferred_element_type=f32)


def dot_nt(a, b):
    return lax.dot_general(a, b, (((1,), (1,)), ((), ())), preferred_element_type=f32)


def swap_halves(values):
    lane = lax.broadcasted_iota(jnp.int32, values.shape, values.ndim - 1)
    ahead = pltpu.roll(values, values.shape[-1] - HD // 2, values.ndim - 1)
    back = pltpu.roll(values, HD // 2, values.ndim - 1)
    return jnp.where(lane % HD < HD // 2, ahead, back)


def rope_tables(positions):
    half = HD // 2
    freqs = THETA ** (-jnp.arange(half, dtype=f32) * 2.0 / HD)
    angles = positions.astype(f32)[:, None] * freqs[None, :]
    cosine, sine = jnp.cos(angles), jnp.sin(angles)
    cos_row = jnp.concatenate([cosine] * 4, axis=1)
    sin_row = jnp.concatenate([-sine, sine] * 2, axis=1)
    return cos_row, sin_row


def head_rows(values, head):
    key_head, member = head // 2, head % 2
    pair = values[:, key_head * LANES : (key_head + 1) * LANES]
    if member != key_head:
        pair = pltpu.roll(pair, HD, 1)
    lane = lax.broadcasted_iota(jnp.int32, pair.shape, 1)
    return jnp.where(lane // HD == key_head, pair, jnp.zeros_like(pair))


def join_heads(first, second, key_head):
    if key_head == 0:
        second = pltpu.roll(second, HD, 1)
    else:
        first = pltpu.roll(first, HD, 1)
    lane = lax.broadcasted_iota(jnp.int32, first.shape, 1)
    return jnp.where(lane < HD, first, second)


def cost(microseconds):
    return pl.CostEstimate(flops=int(microseconds * 6e7), bytes_accessed=1024, transcendentals=0)


def params():
    return pltpu.CompilerParams(vmem_limit_bytes=VMEM_CAP)


def riding(number):
    return pltpu.CompilerParams(vmem_limit_bytes=VMEM_CAP, collective_id=number, has_side_effects=True)


def shape(dims, kind):
    return jax.ShapeDtypeStruct(dims, kind)


def normalised(x, gain):
    inverse = lax.rsqrt(jnp.mean(x * x, axis=-1, keepdims=True) + EPS)
    unit = x * inverse
    return inverse, unit, unit * gain


def qkv_kernel(*refs):
    x_refs = refs[:-6]
    gain_ref, w_ref, cos_ref, sin_ref, q_ref, kv_ref = refs[-6:]
    rows = x_refs[0].shape[0]
    for slot, x_ref in enumerate(x_refs):
        here = slice(slot * rows, (slot + 1) * rows)
        cos_row, sin_row = cos_ref[here, :], sin_ref[here, :]
        _, _, normed = normalised(x_ref[...].astype(f32), gain_ref[...])
        pre = dot_nn(normed.astype(bf16), w_ref[...])
        for part in range(3):
            cols = pre[:, part * LANES : (part + 1) * LANES]
            turned = cols * cos_row + swap_halves(cols) * sin_row
            if part < 2:
                q_ref[here, part * LANES : (part + 1) * LANES] = (turned * HD ** (-0.5)).astype(bf16)
            else:
                kv_ref[here, 0:LANES] = turned.astype(bf16)
        kv_ref[here, LANES : 2 * LANES] = pre[:, 3 * LANES : 4 * LANES].astype(bf16)


def project_qkv(x_slots, gain, weight, cos_row, sin_row):
    span = cos_row.shape[0]
    return pl.pallas_call(
        qkv_kernel,
        out_shape=[shape((span, 2 * LANES), bf16), shape((span, 2 * LANES), bf16)],
        compiler_params=params(),
        cost_estimate=cost(3),
        name="project_qkv",
    )(*x_slots, gain, weight, cos_row, sin_row)


def reversed_bits(index, count):
    result, bit = 0, 1
    while bit < count:
        result = result + ((index // bit) % 2) * (count // (2 * bit))
        bit *= 2
    return result


def places(rank, rows, dims, axis):
    index = lax.broadcasted_iota(jnp.int32, dims, axis)
    return (rank ^ (index // rows)) * rows + index % rows


def allowed_keys(rank, rows, span, key_start, query_start, length):
    key_pos = key_start + places(rank, rows, (span, span), 0)
    query_pos = query_start + places(rank, rows, (span, span), 1)
    return (key_pos <= query_pos) & (key_pos < length)


def block_kind(info_ref, j, span, count):
    mine, length = info_ref[0], info_ref[2]
    other = mine ^ reversed_bits(j, count)
    wanted = (other <= mine) & (mine * span < length) & (other * span < length)
    edge = (other == mine) | ((other + 1) * span > length)
    return other, wanted, edge


def attend_kernel(info_ref, q_ref, kv_ref, *refs):
    heads, best, total, accum = refs[-4:]
    out_refs, log_ref = refs[:-5], refs[-5]
    j = pl.program_id(0)
    count = pl.num_programs(0)
    mine, rank, length = info_ref[0], info_ref[1], info_ref[2]
    rows = out_refs[0].shape[0]
    span = q_ref.shape[0]
    other, wanted, edge = block_kind(info_ref, j, span, BLOCKS[0])

    @pl.when(j == 0)
    def _():
        values = q_ref[...].astype(f32)
        for head in range(4):
            heads[head] = head_rows(values, head).astype(bf16)
        best[...] = jnp.full(best.shape, FILL, f32)
        total[...] = jnp.zeros(total.shape, f32)
        accum[...] = jnp.zeros(accum.shape, f32)

    def block(masked):
        keys = kv_ref[0, :, :LANES]
        values_t = kv_ref[0, :, LANES:].astype(f32).T.astype(bf16)
        if masked:
            allowed = allowed_keys(rank, rows, span, other * span, mine * span, length)
        for head in range(4):
            scores = dot_nt(keys, heads[head])
            if masked:
                scores = jnp.where(allowed, scores, FILL)
            old = best[head : head + 1]
            new = jnp.maximum(old, jnp.max(scores, axis=0, keepdims=True))
            factor = jnp.exp(old - new)
            weights = jnp.exp(scores - new)
            if masked:
                weights = jnp.where(allowed, weights, 0.0)
            best[head : head + 1] = new
            total[head : head + 1] = total[head : head + 1] * factor + jnp.sum(weights, axis=0, keepdims=True)
            accum[head] = accum[head] * factor + dot_nn(values_t, weights.astype(bf16))

    @pl.when(wanted & edge)
    def _():
        block(True)

    @pl.when(wanted & jnp.logical_not(edge))
    def _():
        block(False)

    @pl.when(j == count - 1)
    def _():
        live = mine * span < length
        for key_head in range(2):
            pair = []
            for member in range(2):
                head = key_head * 2 + member
                sums = jnp.where(live, total[head : head + 1], 1.0)
                log_ref[head : head + 1] = best[head : head + 1] + jnp.log(sums)
                pair.append((accum[head] * (1.0 / sums)).T)
            joined = join_heads(pair[0], pair[1], key_head).astype(bf16)
            for slot, out_ref in enumerate(out_refs):
                out_ref[:, key_head * LANES : (key_head + 1) * LANES] = joined[slot * rows : (slot + 1) * rows]


BLOCKS = [0]


def attend(info, query, kv_all, rows):
    span, cols = query.shape
    blocks = kv_all.shape[0]
    slots = span // rows
    BLOCKS[0] = blocks
    return pl.pallas_call(
        attend_kernel,
        grid_spec=pltpu.PrefetchScalarGridSpec(
            num_scalar_prefetch=1,
            grid=(blocks,),
            in_specs=[
                pl.BlockSpec((span, cols), lambda j, info_ref: (0, 0)),
                pl.BlockSpec((1, span, 2 * LANES), lambda j, info_ref: (j, 0, 0)),
            ],
            out_specs=[pl.BlockSpec((rows, cols), lambda j, info_ref: (0, 0))] * slots
            + [pl.BlockSpec((8, span), lambda j, info_ref: (0, 0))],
            scratch_shapes=[
                pltpu.VMEM((4, span, LANES), bf16),
                pltpu.VMEM((8, span), f32),
                pltpu.VMEM((8, span), f32),
                pltpu.VMEM((4, LANES, span), f32),
            ],
        ),
        out_shape=[shape((rows, cols), bf16)] * slots + [shape((8, span), f32)],
        compiler_params=params(),
        cost_estimate=cost(12),
        name="attend",
    )(info, query, kv_all)


def attend_back_kernel(slots, info_ref, q_ref, kv_ref, log_ref, cos_ref, sin_ref, *refs):
    out_refs, grad_refs = refs[:slots], refs[slots : 2 * slots]
    dq_ref, keep_ref, send_ref, heads, grads, delta, accum, dkv = refs[2 * slots :]
    j = pl.program_id(0)
    count = pl.num_programs(0)
    mine, rank, length = info_ref[0], info_ref[1], info_ref[2]
    span, cols = q_ref.shape
    rows = span // slots
    other, wanted, edge = block_kind(info_ref, j, span, BLOCKS[0])

    @pl.when(j == 0)
    def _():
        values = q_ref[...].astype(f32)
        attended = jnp.concatenate([ref[...] for ref in out_refs], axis=0).astype(f32)
        grad = jnp.concatenate([ref[...] for ref in grad_refs], axis=0).astype(f32)
        product = grad * attended
        for head in range(4):
            heads[head] = head_rows(values, head).astype(bf16)
            grads[head] = head_rows(grad, head).astype(bf16)
            delta[head : head + 1] = jnp.sum(head_rows(product, head).T, axis=0, keepdims=True)
        accum[...] = jnp.zeros(accum.shape, f32)

    def block(masked):
        keys = kv_ref[0, :, :LANES]
        values = kv_ref[0, :, LANES:]
        keys_t = keys.astype(f32).T.astype(bf16)
        if masked:
            allowed = allowed_keys(rank, rows, span, other * span, mine * span, length)
        grad_keys = jnp.zeros((span, LANES), f32)
        grad_values = jnp.zeros((span, LANES), f32)
        for head in range(4):
            scores = dot_nt(keys, heads[head])
            probs = jnp.exp(scores - log_ref[head : head + 1])
            if masked:
                probs = jnp.where(allowed, probs, 0.0)
            grad_probs = dot_nt(values, grads[head])
            grad_scores = (probs * (grad_probs - delta[head : head + 1])).astype(bf16)
            grad_values = grad_values + dot_nn(probs.astype(bf16), grads[head])
            grad_keys = grad_keys + dot_nn(grad_scores, heads[head])
            accum[head] = accum[head] + dot_nn(keys_t, grad_scores)
        dkv[:, 0:LANES] = grad_keys.astype(bf16)
        dkv[:, LANES : 2 * LANES] = grad_values.astype(bf16)

    @pl.when(wanted & edge)
    def _():
        block(True)

    @pl.when(wanted & jnp.logical_not(edge))
    def _():
        block(False)

    @pl.when(jnp.logical_not(wanted))
    def _():
        dkv[...] = jnp.zeros(dkv.shape, bf16)

    @pl.when(j < count // 2)
    def _():
        keep_ref[0] = dkv[...]

    @pl.when(j >= count // 2)
    def _():
        send_ref[0] = dkv[...]

    @pl.when(j == count - 1)
    def _():
        for key_head in range(2):
            pair = [accum[key_head * 2 + member].T for member in range(2)]
            joined = join_heads(pair[0], pair[1], key_head) * HD ** (-0.5)
            turned = joined * cos_ref[...] - swap_halves(joined) * sin_ref[...]
            dq_ref[:, key_head * LANES : (key_head + 1) * LANES] = turned.astype(bf16)


def attend_back(info, query, kv_all, log_total, cos_row, sin_row, att_slots, grad_slots):
    span, cols = query.shape
    blocks, slots = kv_all.shape[0], len(att_slots)
    rows, half = span // slots, blocks // 2
    BLOCKS[0] = blocks
    fixed = lambda *dims: pl.BlockSpec(dims, lambda j, info_ref: (0,) * len(dims))
    return pl.pallas_call(
        functools.partial(attend_back_kernel, slots),
        grid_spec=pltpu.PrefetchScalarGridSpec(
            num_scalar_prefetch=1,
            grid=(blocks,),
            in_specs=[
                fixed(span, cols),
                pl.BlockSpec((1, span, 2 * LANES), lambda j, info_ref: (j, 0, 0)),
                fixed(8, span),
                fixed(span, LANES),
                fixed(span, LANES),
            ]
            + [fixed(rows, cols)] * (2 * slots),
            out_specs=[
                fixed(span, cols),
                pl.BlockSpec((1, span, 2 * LANES), lambda j, info_ref: (jnp.minimum(j, half - 1), 0, 0)),
                pl.BlockSpec((1, span, 2 * LANES), lambda j, info_ref: (jnp.maximum(j - half, 0), 0, 0)),
            ],
            scratch_shapes=[
                pltpu.VMEM((4, span, LANES), bf16),
                pltpu.VMEM((4, span, LANES), bf16),
                pltpu.VMEM((8, span), f32),
                pltpu.VMEM((4, LANES, span), f32),
                pltpu.VMEM((span, 2 * LANES), bf16),
            ],
        ),
        out_shape=[shape((span, cols), bf16)] + [shape((half, span, 2 * LANES), bf16)] * 2,
        compiler_params=params(),
        cost_estimate=cost(18),
        name="attend_back",
    )(info, query, kv_all, log_total, cos_row, sin_row, *att_slots, *grad_slots)


def middle_kernel(x_ref, gain_ref, w_ref, *refs):
    att_refs, (att_all, middle_ref, normed_ref) = refs[:-3], refs[-3:]
    cols = att_refs[0].shape[1]
    for slot, att_ref in enumerate(att_refs):
        att_all[:, slot * cols : (slot + 1) * cols] = att_ref[...]
    middle = x_ref[...].astype(f32) + dot_nt(att_all[...], w_ref[...])
    middle_ref[...] = middle
    normed_ref[...] = normalised(middle, gain_ref[...])[2].astype(bf16)


def close_attention(x, gain, weight, att_slots):
    rows, width = x.shape
    return pl.pallas_call(
        middle_kernel,
        out_shape=[shape((rows, weight.shape[1]), bf16), shape((rows, width), f32), shape((rows, width), bf16)],
        compiler_params=params(),
        cost_estimate=cost(2),
        name="middle",
    )(x, gain, weight, *att_slots)


def expert_kernel(slots, ride, info_ref, routes_ref, router_ref, w_ref, *refs):
    x_refs, gm_refs = refs[:slots], refs[slots : 2 * slots]
    ride_in, refs = refs[2 * slots : 2 * slots + len(ride.inputs)], refs[2 * slots + len(ride.inputs) :]
    gin_refs, mixed_refs, refs = refs[:slots], refs[slots : 2 * slots], refs[2 * slots :]
    gates_ref, low_g, low_h = refs[:3]
    ride_out, refs = refs[3 : 3 + len(ride.outputs)], refs[3 + len(ride.outputs) :]
    x_all, gm_all, gates, mixed, gin, gate_sums, send, recv = refs
    step = pl.program_id(0)
    last = pl.num_programs(0) - 1
    span, width = x_all.shape
    rows = span // slots
    wide = PAIR * LANES
    chunk = 256
    rank = lax.axis_index("tp")

    @pl.when(step == 0)
    def _():
        ride.begin(ride_in, ride_out, send, recv)
        lane = lax.broadcasted_iota(jnp.int32, (rows, LANES), 1)
        for slot in range(slots):
            here = slice(slot * rows, (slot + 1) * rows)
            x_all[here, :] = x_refs[slot][...]
            gm_all[here, :] = gm_refs[slot][...]
            named = routes_ref[pl.ds(pl.multiple_of((rank ^ slot) * rows, rows), rows), :]
            picked = lane == named[:, 0:1]
            for k in range(1, named.shape[1]):
                picked = picked | (lane == named[:, k : k + 1])
            logits = jnp.where(picked, dot_nn(x_refs[slot][...], router_ref[...]), FILL)
            peak = jnp.max(logits, axis=1, keepdims=True)
            exps = jnp.where(picked, jnp.exp(logits - peak), 0.0)
            gates[here, :] = exps / jnp.sum(exps, axis=1, keepdims=True)
        gates_ref[...] = gates[0:rows, :]
        mixed[...] = jnp.zeros(mixed.shape, f32)
        gin[...] = jnp.zeros(gin.shape, f32)
        gate_sums[...] = jnp.zeros(gate_sums.shape, f32)

    def rows_step(i, _):
        here = pl.ds(pl.multiple_of(i * chunk, chunk), chunk)
        pre = dot_nn(x_all[here, :], w_ref[:, : 2 * wide])
        gate_pre, up_pre = pre[:, :wide], pre[:, wide:]
        back = dot_nn(gm_all[here, :], w_ref[:, 2 * wide :])
        sig = 1.0 / (1.0 + jnp.exp(-gate_pre))
        silu = gate_pre * sig
        hidden = silu * up_pre
        lane = lax.broadcasted_iota(jnp.int32, (chunk, LANES), 1)
        product = hidden * back
        spread = []
        sums = gate_sums[here, :]
        for member in range(PAIR):
            hit = lane == step * PAIR + member
            gate = jnp.sum(jnp.where(hit, gates[here, :], 0.0), axis=1, keepdims=True)
            spread.append(jnp.broadcast_to(gate, (chunk, LANES)))
            amount = jnp.sum(product[:, member * LANES : (member + 1) * LANES], axis=1, keepdims=True)
            sums = sums + jnp.where(hit, amount, 0.0)
        gate_sums[here, :] = sums
        factor = jnp.concatenate(spread, axis=1)
        grad_hidden = factor * back
        low_hidden = (factor * hidden).astype(bf16)
        grad_up = (grad_hidden * silu).astype(bf16)
        grad_gate = (grad_hidden * up_pre * (sig * (1.0 + gate_pre * (1.0 - sig)))).astype(bf16)
        low_h[here, :] = low_hidden
        low_g[here, 0:wide] = grad_gate
        low_g[here, wide : 2 * wide] = grad_up
        mixed[here, :] += dot_nt(low_hidden, w_ref[:, 2 * wide :])
        gin[here, :] += dot_nt(low_g[here, :], w_ref[:, : 2 * wide])
        return 0

    lax.fori_loop(0, span // chunk, rows_step, 0)

    @pl.when(step == last)
    def _():
        for slot in range(slots):
            here = slice(slot * rows, (slot + 1) * rows)
            mixed_refs[slot][...] = mixed[here, :].astype(bf16)
            gin_refs[slot][:, 0:width] = gin[here, :].astype(bf16)
            gin_refs[slot][:, width : width + LANES] = gate_sums[here, :].astype(bf16)
        ride.finish(ride_in, ride_out, send, recv)


def experts_both(info, routes, router, weight, x_slots, gm_slots, ride, number):
    rows, width = x_slots[0].shape
    slots = len(x_slots)
    span = rows * slots
    wide = PAIR * LANES
    steps = weight.shape[1] // (3 * wide)
    fixed = lambda *dims: pl.BlockSpec(dims, lambda i, info_ref: (0,) * len(dims))
    moving = lambda height, cols: pl.BlockSpec((height, cols), lambda i, info_ref: (0, i))
    anywhere = pl.BlockSpec(memory_space=pl.ANY)
    results = pl.pallas_call(
        functools.partial(expert_kernel, slots, ride),
        grid_spec=pltpu.PrefetchScalarGridSpec(
            num_scalar_prefetch=1,
            grid=(steps,),
            in_specs=[fixed(*routes.shape), fixed(*router.shape), moving(width, 3 * wide)]
            + [fixed(rows, width)] * (2 * slots)
            + [anywhere] * len(ride.inputs),
            out_specs=[fixed(rows, width + LANES)] * slots
            + [fixed(rows, width)] * slots
            + [fixed(rows, LANES), moving(span, 2 * wide), moving(span, wide)]
            + [anywhere] * len(ride.outputs),
            scratch_shapes=[
                pltpu.VMEM((span, width), bf16),
                pltpu.VMEM((span, width), bf16),
                pltpu.VMEM((span, LANES), f32),
                pltpu.VMEM((span, width), f32),
                pltpu.VMEM((span, width), f32),
                pltpu.VMEM((span, LANES), f32),
            ]
            + ride.semaphores(),
        ),
        out_shape=[shape((rows, width + LANES), bf16)] * slots
        + [shape((rows, width), bf16)] * slots
        + [shape((rows, LANES), f32), shape((span, steps * 2 * wide), bf16), shape((span, steps * wide), bf16)]
        + ride.outputs,
        compiler_params=riding(number),
        cost_estimate=cost(24),
        name="experts",
    )(info, routes, router, weight, *x_slots, *gm_slots, *ride.inputs)
    ride.made = list(results[2 * slots + 3 :])
    return results[: 2 * slots + 3]


def expert_grad_kernel(micro, slots, ride, *refs):
    count = micro * slots
    send, recv = refs[-2:]
    given = 2 * count + 2 * micro
    ride_in = refs[given : given + len(ride.inputs)]
    ride_out = refs[given + len(ride.inputs) + 1 : given + len(ride.inputs) + 1 + len(ride.outputs)]
    x_refs, gm_refs = refs[:count], refs[count : 2 * count]
    g_refs, h_refs = refs[2 * count : 2 * count + micro], refs[2 * count + micro : 2 * count + 2 * micro]
    dw_ref, (x_t, gm_t) = refs[given + len(ride.inputs)], refs[-4:-2]
    rows = x_refs[0].shape[0]
    width = x_t.shape[0]
    wide = PAIR * LANES
    chunk = 256

    @pl.when(pl.program_id(0) == 0)
    def _():
        ride.begin(ride_in, ride_out, send, recv)
        for i in range(count):
            x_t[:, i * rows : (i + 1) * rows] = x_refs[i][...].T
            gm_t[:, i * rows : (i + 1) * rows] = gm_refs[i][...].T

    def weight_step(i, _):
        here = pl.ds(pl.multiple_of(i * chunk, chunk), chunk)
        g_sum, h_sum = 0.0, 0.0
        for m in range(micro):
            part = slice(m * slots * rows, (m + 1) * slots * rows)
            g_sum = g_sum + dot_nn(x_t[here, part], g_refs[m][...])
            h_sum = h_sum + dot_nn(gm_t[here, part], h_refs[m][...])
        dw_ref[here, 0 : 2 * wide] = g_sum.astype(bf16)
        dw_ref[here, 2 * wide : 3 * wide] = h_sum.astype(bf16)
        return 0

    lax.fori_loop(0, width // chunk, weight_step, 0)

    @pl.when(pl.program_id(0) == pl.num_programs(0) - 1)
    def _():
        ride.finish(ride_in, ride_out, send, recv)


def expert_grads(x_slots, gm_slots, lows_g, lows_h, ride, number):
    micro, slots = len(x_slots), len(x_slots[0])
    rows, width = x_slots[0][0].shape
    span = rows * slots
    wide = PAIR * LANES
    steps = lows_h[0].shape[1] // wide
    fixed = pl.BlockSpec((rows, width), lambda i: (0, 0))
    moving = lambda height, cols: pl.BlockSpec((height, cols), lambda i: (0, i))
    flat = [block for part in x_slots for block in part] + [block for part in gm_slots for block in part]
    anywhere = pl.BlockSpec(memory_space=pl.ANY)
    summed, *ride.made = pl.pallas_call(
        functools.partial(expert_grad_kernel, micro, slots, ride),
        grid=(steps,),
        in_specs=[fixed] * len(flat) + [moving(span, 2 * wide)] * micro + [moving(span, wide)] * micro
        + [anywhere] * len(ride.inputs),
        out_specs=[pl.BlockSpec((width, 3 * wide), lambda i: (0, i))] + [anywhere] * len(ride.outputs),
        out_shape=[shape((width, steps * 3 * wide), bf16)] + ride.outputs,
        scratch_shapes=[pltpu.VMEM((width, micro * span), bf16), pltpu.VMEM((width, micro * span), bf16)]
        + ride.semaphores(),
        compiler_params=riding(number),
        cost_estimate=cost(12),
        name="expert_grads",
    )(*flat, *lows_g, *lows_h, *ride.inputs)
    return summed


def moe_back_kernel(
    slots, info_ref, *refs
):
    parts, refs = refs[:slots], refs[slots:]
    gates_ref, router_ref, middle_ref, normed_ref, gain_ref, cot_ref, w_ref = refs[:7]
    refs = refs[7:]
    grad_middle_ref, grad_attn_ref, sums_ref = refs[:3]
    out_refs = refs[3:]
    rows, width = middle_ref.shape
    gate = lambda ref: ref[:, width : width + LANES].astype(f32)
    gates = gates_ref[...]
    gate_grads = sum(gate(part) for part in parts)
    grad_logits = gates * (gate_grads - jnp.sum(gates * gate_grads, axis=1, keepdims=True))
    grad_logits = grad_logits.astype(bf16)
    main = lambda ref: ref[:, 0:width].astype(f32)
    grad_moe = sum(main(part) for part in parts) + dot_nt(grad_logits, router_ref[...])
    middle, gain = middle_ref[...], gain_ref[...]
    inverse, unit, _ = normalised(middle, gain)
    weighted = grad_moe * gain
    inner = jnp.mean(weighted * middle, axis=-1, keepdims=True)
    grad_norm = inverse * weighted - middle * (inverse * inverse * inverse) * inner
    start = info_ref[0] * rows * slots + info_ref[1] * rows
    row_pos = start + lax.broadcasted_iota(jnp.int32, (rows, width), 0)
    grad_out = jnp.where(row_pos < info_ref[2], cot_ref[...].astype(f32), 0.0)
    grad_middle = grad_out + grad_norm
    grad_middle_ref[...] = grad_middle
    low = grad_middle.astype(bf16)
    grad_attn_ref[...] = low
    router_part = dot_nn(grad_logits.astype(f32).T.astype(bf16), normed_ref[...])
    gain_part = jnp.sum(grad_moe * unit, axis=0, keepdims=True)
    first = lax.broadcasted_iota(jnp.int32, (8, width), 0) == 0
    sums_ref[0:8, :] = jnp.where(first, jnp.broadcast_to(gain_part, (8, width)), 0.0)
    sums_ref[8:24, :] = router_part[0:16, :]
    grads = dot_nn(low, w_ref[...]).astype(bf16)
    cols = grads.shape[1] // slots
    for slot in range(slots):
        out_refs[slot][...] = grads[:, slot * cols : (slot + 1) * cols]


def moe_back(info, parts, gates, router, middle, normed, gain, cot, weight, slots):
    rows, width = middle.shape
    fixed = lambda value: pl.BlockSpec(value.shape, lambda i, info_ref: (0, 0))
    outs = [shape((rows, width), f32), shape((rows, width), bf16), shape((24, width), f32)]
    outs = outs + [shape((rows, weight.shape[1] // slots), bf16)] * slots
    operands = [*parts, gates, router, middle, normed, gain, cot, weight]
    return pl.pallas_call(
        functools.partial(moe_back_kernel, slots),
        grid_spec=pltpu.PrefetchScalarGridSpec(
            num_scalar_prefetch=1, grid=(1,), in_specs=[fixed(v) for v in operands], out_specs=[fixed(v) for v in outs]
        ),
        out_shape=outs,
        compiler_params=params(),
        cost_estimate=cost(3),
        name="moe_back",
    )(info, *operands)


def qkv_back_kernel(slots, blocks, dq_ref, cos_ref, sin_ref, gain_ref, w_ref, *refs):
    dkv_refs, refs = refs[:blocks], refs[blocks:]
    dkv = sum(ref[...].astype(f32) for ref in dkv_refs)
    x_refs, part_refs = refs[:slots], refs[slots : 2 * slots]
    grads_ref, normed_ref, sums_ref = refs[2 * slots :]
    rows = x_refs[0].shape[0]
    width = w_ref.shape[0]
    cols = dq_ref.shape[1]
    dk = dkv[:, 0:LANES]
    turned = dk * cos_ref[...] - swap_halves(dk) * sin_ref[...]
    grads_ref[:, 0:cols] = dq_ref[...]
    grads_ref[:, cols : cols + LANES] = turned.astype(bf16)
    grads_ref[:, cols + LANES : cols + 2 * LANES] = dkv[:, LANES : 2 * LANES].astype(bf16)
    total = jnp.zeros((1, width), f32)
    for slot in range(slots):
        here = slice(slot * rows, (slot + 1) * rows)
        _, unit, normed = normalised(x_refs[slot][...].astype(f32), gain_ref[...])
        normed_ref[here, :] = normed.astype(bf16)
        part = dot_nt(grads_ref[here, :], w_ref[...])
        part_refs[slot][...] = part.astype(bf16)
        total = total + jnp.sum(part * unit, axis=0, keepdims=True)
    first = lax.broadcasted_iota(jnp.int32, (8, width), 0) == 0
    sums_ref[...] = jnp.where(first, jnp.broadcast_to(total, (8, width)), 0.0)


def qkv_back(dq, dkv_parts, cos_row, sin_row, gain, weight, x_slots):
    slots = len(x_slots)
    rows, width = x_slots[0].shape
    span = rows * slots
    return pl.pallas_call(
        functools.partial(qkv_back_kernel, slots, len(dkv_parts)),
        out_shape=[shape((rows, width), bf16)] * slots
        + [shape((span, weight.shape[1]), bf16), shape((span, width), bf16), shape((8, width), f32)],
        compiler_params=params(),
        cost_estimate=cost(4),
        name="qkv_back",
    )(dq, cos_row, sin_row, gain, weight, *dkv_parts, *x_slots)


def input_grad_kernel(micro, slots, *refs):
    part_refs, middle_refs = refs[: slots * micro], refs[slots * micro : (slots + 1) * micro]
    x_ref, gain_ref, out_ref = refs[(slots + 1) * micro :]
    for m in range(micro):
        grad_normed = sum(ref[...].astype(f32) for ref in part_refs[slots * m : slots * (m + 1)])
        x = x_ref[m].astype(f32)
        inverse, _, _ = normalised(x, gain_ref[...])
        weighted = grad_normed * gain_ref[...]
        inner = jnp.mean(weighted * x, axis=-1, keepdims=True)
        out_ref[m] = middle_refs[m][...] + inverse * weighted - x * (inverse * inverse * inverse) * inner


def close_input_grad(parts, grad_middles, x, gain):
    micro = x.shape[0]
    return pl.pallas_call(
        functools.partial(input_grad_kernel, micro, len(parts[0])),
        out_shape=shape(x.shape, f32),
        compiler_params=params(),
        cost_estimate=cost(2),
        name="input_grad",
    )(*[part for group in parts for part in group], *grad_middles, x, gain)


def outputs_kernel(micro, slots, info_ref, *refs):
    part_refs, middle_refs, out_ref = refs[: slots * micro], refs[slots * micro : -1], refs[-1]
    rows, width = middle_refs[0].shape
    start = info_ref[0] * rows * slots + info_ref[1] * rows
    row_pos = start + lax.broadcasted_iota(jnp.int32, (rows, width), 0)
    for m in range(micro):
        mixed = sum(ref[...].astype(f32) for ref in part_refs[slots * m : slots * (m + 1)])
        total = middle_refs[m][...] + mixed
        out_ref[m] = jnp.where(row_pos < info_ref[2 + m], total, 0.0).astype(bf16)


def close_outputs(info, parts, middles, slots):
    micro = len(middles)
    rows, width = middles[0].shape
    operands = [part for group in parts for part in group] + middles
    fixed = pl.BlockSpec((rows, width), lambda i, info_ref: (0, 0))
    return pl.pallas_call(
        functools.partial(outputs_kernel, micro, slots),
        grid_spec=pltpu.PrefetchScalarGridSpec(
            num_scalar_prefetch=1,
            grid=(1,),
            in_specs=[fixed] * len(operands),
            out_specs=pl.BlockSpec((micro, rows, width), lambda i, info_ref: (0, 0, 0)),
        ),
        out_shape=shape((micro, rows, width), bf16),
        compiler_params=params(),
        cost_estimate=cost(2),
        name="outputs",
    )(info, *operands)


def weights_kernel(first, info_ref, all_ref, small_ref, weight_ref, router_ref, gains_ref, table):
    blocks, rows, _ = all_ref.shape
    slots, few = small_ref.shape[1:3]
    for j in range(blocks):
        place = info_ref[0] ^ reversed_bits(j, blocks)
        weight_ref[pl.ds(pl.multiple_of(place * rows, rows), rows), :] = all_ref[j]
        for slot in range(slots):
            start = place * rows + (info_ref[1] ^ slot) * few
            table[pl.ds(pl.multiple_of(start, few), few), :] = small_ref[j, slot]
    router_ref[...] = table[...].astype(bf16)
    gains_ref[...] = table[...].T[first : first + 8, :]


def place_weights(info, weight_all, small_all, first):
    blocks, rows, cols = weight_all.shape
    whole = lambda dims: pl.BlockSpec(dims, lambda i, info_ref: (0,) * len(dims))
    outs = [shape((blocks * rows, cols), bf16), shape((blocks * rows, LANES), bf16), shape((8, blocks * rows), f32)]
    return pl.pallas_call(
        functools.partial(weights_kernel, first),
        grid_spec=pltpu.PrefetchScalarGridSpec(
            num_scalar_prefetch=1,
            grid=(1,),
            in_specs=[whole(weight_all.shape), whole(small_all.shape)],
            out_specs=[whole(out.shape) for out in outs],
            scratch_shapes=[pltpu.VMEM((blocks * rows, LANES), f32)],
        ),
        out_shape=outs,
        compiler_params=params(),
        cost_estimate=cost(3),
        name="place_weights",
    )(info, weight_all, small_all)


def output_weight_kernel(info_ref, all_ref, weight_ref):
    blocks, slots, rows, cols = all_ref.shape
    for j in range(blocks):
        place = info_ref[0] ^ reversed_bits(j, blocks)
        here = pl.ds(pl.multiple_of(place * rows, rows), rows)
        for slot in range(slots):
            weight_ref[here, slot * cols : (slot + 1) * cols] = all_ref[j, slot]


def place_output_weight(info, weight_all):
    blocks, slots, rows, cols = weight_all.shape
    out = shape((blocks * rows, slots * cols), bf16)
    return pl.pallas_call(
        output_weight_kernel,
        grid_spec=pltpu.PrefetchScalarGridSpec(
            num_scalar_prefetch=1,
            grid=(1,),
            in_specs=[pl.BlockSpec(weight_all.shape, lambda i, info_ref: (0, 0, 0, 0))],
            out_specs=pl.BlockSpec(out.shape, lambda i, info_ref: (0, 0)),
        ),
        out_shape=out,
        compiler_params=params(),
        cost_estimate=cost(3),
        name="place_output_weight",
    )(info, weight_all)


def weight_grad_kernel(micro, blocks, info_ref, *refs):
    left_refs, right_refs = refs[:micro], refs[micro : 2 * micro]
    keep_ref, send_ref = refs[2 * micro : 2 * micro + 2]
    flipped = refs[2 * micro + 2 :]
    half, high, _ = keep_ref.shape
    for m in range(micro):
        flipped[m][...] = left_refs[m][...].T

    for j in range(blocks):
        place = info_ref[0] ^ reversed_bits(j, blocks)
        here = pl.ds(pl.multiple_of(place * high, high), high)
        total = dot_nn(flipped[0][here, :], right_refs[0][...])
        for m in range(1, micro):
            total = total + dot_nn(flipped[m][here, :], right_refs[m][...])
        if j < half:
            keep_ref[j] = total.astype(bf16)
        else:
            send_ref[j - half] = total.astype(bf16)


def weight_grad(info, lefts, rights, blocks):
    micro, half = len(lefts), blocks // 2
    rows, width = lefts[0].shape
    cols = rights[0].shape[1]
    whole = lambda dims: pl.BlockSpec(dims, lambda j, info_ref: (0,) * len(dims))
    out = (half, width // blocks, cols)
    return pl.pallas_call(
        functools.partial(weight_grad_kernel, micro, blocks),
        grid_spec=pltpu.PrefetchScalarGridSpec(
            num_scalar_prefetch=1,
            grid=(1,),
            in_specs=[whole(value.shape) for value in [*lefts, *rights]],
            out_specs=[whole(out)] * 2,
            scratch_shapes=[pltpu.VMEM((width, rows), bf16)] * micro,
        ),
        out_shape=[shape(out, bf16)] * 2,
        compiler_params=params(),
        cost_estimate=cost(4),
        name="weight_grad",
    )(info, *lefts, *rights)


def unpack_kernel(sum_ref, gate_ref, up_ref, down_ref):
    for member in range(PAIR):
        cut = lambda kind: sum_ref[:, (kind * PAIR + member) * LANES : (kind * PAIR + member + 1) * LANES].astype(f32)
        gate_ref[member] = cut(0)
        up_ref[member] = cut(1)
        down_ref[member] = cut(2).T


def unpack_experts(summed):
    rows, cols = summed.shape
    part = 3 * PAIR * LANES
    count = cols // part
    experts = count * PAIR
    return pl.pallas_call(
        unpack_kernel,
        grid=(count,),
        in_specs=[pl.BlockSpec((rows, part), lambda i: (0, i))],
        out_specs=[
            pl.BlockSpec((PAIR, rows, LANES), lambda i: (i, 0, 0)),
            pl.BlockSpec((PAIR, rows, LANES), lambda i: (i, 0, 0)),
            pl.BlockSpec((PAIR, LANES, rows), lambda i: (i, 0, 0)),
        ],
        out_shape=[
            shape((experts, rows, LANES), f32),
            shape((experts, rows, LANES), f32),
            shape((experts, LANES, rows), f32),
        ],
        compiler_params=params(),
        cost_estimate=cost(5),
        name="unpack",
    )(summed)


def exchange(values, axis, bit):
    count = lax.axis_size(axis)
    return lax.ppermute(values, axis, [(i, i ^ bit) for i in range(count)])


class Moves:
    def __init__(self):
        self.inputs, self.outputs, self.steps = [], [], []

    def take(self, value):
        self.inputs.append(value)
        return ("in", len(self.inputs) - 1)

    def make(self, dims, kind):
        self.outputs.append(shape(dims, kind))
        return ("out", len(self.outputs) - 1)

    def copy(self, source, target, place, needs, size):
        ready = max([self.steps[need][5] for need in needs], default=0.0)
        rate = 45e3 if place and place[1] != 1 or place and place[0] == "tp" else 150e3
        finish = ready + 1.0 + size / rate
        self.steps.append((source, target, place, needs, ready, finish))
        return len(self.steps) - 1

    def gather_tp(self, value, pieces=2):
        count = lax.axis_size("tp")
        rows, size = value.shape[0] // pieces, value.size * 2 // pieces
        arrays = [self.take(value)] + [self.make(value.shape, value.dtype) for _ in range(count - 1)]
        for piece in range(pieces):
            index = (pl.ds(piece * rows, rows),)
            came, bit = {0: []}, count // 2
            while bit:
                for slot in sorted(came):
                    step = self.copy(
                        (arrays[slot], index), (arrays[slot | bit], index), ("tp", bit), came[slot], size * (1 + bit // 2)
                    )
                    came[slot | bit] = [step]
                bit //= 2
        return arrays[1:]

    def trade_tp(self, blocks):
        made = []
        for slot in range(1, len(blocks)):
            made.append(self.make(blocks[slot].shape, blocks[slot].dtype))
            self.copy((self.take(blocks[slot]), ()), (made[-1], ()), ("tp", slot), [], blocks[slot].size * 4)
        return made

    def share_tp(self, value):
        held, made = self.take(value), []
        for slot in range(1, lax.axis_size("tp")):
            made.append(self.make(value.shape, value.dtype))
            self.copy((held, ()), (made[-1], ()), ("tp", slot), [], value.size * 4)
        return made

    def swap(self, value):
        held, target = self.take(value), self.make(value.shape, value.dtype)
        self.copy((held, ()), (target, ()), ("fsdp", 1), [], value.size * 2)
        return target

    def trade_fsdp(self, blocks):
        made = []
        for place in range(1, len(blocks)):
            made.append(self.make(blocks[place].shape, blocks[place].dtype))
            slot = 2 * reversed_bits(place, len(blocks))
            self.copy((self.take(blocks[place]), ()), (made[-1], ()), ("fsdp", slot), [], blocks[place].size * 4)
        return made

    def trade_stack(self, value, first, count):
        skip = int(first == 0)
        held, target = self.take(value), self.make((value.shape[0] - skip,) + value.shape[1:], value.dtype)
        for j in range(skip, value.shape[0]):
            slot = reversed_bits(first + j, count)
            self.copy((held, (j,)), (target, (j - skip,)), ("fsdp", slot), [], value[0].size * 4)
        return target

    def trade_rows(self, value, count):
        rows = value.shape[0] // count
        held, target = self.take(value), self.make((count - 1, rows) + value.shape[1:], value.dtype)
        for slot in range(1, count):
            source = lambda ranks, slot=slot: (pl.ds(pl.multiple_of((ranks["fsdp"] ^ slot) * rows, rows), rows),)
            self.copy((held, source), (target, (slot - 1,)), ("fsdp", slot), [], rows * 512)
        return target

    def spread(self, source, target, rows, size, pieces, needs):
        count = lax.axis_size("fsdp")
        bits = []
        while count >> (len(bits) + 1):
            bits.append(count >> (len(bits) + 1))
        upper = bits[:-1]
        turned = upper[len(upper) // 2 :] + upper[: len(upper) // 2]
        orders = [upper + [1], turned + [1]]
        for piece in range(pieces):
            inner = (pl.ds(piece * (rows // pieces), rows // pieces),) if pieces > 1 else ()
            came = {0: list(needs)}
            for bit in orders[piece % 2]:
                for slot in sorted(came):
                    origin = source(inner) if slot == 0 else (target, (reversed_bits(slot, count),) + inner)
                    goal = (target, (reversed_bits(slot | bit, count),) + inner)
                    came[slot | bit] = [self.copy(origin, goal, ("fsdp", bit), came[slot], size // pieces)]

    def gather_fsdp(self, value, pieces=2):
        count = lax.axis_size("fsdp")
        held, target = self.take(value), self.make((count,) + value.shape, value.dtype)
        self.spread(lambda inner: (held, inner), target, value.shape[0], value.size * 2, pieces, [])
        self.copy((held, ()), (target, (0,)), None, [], value.size)
        return target

    def gather_both(self, value):
        count, slots = lax.axis_size("fsdp"), lax.axis_size("tp")
        held, target = self.take(value), self.make((count, slots) + value.shape, value.dtype)
        needs = [self.copy((held, ()), (target, (0, 0)), None, [], value.size)]
        for slot in range(1, slots):
            needs.append(self.copy((held, ()), (target, (0, slot)), ("tp", slot), [], value.size * 2))
        self.spread(lambda inner: (target, (0,) + inner), target, slots, value.size * 2 * slots, 2, needs)
        return target

    def meet(self):
        ranks = {axis: lax.axis_index(axis) for axis in ("fsdp", "tp")}
        barrier = pltpu.get_barrier_semaphore()
        places = sorted({step[2] for step in self.steps if step[2]})
        for axis, bit in places:
            pl.semaphore_signal(
                barrier, inc=1, device_id={axis: ranks[axis] ^ bit}, device_id_type=pl.DeviceIdType.MESH
            )
        pl.semaphore_wait(barrier, len(places))

    def describe(self, number, ins, outs, send, recv):
        ranks = {axis: lax.axis_index(axis) for axis in ("fsdp", "tp")}

        def view(spot):
            (kind, which), index = spot
            ref = (ins if kind == "in" else outs)[which]
            index = index(ranks) if callable(index) else index
            return ref.at[index] if index else ref

        source, target, place = self.steps[number][:3]
        if place is None:
            return pltpu.make_async_copy(view(source), view(target), send.at[number])
        axis, bit = place
        return pltpu.make_async_remote_copy(
            src_ref=view(source),
            dst_ref=view(target),
            send_sem=send.at[number],
            recv_sem=recv.at[number],
            device_id={axis: ranks[axis] ^ bit},
            device_id_type=pl.DeviceIdType.MESH,
        )

    def begin(self, ins, outs, send, recv):
        self.meet()
        for number in range(len(self.steps)):
            self.describe(number, ins, outs, send, recv).start()

    def finish(self, ins, outs, send, recv):
        for number in range(len(self.steps)):
            self.describe(number, ins, outs, send, recv).wait()

    def kernel(self, *refs):
        ins, outs = refs[: len(self.inputs)], refs[len(self.inputs) : len(self.inputs) + len(self.outputs)]
        send, recv = refs[-2:]
        self.meet()
        started, arrived = {}, set()

        def arrive(number):
            if number not in arrived:
                arrived.add(number)
                if self.steps[number][2]:
                    started[number].wait_recv()
                else:
                    started[number].wait()

        for number in sorted(range(len(self.steps)), key=lambda i: self.steps[i][4]):
            for need in self.steps[number][3]:
                arrive(need)
            started[number] = self.describe(number, ins, outs, send, recv)
            started[number].start()
        for number in sorted(range(len(self.steps)), key=lambda i: self.steps[i][5]):
            arrive(number)
            if self.steps[number][2]:
                started[number].wait_send()

    def semaphores(self):
        return [pltpu.SemaphoreType.DMA((len(self.steps),)), pltpu.SemaphoreType.DMA((len(self.steps),))]

    def run(self, number, time, name):
        count = len(self.steps)
        anywhere = pl.BlockSpec(memory_space=pl.ANY)
        made = pl.pallas_call(
            self.kernel,
            out_shape=self.outputs,
            in_specs=[anywhere] * len(self.inputs),
            out_specs=[anywhere] * len(self.outputs),
            scratch_shapes=[pltpu.SemaphoreType.DMA((count,)), pltpu.SemaphoreType.DMA((count,))],
            compiler_params=pltpu.CompilerParams(collective_id=number, has_side_effects=True),
            cost_estimate=cost(time),
            name=name,
        )(*self.inputs)
        self.made = list(made)

    def get(self, spot):
        return [self.made[part[1]] for part in spot] if isinstance(spot, list) else self.made[spot[1]]


def trade_slots(blocks, axis):
    return [blocks[0]] + [exchange(blocks[slot], axis, slot) for slot in range(1, len(blocks))]


def after(value, *others):
    return lax.optimization_barrier((value, *others))[0]


def local(
    inputs,
    cotangent,
    lengths,
    routes,
    attn_gain,
    moe_gain,
    router_weight,
    query_weight,
    key_weight,
    value_weight,
    output_weight,
    gate_weight,
    up_weight,
    down_weight,
):
    tensor_count = lax.axis_size("tp")
    tensor_rank = lax.axis_index("tp")
    shard_rank = lax.axis_index("fsdp")
    micro, rows, width = inputs.shape
    span = rows * tensor_count
    experts, shard_width, hidden = gate_weight.shape
    steps = range(micro)
    slots, blocks = tensor_count, lax.axis_size("fsdp")
    slot_ranks = [tensor_rank ^ slot for slot in range(slots)]
    odd, upper = tensor_rank % 2 == 1, tensor_rank // 2 % 2 == 1
    info_all = jnp.concatenate([jnp.stack([shard_rank, tensor_rank]).astype(jnp.int32), lengths])
    infos = [jnp.stack([info_all[0], info_all[1], info_all[2 + m]]) for m in steps]

    small = jnp.concatenate([router_weight, attn_gain[:, None], moe_gain[:, None]], axis=1).astype(f32)
    small = jnp.pad(small, ((0, 0), (0, LANES - small.shape[1])))
    qkv_local = jnp.concatenate([query_weight, key_weight, value_weight], axis=1)
    qkv_cols = qkv_local.shape[1]

    stacked = jnp.stack(
        [gate_weight.transpose(1, 0, 2), up_weight.transpose(1, 0, 2), down_weight.transpose(2, 0, 1)], axis=1
    )
    expert_local = (
        stacked.reshape(shard_width, 3, experts // PAIR, PAIR, hidden)
        .transpose(0, 2, 1, 3, 4)
        .reshape(shard_width, 3 * experts * hidden)
    )

    row_place = jnp.arange(rows, dtype=jnp.int32)
    span_pos = jnp.concatenate([shard_rank * span + rank * rows + row_place for rank in slot_ranks])
    cos_row, sin_row = rope_tables(span_pos)
    row_pos = shard_rank * span + tensor_rank * rows + row_place
    valid = row_pos[None, :] < lengths[:, None]
    own_grads = jnp.where(valid[:, :, None], cotangent, jnp.zeros_like(cotangent))

    x_slots, queries, kvs, kv_alls, gm_slots = [], [], [], [], []
    for m in range(micro + 1):
        moves = Moves()
        wanted = {}
        if m < micro:
            wanted["x"] = moves.gather_tp(after(inputs[m], kvs[-1]) if m else inputs[m])
        if m:
            wanted["kv"] = moves.gather_fsdp(kvs[m - 1])
        if m == 0:
            wanted["weights"] = moves.gather_fsdp(qkv_local)
            wanted["small"] = moves.gather_both(small)
            wanted["out"] = moves.gather_both(output_weight.T)
        if m == micro:
            wanted["gm"] = moves.gather_tp(own_grads[0])
        moves.run(m, 25, "open")
        if m == 0:
            qkv_full, router_full, gains = place_weights(
                info_all, moves.get(wanted["weights"]), moves.get(wanted["small"]), experts
            )
            gain_attn, gain_moe = gains[0:1], gains[1:2]
            out_all = moves.get(wanted["out"])
        if m:
            kv_alls.append(moves.get(wanted["kv"]))
        if m < micro:
            x_slots.append([inputs[m]] + moves.get(wanted["x"]))
            query, kv = project_qkv(x_slots[m], gain_attn, qkv_full, cos_row, sin_row)
            queries.append(query)
            kvs.append(kv)
        else:
            gm_slots.append([own_grads[0]] + moves.get(wanted["gm"]))
    for m in range(1, micro):
        gm_slots.append(trade_slots([after(own_grads[m], gm_slots[m - 1][-1])] * slots, "tp"))

    expert_full = lax.all_gather(after(expert_local, kv_alls[-1]), "fsdp", axis=0, tiled=True)
    order = kv_alls[-1]
    attended, logs, att_owns, middles, normeds = [], [], [], [], []
    moves, spots = Moves(), []
    for m in steps:
        *att_slots, log_total = attend(after(infos[m], order), queries[m], kv_alls[m], rows)
        order = log_total
        attended.append(att_slots)
        logs.append(log_total)
        spots.append(moves.trade_tp(att_slots))
    out_full = place_output_weight(after(info_all, logs[0]), out_all)
    moves.run(micro + 1, 12, "trade")
    for m in steps:
        att_own, middle, normed = close_attention(
            inputs[m], gain_moe, out_full, [attended[m][0]] + moves.get(spots[m])
        )
        order = middle
        att_owns.append(att_own)
        middles.append(middle)
        normeds.append(normed)
    moves = Moves()
    spot = moves.gather_tp(normeds[0])
    moves.run(micro + 2, 18, "gather_normed")
    moe_slots = [[normeds[0]] + moves.get(spot)]

    expert_outs, gin_parts = [], []
    for m in steps:
        ride = Moves()
        ahead = ride.share_tp(normeds[m + 1]) if m + 1 < micro else None
        behind = ride.trade_tp(expert_outs[m - 1][:slots]) if m else None
        results = experts_both(
            after(infos[m], order),
            routes[m],
            router_full,
            expert_full,
            moe_slots[m],
            gm_slots[m],
            ride,
            2 * micro + 4 + m,
        )
        expert_outs.append(results)
        if ahead:
            moe_slots.append([normeds[m + 1]] + ride.get(ahead))
        if behind:
            gin_parts.append([expert_outs[m - 1][0]] + ride.get(behind))
        order = results[2 * slots]
    lows_g = [results[2 * slots + 1] for results in expert_outs]
    lows_h = [results[2 * slots + 2] for results in expert_outs]
    ride = Moves()
    behind = ride.trade_tp(expert_outs[-1][:slots])
    expert_grad = expert_grads(moe_slots, gm_slots, lows_g, lows_h, ride, 3 * micro + 4)
    gin_parts.append([expert_outs[-1][0]] + ride.get(behind))
    expert_sum = lax.psum_scatter(expert_grad, "fsdp", scatter_dimension=0, tiled=True)

    sums = 0.0
    order = expert_grad
    grad_middles, grad_attns, grad_slots = [], [], []
    moves = Moves()
    for m in steps:
        grad_middle, grad_attn, sums_moe, *grads = moe_back(
            after(infos[m], order),
            gin_parts[m],
            expert_outs[m][2 * slots],
            router_full,
            middles[m],
            normeds[m],
            gain_moe,
            cotangent[m],
            out_full,
            slots,
        )
        order = sums_moe
        sums = sums + sums_moe
        grad_middles.append(grad_middle)
        grad_attns.append(grad_attn)
        grad_slots.append((grads[0], moves.trade_tp(grads)))
    out_keep, out_send = weight_grad(after(info_all, order), grad_attns, att_owns, blocks)
    out_spot = moves.swap(out_send)
    moves.run(3 * micro + 5, 12, "trade_back")
    grad_slots = [[own] + moves.get(spots) for own, spots in grad_slots]
    order = out_keep
    out_stack = (out_keep.astype(f32) + moves.get(out_spot).astype(f32)).astype(bf16)

    dqs, dkvs, mixed_parts = [], [], []
    for m in steps:
        dq, keep, send = attend_back(
            after(infos[m], order), queries[m], kv_alls[m], logs[m], cos_row, sin_row, attended[m], grad_slots[m]
        )
        mixed = expert_outs[m][slots : 2 * slots]
        mixed_parts.append(trade_slots([mixed[0]] + [after(part, order) for part in mixed[1:]], "tp"))
        order = dq
        dqs.append(dq)
        met = exchange(send, "fsdp", 1)
        half = blocks // 2
        dkv = [(keep[j].astype(f32) + met[j].astype(f32)).astype(bf16) for j in range(half)]
        if m + 1 < micro:
            dkv = [dkv[0]] + [exchange(dkv[j], "fsdp", 2 * reversed_bits(j, half)) for j in range(1, half)]
        dkvs.append(dkv)

    normed_all, qkv_grads, normed_parts = [], [], []
    for m in steps:
        if m + 1 == micro:
            moves = Moves()
            came = moves.trade_fsdp(dkvs[m])
            met = [moves.trade_tp(parts) for parts in normed_parts]
            moves.run(2 * micro + 1, 24, "close_keys")
            dkvs[m] = [dkvs[m][0]] + moves.get(came)
            normed_parts = [[parts[0]] + moves.get(spots) for parts, spots in zip(normed_parts, met)]
        *parts, grads, normed_attn, sums_attn = qkv_back(
            dqs[m], dkvs[m], cos_row, sin_row, after(gain_attn, order), qkv_full, x_slots[m]
        )
        order = sums_attn
        sums = sums + jnp.pad(sums_attn[0:1], ((1, 22), (0, 0)))
        normed_all.append(normed_attn)
        qkv_grads.append(grads)
        normed_parts.append(parts)
    qkv_keep, qkv_send = weight_grad(after(info_all, order), normed_all, qkv_grads, blocks)
    table = jnp.pad(sums, ((0, LANES - sums.shape[0]), (0, 0))).T

    moves = Moves()
    met = moves.trade_tp(normed_parts[-1])
    near, far = moves.trade_stack(qkv_keep, 0, blocks), moves.trade_stack(qkv_send, blocks // 2, blocks)
    out_spot = moves.trade_stack(out_stack, 0, blocks)
    table_spot = moves.trade_rows(table.astype(bf16), blocks)
    moves.run(2 * micro + 2, 24, "close_weights")
    normed_parts[-1] = [normed_parts[-1][0]] + moves.get(met)
    total = lambda first, *stacks: first.astype(f32) + sum(jnp.sum(stack.astype(f32), axis=0) for stack in stacks)
    out_sum = total(out_stack[0], moves.get(out_spot)).astype(bf16)
    own_rows = lax.dynamic_slice_in_dim(table, shard_rank * shard_width, shard_width, 0)
    table_sum = total(own_rows, moves.get(table_spot))
    qkv_sum = total(qkv_keep[0], moves.get(near), moves.get(far))
    head_cols, few = output_weight.shape[0], small.shape[0]
    out_parts = [out_sum[:, slot * head_cols : (slot + 1) * head_cols] for slot in range(slots)]
    table_parts = [lax.dynamic_slice_in_dim(table_sum, rank * few, few, 0) for rank in slot_ranks]
    moves = Moves()
    out_spots, table_spots = moves.trade_tp(out_parts), moves.trade_tp(table_parts)
    moves.run(2 * micro + 3, 6, "close_small")
    out_final = sum(part.astype(f32) for part in [out_parts[0]] + moves.get(out_spots))
    small_sum = sum([table_parts[0]] + moves.get(table_spots))

    outputs = close_outputs(after(info_all, normed_parts[-1][-1]), mixed_parts, middles, slots)
    gate_sum, up_sum, down_sum = unpack_experts(expert_sum)
    input_grad = close_input_grad(normed_parts, grad_middles, inputs, gain_attn)
    q_cols, k_cols = query_weight.shape[1], key_weight.shape[1]
    return (
        outputs,
        input_grad,
        small_sum[:, 1],
        small_sum[:, 0],
        small_sum[:, 8 : 8 + experts],
        qkv_sum[:, :q_cols],
        qkv_sum[:, q_cols : q_cols + k_cols],
        qkv_sum[:, q_cols + k_cols : qkv_cols],
        out_final.T,
        gate_sum,
        up_sum,
        down_sum,
    )


def solution(mesh):
    rows_spec = P(None, ("fsdp", "tp"), None)
    small_specs = (P(("fsdp", "tp")), P(("fsdp", "tp")), P(("fsdp", "tp"), None))
    weight_specs = (
        P("fsdp", "tp"),
        P("fsdp", "tp"),
        P("fsdp", "tp"),
        P("tp", "fsdp"),
        P(None, "fsdp", "tp"),
        P(None, "fsdp", "tp"),
        P(None, "tp", "fsdp"),
    )
    in_specs = (rows_spec, rows_spec, P(), P(None, "fsdp", None)) + small_specs + weight_specs
    out_specs = (rows_spec, rows_spec) + small_specs + weight_specs
    return jax.shard_map(local, mesh=mesh, in_specs=in_specs, out_specs=out_specs, check_vma=False)
```

```python
import functools

import jax
import jax.numpy as jnp
from jax import lax
from jax.experimental import pallas as pl
from jax.experimental.pallas import tpu as pltpu
from jax.sharding import PartitionSpec as P

HD = 64
LANES = 128
PAIR = 2
EPS = 1e-06
FILL = -1e30
THETA = 10000.0
VMEM_CAP = 60 * 1024 * 1024
f32 = jnp.float32
bf16 = jnp.bfloat16


def dot_nn(a, b):
    return lax.dot_general(a, b, (((1,), (0,)), ((), ())), preferred_element_type=f32)


def dot_nt(a, b):
    return lax.dot_general(a, b, (((1,), (1,)), ((), ())), preferred_element_type=f32)


def swap_halves(values):
    lane = lax.broadcasted_iota(jnp.int32, values.shape, values.ndim - 1)
    ahead = pltpu.roll(values, values.shape[-1] - HD // 2, values.ndim - 1)
    back = pltpu.roll(values, HD // 2, values.ndim - 1)
    return jnp.where(lane % HD < HD // 2, ahead, back)


def rope_tables(positions):
    half = HD // 2
    freqs = THETA ** (-jnp.arange(half, dtype=f32) * 2.0 / HD)
    angles = positions.astype(f32)[:, None] * freqs[None, :]
    cosine, sine = jnp.cos(angles), jnp.sin(angles)
    cos_row = jnp.concatenate([cosine] * 4, axis=1)
    sin_row = jnp.concatenate([-sine, sine] * 2, axis=1)
    return cos_row, sin_row


def head_rows(values, head):
    key_head, member = head // 2, head % 2
    pair = values[:, key_head * LANES : (key_head + 1) * LANES]
    if member != key_head:
        pair = pltpu.roll(pair, HD, 1)
    lane = lax.broadcasted_iota(jnp.int32, pair.shape, 1)
    return jnp.where(lane // HD == key_head, pair, jnp.zeros_like(pair))


def join_heads(first, second, key_head):
    if key_head == 0:
        second = pltpu.roll(second, HD, 1)
    else:
        first = pltpu.roll(first, HD, 1)
    lane = lax.broadcasted_iota(jnp.int32, first.shape, 1)
    return jnp.where(lane < HD, first, second)


def cost(microseconds):
    return pl.CostEstimate(flops=int(microseconds * 6e7), bytes_accessed=1024, transcendentals=0)


def params():
    return pltpu.CompilerParams(vmem_limit_bytes=VMEM_CAP)


def riding(number):
    return pltpu.CompilerParams(vmem_limit_bytes=VMEM_CAP, collective_id=number, has_side_effects=True)


def shape(dims, kind):
    return jax.ShapeDtypeStruct(dims, kind)


def normalised(x, gain):
    inverse = lax.rsqrt(jnp.mean(x * x, axis=-1, keepdims=True) + EPS)
    unit = x * inverse
    return inverse, unit, unit * gain


def qkv_kernel(*refs):
    x_refs = refs[:-6]
    gain_ref, w_ref, cos_ref, sin_ref, q_ref, kv_ref = refs[-6:]
    rows = x_refs[0].shape[0]
    for slot, x_ref in enumerate(x_refs):
        here = slice(slot * rows, (slot + 1) * rows)
        cos_row, sin_row = cos_ref[here, :], sin_ref[here, :]
        _, _, normed = normalised(x_ref[...].astype(f32), gain_ref[...])
        pre = dot_nn(normed.astype(bf16), w_ref[...])
        for part in range(3):
            cols = pre[:, part * LANES : (part + 1) * LANES]
            turned = cols * cos_row + swap_halves(cols) * sin_row
            if part < 2:
                q_ref[here, part * LANES : (part + 1) * LANES] = (turned * HD ** (-0.5)).astype(bf16)
            else:
                kv_ref[here, 0:LANES] = turned.astype(bf16)
        kv_ref[here, LANES : 2 * LANES] = pre[:, 3 * LANES : 4 * LANES].astype(bf16)


def project_qkv(x_slots, gain, weight, cos_row, sin_row):
    span = cos_row.shape[0]
    return pl.pallas_call(
        qkv_kernel,
        out_shape=[shape((span, 2 * LANES), bf16), shape((span, 2 * LANES), bf16)],
        compiler_params=params(),
        cost_estimate=cost(3),
        name="project_qkv",
    )(*x_slots, gain, weight, cos_row, sin_row)


def reversed_bits(index, count):
    result, bit = 0, 1
    while bit < count:
        result = result + ((index // bit) % 2) * (count // (2 * bit))
        bit *= 2
    return result


def places(rank, rows, dims, axis):
    index = lax.broadcasted_iota(jnp.int32, dims, axis)
    return (rank ^ (index // rows)) * rows + index % rows


def allowed_keys(rank, rows, span, key_start, query_start, length):
    key_pos = key_start + places(rank, rows, (span, span), 0)
    query_pos = query_start + places(rank, rows, (span, span), 1)
    return (key_pos <= query_pos) & (key_pos < length)


def block_kind(info_ref, j, span, count):
    mine, length = info_ref[0], info_ref[2]
    other = mine ^ reversed_bits(j, count)
    wanted = (other <= mine) & (mine * span < length) & (other * span < length)
    edge = (other == mine) | ((other + 1) * span > length)
    return other, wanted, edge


def attend_kernel(info_ref, q_ref, kv_ref, *refs):
    heads, best, total, accum = refs[-4:]
    out_refs, log_ref = refs[:-5], refs[-5]
    j = pl.program_id(0)
    count = pl.num_programs(0)
    mine, rank, length = info_ref[0], info_ref[1], info_ref[2]
    rows = out_refs[0].shape[0]
    span = q_ref.shape[0]
    other, wanted, edge = block_kind(info_ref, j, span, BLOCKS[0])

    @pl.when(j == 0)
    def _():
        values = q_ref[...].astype(f32)
        for head in range(4):
            heads[head] = head_rows(values, head).astype(bf16)
        best[...] = jnp.full(best.shape, FILL, f32)
        total[...] = jnp.zeros(total.shape, f32)
        accum[...] = jnp.zeros(accum.shape, f32)

    def block(masked):
        keys = kv_ref[0, :, :LANES]
        values_t = kv_ref[0, :, LANES:].astype(f32).T.astype(bf16)
        if masked:
            allowed = allowed_keys(rank, rows, span, other * span, mine * span, length)
        for head in range(4):
            scores = dot_nt(keys, heads[head])
            if masked:
                scores = jnp.where(allowed, scores, FILL)
            old = best[head : head + 1]
            new = jnp.maximum(old, jnp.max(scores, axis=0, keepdims=True))
            factor = jnp.exp(old - new)
            weights = jnp.exp(scores - new)
            if masked:
                weights = jnp.where(allowed, weights, 0.0)
            best[head : head + 1] = new
            total[head : head + 1] = total[head : head + 1] * factor + jnp.sum(weights, axis=0, keepdims=True)
            accum[head] = accum[head] * factor + dot_nn(values_t, weights.astype(bf16))

    @pl.when(wanted & edge)
    def _():
        block(True)

    @pl.when(wanted & jnp.logical_not(edge))
    def _():
        block(False)

    @pl.when(j == count - 1)
    def _():
        live = mine * span < length
        for key_head in range(2):
            pair = []
            for member in range(2):
                head = key_head * 2 + member
                sums = jnp.where(live, total[head : head + 1], 1.0)
                log_ref[head : head + 1] = best[head : head + 1] + jnp.log(sums)
                pair.append((accum[head] * (1.0 / sums)).T)
            joined = join_heads(pair[0], pair[1], key_head).astype(bf16)
            for slot, out_ref in enumerate(out_refs):
                out_ref[:, key_head * LANES : (key_head + 1) * LANES] = joined[slot * rows : (slot + 1) * rows]


BLOCKS = [0]


def attend(info, query, kv_all, rows):
    span, cols = query.shape
    blocks = kv_all.shape[0]
    slots = span // rows
    BLOCKS[0] = blocks
    return pl.pallas_call(
        attend_kernel,
        grid_spec=pltpu.PrefetchScalarGridSpec(
            num_scalar_prefetch=1,
            grid=(blocks,),
            in_specs=[
                pl.BlockSpec((span, cols), lambda j, info_ref: (0, 0)),
                pl.BlockSpec((1, span, 2 * LANES), lambda j, info_ref: (j, 0, 0)),
            ],
            out_specs=[pl.BlockSpec((rows, cols), lambda j, info_ref: (0, 0))] * slots
            + [pl.BlockSpec((8, span), lambda j, info_ref: (0, 0))],
            scratch_shapes=[
                pltpu.VMEM((4, span, LANES), bf16),
                pltpu.VMEM((8, span), f32),
                pltpu.VMEM((8, span), f32),
                pltpu.VMEM((4, LANES, span), f32),
            ],
        ),
        out_shape=[shape((rows, cols), bf16)] * slots + [shape((8, span), f32)],
        compiler_params=params(),
        cost_estimate=cost(12),
        name="attend",
    )(info, query, kv_all)


def attend_back_kernel(slots, info_ref, q_ref, kv_ref, log_ref, cos_ref, sin_ref, *refs):
    out_refs, grad_refs = refs[:slots], refs[slots : 2 * slots]
    dq_ref, keep_ref, send_ref, heads, grads, delta, accum, dkv = refs[2 * slots :]
    j = pl.program_id(0)
    count = pl.num_programs(0)
    mine, rank, length = info_ref[0], info_ref[1], info_ref[2]
    span, cols = q_ref.shape
    rows = span // slots
    other, wanted, edge = block_kind(info_ref, j, span, BLOCKS[0])

    @pl.when(j == 0)
    def _():
        values = q_ref[...].astype(f32)
        attended = jnp.concatenate([ref[...] for ref in out_refs], axis=0).astype(f32)
        grad = jnp.concatenate([ref[...] for ref in grad_refs], axis=0).astype(f32)
        product = grad * attended
        for head in range(4):
            heads[head] = head_rows(values, head).astype(bf16)
            grads[head] = head_rows(grad, head).astype(bf16)
            delta[head : head + 1] = jnp.sum(head_rows(product, head).T, axis=0, keepdims=True)
        accum[...] = jnp.zeros(accum.shape, f32)

    def block(masked):
        keys = kv_ref[0, :, :LANES]
        values = kv_ref[0, :, LANES:]
        keys_t = keys.astype(f32).T.astype(bf16)
        if masked:
            allowed = allowed_keys(rank, rows, span, other * span, mine * span, length)
        grad_keys = jnp.zeros((span, LANES), f32)
        grad_values = jnp.zeros((span, LANES), f32)
        for head in range(4):
            scores = dot_nt(keys, heads[head])
            probs = jnp.exp(scores - log_ref[head : head + 1])
            if masked:
                probs = jnp.where(allowed, probs, 0.0)
            grad_probs = dot_nt(values, grads[head])
            grad_scores = (probs * (grad_probs - delta[head : head + 1])).astype(bf16)
            grad_values = grad_values + dot_nn(probs.astype(bf16), grads[head])
            grad_keys = grad_keys + dot_nn(grad_scores, heads[head])
            accum[head] = accum[head] + dot_nn(keys_t, grad_scores)
        dkv[:, 0:LANES] = grad_keys.astype(bf16)
        dkv[:, LANES : 2 * LANES] = grad_values.astype(bf16)

    @pl.when(wanted & edge)
    def _():
        block(True)

    @pl.when(wanted & jnp.logical_not(edge))
    def _():
        block(False)

    @pl.when(jnp.logical_not(wanted))
    def _():
        dkv[...] = jnp.zeros(dkv.shape, bf16)

    @pl.when(j < count // 2)
    def _():
        keep_ref[0] = dkv[...]

    @pl.when(j >= count // 2)
    def _():
        send_ref[0] = dkv[...]

    @pl.when(j == count - 1)
    def _():
        for key_head in range(2):
            pair = [accum[key_head * 2 + member].T for member in range(2)]
            joined = join_heads(pair[0], pair[1], key_head) * HD ** (-0.5)
            turned = joined * cos_ref[...] - swap_halves(joined) * sin_ref[...]
            dq_ref[:, key_head * LANES : (key_head + 1) * LANES] = turned.astype(bf16)


def attend_back(info, query, kv_all, log_total, cos_row, sin_row, att_slots, grad_slots):
    span, cols = query.shape
    blocks, slots = kv_all.shape[0], len(att_slots)
    rows, half = span // slots, blocks // 2
    BLOCKS[0] = blocks
    fixed = lambda *dims: pl.BlockSpec(dims, lambda j, info_ref: (0,) * len(dims))
    return pl.pallas_call(
        functools.partial(attend_back_kernel, slots),
        grid_spec=pltpu.PrefetchScalarGridSpec(
            num_scalar_prefetch=1,
            grid=(blocks,),
            in_specs=[
                fixed(span, cols),
                pl.BlockSpec((1, span, 2 * LANES), lambda j, info_ref: (j, 0, 0)),
                fixed(8, span),
                fixed(span, LANES),
                fixed(span, LANES),
            ]
            + [fixed(rows, cols)] * (2 * slots),
            out_specs=[
                fixed(span, cols),
                pl.BlockSpec((1, span, 2 * LANES), lambda j, info_ref: (jnp.minimum(j, half - 1), 0, 0)),
                pl.BlockSpec((1, span, 2 * LANES), lambda j, info_ref: (jnp.maximum(j - half, 0), 0, 0)),
            ],
            scratch_shapes=[
                pltpu.VMEM((4, span, LANES), bf16),
                pltpu.VMEM((4, span, LANES), bf16),
                pltpu.VMEM((8, span), f32),
                pltpu.VMEM((4, LANES, span), f32),
                pltpu.VMEM((span, 2 * LANES), bf16),
            ],
        ),
        out_shape=[shape((span, cols), bf16)] + [shape((half, span, 2 * LANES), bf16)] * 2,
        compiler_params=params(),
        cost_estimate=cost(18),
        name="attend_back",
    )(info, query, kv_all, log_total, cos_row, sin_row, *att_slots, *grad_slots)


def middle_kernel(x_ref, gain_ref, w_ref, *refs):
    att_refs, (att_all, middle_ref, normed_ref) = refs[:-3], refs[-3:]
    cols = att_refs[0].shape[1]
    for slot, att_ref in enumerate(att_refs):
        att_all[:, slot * cols : (slot + 1) * cols] = att_ref[...]
    middle = x_ref[...].astype(f32) + dot_nt(att_all[...], w_ref[...])
    middle_ref[...] = middle
    normed_ref[...] = normalised(middle, gain_ref[...])[2].astype(bf16)


def close_attention(x, gain, weight, att_slots):
    rows, width = x.shape
    return pl.pallas_call(
        middle_kernel,
        out_shape=[shape((rows, weight.shape[1]), bf16), shape((rows, width), f32), shape((rows, width), bf16)],
        compiler_params=params(),
        cost_estimate=cost(2),
        name="middle",
    )(x, gain, weight, *att_slots)


def expert_kernel(slots, ride, info_ref, routes_ref, router_ref, w_ref, *refs):
    x_refs, gm_refs = refs[:slots], refs[slots : 2 * slots]
    ride_in, refs = refs[2 * slots : 2 * slots + len(ride.inputs)], refs[2 * slots + len(ride.inputs) :]
    gin_refs, mixed_refs, refs = refs[:slots], refs[slots : 2 * slots], refs[2 * slots :]
    gates_ref, low_g, low_h = refs[:3]
    ride_out, refs = refs[3 : 3 + len(ride.outputs)], refs[3 + len(ride.outputs) :]
    x_all, gm_all, gates, mixed, gin, gate_sums, send, recv = refs
    step = pl.program_id(0)
    last = pl.num_programs(0) - 1
    span, width = x_all.shape
    rows = span // slots
    wide = PAIR * LANES
    chunk = 256
    rank = lax.axis_index("tp")

    @pl.when(step == 0)
    def _():
        ride.begin(ride_in, ride_out, send, recv)
        lane = lax.broadcasted_iota(jnp.int32, (rows, LANES), 1)
        for slot in range(slots):
            here = slice(slot * rows, (slot + 1) * rows)
            x_all[here, :] = x_refs[slot][...]
            gm_all[here, :] = gm_refs[slot][...]
            named = routes_ref[pl.ds(pl.multiple_of((rank ^ slot) * rows, rows), rows), :]
            picked = lane == named[:, 0:1]
            for k in range(1, named.shape[1]):
                picked = picked | (lane == named[:, k : k + 1])
            logits = jnp.where(picked, dot_nn(x_refs[slot][...], router_ref[...]), FILL)
            peak = jnp.max(logits, axis=1, keepdims=True)
            exps = jnp.where(picked, jnp.exp(logits - peak), 0.0)
            gates[here, :] = exps / jnp.sum(exps, axis=1, keepdims=True)
        gates_ref[...] = gates[0:rows, :]
        mixed[...] = jnp.zeros(mixed.shape, f32)
        gin[...] = jnp.zeros(gin.shape, f32)
        gate_sums[...] = jnp.zeros(gate_sums.shape, f32)

    def rows_step(i, _):
        here = pl.ds(pl.multiple_of(i * chunk, chunk), chunk)
        pre = dot_nn(x_all[here, :], w_ref[:, : 2 * wide])
        gate_pre, up_pre = pre[:, :wide], pre[:, wide:]
        back = dot_nn(gm_all[here, :], w_ref[:, 2 * wide :])
        sig = 1.0 / (1.0 + jnp.exp(-gate_pre))
        silu = gate_pre * sig
        hidden = silu * up_pre
        lane = lax.broadcasted_iota(jnp.int32, (chunk, LANES), 1)
        product = hidden * back
        spread = []
        sums = gate_sums[here, :]
        for member in range(PAIR):
            hit = lane == step * PAIR + member
            gate = jnp.sum(jnp.where(hit, gates[here, :], 0.0), axis=1, keepdims=True)
            spread.append(jnp.broadcast_to(gate, (chunk, LANES)))
            amount = jnp.sum(product[:, member * LANES : (member + 1) * LANES], axis=1, keepdims=True)
            sums = sums + jnp.where(hit, amount, 0.0)
        gate_sums[here, :] = sums
        factor = jnp.concatenate(spread, axis=1)
        grad_hidden = factor * back
        low_hidden = (factor * hidden).astype(bf16)
        grad_up = (grad_hidden * silu).astype(bf16)
        grad_gate = (grad_hidden * up_pre * (sig * (1.0 + gate_pre * (1.0 - sig)))).astype(bf16)
        low_h[here, :] = low_hidden
        low_g[here, 0:wide] = grad_gate
        low_g[here, wide : 2 * wide] = grad_up
        mixed[here, :] += dot_nt(low_hidden, w_ref[:, 2 * wide :])
        gin[here, :] += dot_nt(low_g[here, :], w_ref[:, : 2 * wide])
        return 0

    lax.fori_loop(0, span // chunk, rows_step, 0)

    @pl.when(step == last)
    def _():
        for slot in range(slots):
            here = slice(slot * rows, (slot + 1) * rows)
            mixed_refs[slot][...] = mixed[here, :].astype(bf16)
            gin_refs[slot][:, 0:width] = gin[here, :].astype(bf16)
            gin_refs[slot][:, width : width + LANES] = gate_sums[here, :].astype(bf16)
        ride.finish(ride_in, ride_out, send, recv)


def experts_both(info, routes, router, weight, x_slots, gm_slots, ride, number):
    rows, width = x_slots[0].shape
    slots = len(x_slots)
    span = rows * slots
    wide = PAIR * LANES
    steps = weight.shape[1] // (3 * wide)
    fixed = lambda *dims: pl.BlockSpec(dims, lambda i, info_ref: (0,) * len(dims))
    moving = lambda height, cols: pl.BlockSpec((height, cols), lambda i, info_ref: (0, i))
    anywhere = pl.BlockSpec(memory_space=pl.ANY)
    results = pl.pallas_call(
        functools.partial(expert_kernel, slots, ride),
        grid_spec=pltpu.PrefetchScalarGridSpec(
            num_scalar_prefetch=1,
            grid=(steps,),
            in_specs=[fixed(*routes.shape), fixed(*router.shape), moving(width, 3 * wide)]
            + [fixed(rows, width)] * (2 * slots)
            + [anywhere] * len(ride.inputs),
            out_specs=[fixed(rows, width + LANES)] * slots
            + [fixed(rows, width)] * slots
            + [fixed(rows, LANES), moving(span, 2 * wide), moving(span, wide)]
            + [anywhere] * len(ride.outputs),
            scratch_shapes=[
                pltpu.VMEM((span, width), bf16),
                pltpu.VMEM((span, width), bf16),
                pltpu.VMEM((span, LANES), f32),
                pltpu.VMEM((span, width), f32),
                pltpu.VMEM((span, width), f32),
                pltpu.VMEM((span, LANES), f32),
            ]
            + ride.semaphores(),
        ),
        out_shape=[shape((rows, width + LANES), bf16)] * slots
        + [shape((rows, width), bf16)] * slots
        + [shape((rows, LANES), f32), shape((span, steps * 2 * wide), bf16), shape((span, steps * wide), bf16)]
        + ride.outputs,
        compiler_params=riding(number),
        cost_estimate=cost(24),
        name="experts",
    )(info, routes, router, weight, *x_slots, *gm_slots, *ride.inputs)
    ride.made = list(results[2 * slots + 3 :])
    return results[: 2 * slots + 3]


def expert_grad_kernel(micro, slots, ride, *refs):
    count = micro * slots
    send, recv = refs[-2:]
    given = 2 * count + 2 * micro
    ride_in = refs[given : given + len(ride.inputs)]
    ride_out = refs[given + len(ride.inputs) + 1 : given + len(ride.inputs) + 1 + len(ride.outputs)]
    x_refs, gm_refs = refs[:count], refs[count : 2 * count]
    g_refs, h_refs = refs[2 * count : 2 * count + micro], refs[2 * count + micro : 2 * count + 2 * micro]
    dw_ref, (x_t, gm_t) = refs[given + len(ride.inputs)], refs[-4:-2]
    rows = x_refs[0].shape[0]
    width = x_t.shape[0]
    wide = PAIR * LANES
    chunk = 256

    @pl.when(pl.program_id(0) == 0)
    def _():
        ride.begin(ride_in, ride_out, send, recv)
        for i in range(count):
            x_t[:, i * rows : (i + 1) * rows] = x_refs[i][...].T
            gm_t[:, i * rows : (i + 1) * rows] = gm_refs[i][...].T

    def weight_step(i, _):
        here = pl.ds(pl.multiple_of(i * chunk, chunk), chunk)
        g_sum, h_sum = 0.0, 0.0
        for m in range(micro):
            part = slice(m * slots * rows, (m + 1) * slots * rows)
            g_sum = g_sum + dot_nn(x_t[here, part], g_refs[m][...])
            h_sum = h_sum + dot_nn(gm_t[here, part], h_refs[m][...])
        dw_ref[here, 0 : 2 * wide] = g_sum.astype(bf16)
        dw_ref[here, 2 * wide : 3 * wide] = h_sum.astype(bf16)
        return 0

    lax.fori_loop(0, width // chunk, weight_step, 0)

    @pl.when(pl.program_id(0) == pl.num_programs(0) - 1)
    def _():
        ride.finish(ride_in, ride_out, send, recv)


def expert_grads(x_slots, gm_slots, lows_g, lows_h, ride, number):
    micro, slots = len(x_slots), len(x_slots[0])
    rows, width = x_slots[0][0].shape
    span = rows * slots
    wide = PAIR * LANES
    steps = lows_h[0].shape[1] // wide
    fixed = pl.BlockSpec((rows, width), lambda i: (0, 0))
    moving = lambda height, cols: pl.BlockSpec((height, cols), lambda i: (0, i))
    flat = [block for part in x_slots for block in part] + [block for part in gm_slots for block in part]
    anywhere = pl.BlockSpec(memory_space=pl.ANY)
    summed, *ride.made = pl.pallas_call(
        functools.partial(expert_grad_kernel, micro, slots, ride),
        grid=(steps,),
        in_specs=[fixed] * len(flat) + [moving(span, 2 * wide)] * micro + [moving(span, wide)] * micro
        + [anywhere] * len(ride.inputs),
        out_specs=[pl.BlockSpec((width, 3 * wide), lambda i: (0, i))] + [anywhere] * len(ride.outputs),
        out_shape=[shape((width, steps * 3 * wide), bf16)] + ride.outputs,
        scratch_shapes=[pltpu.VMEM((width, micro * span), bf16), pltpu.VMEM((width, micro * span), bf16)]
        + ride.semaphores(),
        compiler_params=riding(number),
        cost_estimate=cost(12),
        name="expert_grads",
    )(*flat, *lows_g, *lows_h, *ride.inputs)
    return summed


def moe_back_kernel(
    slots, info_ref, *refs
):
    parts, refs = refs[:slots], refs[slots:]
    gates_ref, router_ref, middle_ref, normed_ref, gain_ref, cot_ref, w_ref = refs[:7]
    refs = refs[7:]
    grad_middle_ref, grad_attn_ref, sums_ref = refs[:3]
    out_refs = refs[3:]
    rows, width = middle_ref.shape
    gate = lambda ref: ref[:, width : width + LANES].astype(f32)
    gates = gates_ref[...]
    gate_grads = sum(gate(part) for part in parts)
    grad_logits = gates * (gate_grads - jnp.sum(gates * gate_grads, axis=1, keepdims=True))
    grad_logits = grad_logits.astype(bf16)
    main = lambda ref: ref[:, 0:width].astype(f32)
    grad_moe = sum(main(part) for part in parts) + dot_nt(grad_logits, router_ref[...])
    middle, gain = middle_ref[...], gain_ref[...]
    inverse, unit, _ = normalised(middle, gain)
    weighted = grad_moe * gain
    inner = jnp.mean(weighted * middle, axis=-1, keepdims=True)
    grad_norm = inverse * weighted - middle * (inverse * inverse * inverse) * inner
    start = info_ref[0] * rows * slots + info_ref[1] * rows
    row_pos = start + lax.broadcasted_iota(jnp.int32, (rows, width), 0)
    grad_out = jnp.where(row_pos < info_ref[2], cot_ref[...].astype(f32), 0.0)
    grad_middle = grad_out + grad_norm
    grad_middle_ref[...] = grad_middle
    low = grad_middle.astype(bf16)
    grad_attn_ref[...] = low
    router_part = dot_nn(grad_logits.astype(f32).T.astype(bf16), normed_ref[...])
    gain_part = jnp.sum(grad_moe * unit, axis=0, keepdims=True)
    first = lax.broadcasted_iota(jnp.int32, (8, width), 0) == 0
    sums_ref[0:8, :] = jnp.where(first, jnp.broadcast_to(gain_part, (8, width)), 0.0)
    sums_ref[8:24, :] = router_part[0:16, :]
    grads = dot_nn(low, w_ref[...]).astype(bf16)
    cols = grads.shape[1] // slots
    for slot in range(slots):
        out_refs[slot][...] = grads[:, slot * cols : (slot + 1) * cols]


def moe_back(info, parts, gates, router, middle, normed, gain, cot, weight, slots):
    rows, width = middle.shape
    fixed = lambda value: pl.BlockSpec(value.shape, lambda i, info_ref: (0, 0))
    outs = [shape((rows, width), f32), shape((rows, width), bf16), shape((24, width), f32)]
    outs = outs + [shape((rows, weight.shape[1] // slots), bf16)] * slots
    operands = [*parts, gates, router, middle, normed, gain, cot, weight]
    return pl.pallas_call(
        functools.partial(moe_back_kernel, slots),
        grid_spec=pltpu.PrefetchScalarGridSpec(
            num_scalar_prefetch=1, grid=(1,), in_specs=[fixed(v) for v in operands], out_specs=[fixed(v) for v in outs]
        ),
        out_shape=outs,
        compiler_params=params(),
        cost_estimate=cost(3),
        name="moe_back",
    )(info, *operands)


def qkv_back_kernel(slots, blocks, dq_ref, cos_ref, sin_ref, gain_ref, w_ref, *refs):
    dkv_refs, refs = refs[:blocks], refs[blocks:]
    dkv = sum(ref[...].astype(f32) for ref in dkv_refs)
    x_refs, part_refs = refs[:slots], refs[slots : 2 * slots]
    grads_ref, normed_ref, sums_ref = refs[2 * slots :]
    rows = x_refs[0].shape[0]
    width = w_ref.shape[0]
    cols = dq_ref.shape[1]
    dk = dkv[:, 0:LANES]
    turned = dk * cos_ref[...] - swap_halves(dk) * sin_ref[...]
    grads_ref[:, 0:cols] = dq_ref[...]
    grads_ref[:, cols : cols + LANES] = turned.astype(bf16)
    grads_ref[:, cols + LANES : cols + 2 * LANES] = dkv[:, LANES : 2 * LANES].astype(bf16)
    total = jnp.zeros((1, width), f32)
    for slot in range(slots):
        here = slice(slot * rows, (slot + 1) * rows)
        _, unit, normed = normalised(x_refs[slot][...].astype(f32), gain_ref[...])
        normed_ref[here, :] = normed.astype(bf16)
        part = dot_nt(grads_ref[here, :], w_ref[...])
        part_refs[slot][...] = part.astype(bf16)
        total = total + jnp.sum(part * unit, axis=0, keepdims=True)
    first = lax.broadcasted_iota(jnp.int32, (8, width), 0) == 0
    sums_ref[...] = jnp.where(first, jnp.broadcast_to(total, (8, width)), 0.0)


def qkv_back(dq, dkv_parts, cos_row, sin_row, gain, weight, x_slots):
    slots = len(x_slots)
    rows, width = x_slots[0].shape
    span = rows * slots
    return pl.pallas_call(
        functools.partial(qkv_back_kernel, slots, len(dkv_parts)),
        out_shape=[shape((rows, width), bf16)] * slots
        + [shape((span, weight.shape[1]), bf16), shape((span, width), bf16), shape((8, width), f32)],
        compiler_params=params(),
        cost_estimate=cost(4),
        name="qkv_back",
    )(dq, cos_row, sin_row, gain, weight, *dkv_parts, *x_slots)


def input_grad_kernel(micro, slots, *refs):
    part_refs, middle_refs = refs[: slots * micro], refs[slots * micro : (slots + 1) * micro]
    x_ref, gain_ref, out_ref = refs[(slots + 1) * micro :]
    for m in range(micro):
        grad_normed = sum(ref[...].astype(f32) for ref in part_refs[slots * m : slots * (m + 1)])
        x = x_ref[m].astype(f32)
        inverse, _, _ = normalised(x, gain_ref[...])
        weighted = grad_normed * gain_ref[...]
        inner = jnp.mean(weighted * x, axis=-1, keepdims=True)
        out_ref[m] = middle_refs[m][...] + inverse * weighted - x * (inverse * inverse * inverse) * inner


def close_input_grad(parts, grad_middles, x, gain):
    micro = x.shape[0]
    return pl.pallas_call(
        functools.partial(input_grad_kernel, micro, len(parts[0])),
        out_shape=shape(x.shape, f32),
        compiler_params=params(),
        cost_estimate=cost(2),
        name="input_grad",
    )(*[part for group in parts for part in group], *grad_middles, x, gain)


def outputs_kernel(micro, slots, info_ref, *refs):
    part_refs, middle_refs, out_ref = refs[: slots * micro], refs[slots * micro : -1], refs[-1]
    rows, width = middle_refs[0].shape
    start = info_ref[0] * rows * slots + info_ref[1] * rows
    row_pos = start + lax.broadcasted_iota(jnp.int32, (rows, width), 0)
    for m in range(micro):
        mixed = sum(ref[...].astype(f32) for ref in part_refs[slots * m : slots * (m + 1)])
        total = middle_refs[m][...] + mixed
        out_ref[m] = jnp.where(row_pos < info_ref[2 + m], total, 0.0).astype(bf16)


def close_outputs(info, parts, middles, slots):
    micro = len(middles)
    rows, width = middles[0].shape
    operands = [part for group in parts for part in group] + middles
    fixed = pl.BlockSpec((rows, width), lambda i, info_ref: (0, 0))
    return pl.pallas_call(
        functools.partial(outputs_kernel, micro, slots),
        grid_spec=pltpu.PrefetchScalarGridSpec(
            num_scalar_prefetch=1,
            grid=(1,),
            in_specs=[fixed] * len(operands),
            out_specs=pl.BlockSpec((micro, rows, width), lambda i, info_ref: (0, 0, 0)),
        ),
        out_shape=shape((micro, rows, width), bf16),
        compiler_params=params(),
        cost_estimate=cost(2),
        name="outputs",
    )(info, *operands)


def weights_kernel(first, info_ref, all_ref, small_ref, weight_ref, router_ref, gains_ref, table):
    blocks, rows, _ = all_ref.shape
    slots, few = small_ref.shape[1:3]
    for j in range(blocks):
        place = info_ref[0] ^ reversed_bits(j, blocks)
        weight_ref[pl.ds(pl.multiple_of(place * rows, rows), rows), :] = all_ref[j]
        for slot in range(slots):
            start = place * rows + (info_ref[1] ^ slot) * few
            table[pl.ds(pl.multiple_of(start, few), few), :] = small_ref[j, slot]
    router_ref[...] = table[...].astype(bf16)
    gains_ref[...] = table[...].T[first : first + 8, :]


def place_weights(info, weight_all, small_all, first):
    blocks, rows, cols = weight_all.shape
    whole = lambda dims: pl.BlockSpec(dims, lambda i, info_ref: (0,) * len(dims))
    outs = [shape((blocks * rows, cols), bf16), shape((blocks * rows, LANES), bf16), shape((8, blocks * rows), f32)]
    return pl.pallas_call(
        functools.partial(weights_kernel, first),
        grid_spec=pltpu.PrefetchScalarGridSpec(
            num_scalar_prefetch=1,
            grid=(1,),
            in_specs=[whole(weight_all.shape), whole(small_all.shape)],
            out_specs=[whole(out.shape) for out in outs],
            scratch_shapes=[pltpu.VMEM((blocks * rows, LANES), f32)],
        ),
        out_shape=outs,
        compiler_params=params(),
        cost_estimate=cost(3),
        name="place_weights",
    )(info, weight_all, small_all)


def output_weight_kernel(info_ref, all_ref, weight_ref):
    blocks, slots, rows, cols = all_ref.shape
    for j in range(blocks):
        place = info_ref[0] ^ reversed_bits(j, blocks)
        here = pl.ds(pl.multiple_of(place * rows, rows), rows)
        for slot in range(slots):
            weight_ref[here, slot * cols : (slot + 1) * cols] = all_ref[j, slot]


def place_output_weight(info, weight_all):
    blocks, slots, rows, cols = weight_all.shape
    out = shape((blocks * rows, slots * cols), bf16)
    return pl.pallas_call(
        output_weight_kernel,
        grid_spec=pltpu.PrefetchScalarGridSpec(
            num_scalar_prefetch=1,
            grid=(1,),
            in_specs=[pl.BlockSpec(weight_all.shape, lambda i, info_ref: (0, 0, 0, 0))],
            out_specs=pl.BlockSpec(out.shape, lambda i, info_ref: (0, 0)),
        ),
        out_shape=out,
        compiler_params=params(),
        cost_estimate=cost(3),
        name="place_output_weight",
    )(info, weight_all)


def weight_grad_kernel(micro, blocks, info_ref, *refs):
    left_refs, right_refs = refs[:micro], refs[micro : 2 * micro]
    keep_ref, send_ref = refs[2 * micro : 2 * micro + 2]
    flipped = refs[2 * micro + 2 :]
    half, high, _ = keep_ref.shape
    for m in range(micro):
        flipped[m][...] = left_refs[m][...].T

    for j in range(blocks):
        place = info_ref[0] ^ reversed_bits(j, blocks)
        here = pl.ds(pl.multiple_of(place * high, high), high)
        total = dot_nn(flipped[0][here, :], right_refs[0][...])
        for m in range(1, micro):
            total = total + dot_nn(flipped[m][here, :], right_refs[m][...])
        if j < half:
            keep_ref[j] = total.astype(bf16)
        else:
            send_ref[j - half] = total.astype(bf16)


def weight_grad(info, lefts, rights, blocks):
    micro, half = len(lefts), blocks // 2
    rows, width = lefts[0].shape
    cols = rights[0].shape[1]
    whole = lambda dims: pl.BlockSpec(dims, lambda j, info_ref: (0,) * len(dims))
    out = (half, width // blocks, cols)
    return pl.pallas_call(
        functools.partial(weight_grad_kernel, micro, blocks),
        grid_spec=pltpu.PrefetchScalarGridSpec(
            num_scalar_prefetch=1,
            grid=(1,),
            in_specs=[whole(value.shape) for value in [*lefts, *rights]],
            out_specs=[whole(out)] * 2,
            scratch_shapes=[pltpu.VMEM((width, rows), bf16)] * micro,
        ),
        out_shape=[shape(out, bf16)] * 2,
        compiler_params=params(),
        cost_estimate=cost(4),
        name="weight_grad",
    )(info, *lefts, *rights)


def unpack_kernel(sum_ref, gate_ref, up_ref, down_ref):
    for member in range(PAIR):
        cut = lambda kind: sum_ref[:, (kind * PAIR + member) * LANES : (kind * PAIR + member + 1) * LANES].astype(f32)
        gate_ref[member] = cut(0)
        up_ref[member] = cut(1)
        down_ref[member] = cut(2).T


def unpack_experts(summed):
    rows, cols = summed.shape
    part = 3 * PAIR * LANES
    count = cols // part
    experts = count * PAIR
    return pl.pallas_call(
        unpack_kernel,
        grid=(count,),
        in_specs=[pl.BlockSpec((rows, part), lambda i: (0, i))],
        out_specs=[
            pl.BlockSpec((PAIR, rows, LANES), lambda i: (i, 0, 0)),
            pl.BlockSpec((PAIR, rows, LANES), lambda i: (i, 0, 0)),
            pl.BlockSpec((PAIR, LANES, rows), lambda i: (i, 0, 0)),
        ],
        out_shape=[
            shape((experts, rows, LANES), f32),
            shape((experts, rows, LANES), f32),
            shape((experts, LANES, rows), f32),
        ],
        compiler_params=params(),
        cost_estimate=cost(5),
        name="unpack",
    )(summed)


def exchange(values, axis, bit):
    count = lax.axis_size(axis)
    return lax.ppermute(values, axis, [(i, i ^ bit) for i in range(count)])


class Moves:
    def __init__(self):
        self.inputs, self.outputs, self.steps = [], [], []

    def take(self, value):
        self.inputs.append(value)
        return ("in", len(self.inputs) - 1)

    def make(self, dims, kind):
        self.outputs.append(shape(dims, kind))
        return ("out", len(self.outputs) - 1)

    def copy(self, source, target, place, needs, size):
        ready = max([self.steps[need][5] for need in needs], default=0.0)
        rate = 45e3 if place and place[1] != 1 or place and place[0] == "tp" else 150e3
        finish = ready + 1.0 + size / rate
        self.steps.append((source, target, place, needs, ready, finish))
        return len(self.steps) - 1

    def gather_tp(self, value, pieces=2):
        count = lax.axis_size("tp")
        rows, size = value.shape[0] // pieces, value.size * 2 // pieces
        arrays = [self.take(value)] + [self.make(value.shape, value.dtype) for _ in range(count - 1)]
        for piece in range(pieces):
            index = (pl.ds(piece * rows, rows),)
            came, bit = {0: []}, count // 2
            while bit:
                for slot in sorted(came):
                    step = self.copy(
                        (arrays[slot], index), (arrays[slot | bit], index), ("tp", bit), came[slot], size * (1 + bit // 2)
                    )
                    came[slot | bit] = [step]
                bit //= 2
        return arrays[1:]

    def trade_tp(self, blocks):
        made = []
        for slot in range(1, len(blocks)):
            made.append(self.make(blocks[slot].shape, blocks[slot].dtype))
            self.copy((self.take(blocks[slot]), ()), (made[-1], ()), ("tp", slot), [], blocks[slot].size * 4)
        return made

    def share_tp(self, value):
        held, made = self.take(value), []
        for slot in range(1, lax.axis_size("tp")):
            made.append(self.make(value.shape, value.dtype))
            self.copy((held, ()), (made[-1], ()), ("tp", slot), [], value.size * 4)
        return made

    def swap(self, value):
        held, target = self.take(value), self.make(value.shape, value.dtype)
        self.copy((held, ()), (target, ()), ("fsdp", 1), [], value.size * 2)
        return target

    def trade_fsdp(self, blocks):
        made = []
        for place in range(1, len(blocks)):
            made.append(self.make(blocks[place].shape, blocks[place].dtype))
            slot = 2 * reversed_bits(place, len(blocks))
            self.copy((self.take(blocks[place]), ()), (made[-1], ()), ("fsdp", slot), [], blocks[place].size * 4)
        return made

    def trade_stack(self, value, first, count):
        skip = int(first == 0)
        held, target = self.take(value), self.make((value.shape[0] - skip,) + value.shape[1:], value.dtype)
        for j in range(skip, value.shape[0]):
            slot = reversed_bits(first + j, count)
            self.copy((held, (j,)), (target, (j - skip,)), ("fsdp", slot), [], value[0].size * 4)
        return target

    def trade_rows(self, value, count):
        rows = value.shape[0] // count
        held, target = self.take(value), self.make((count - 1, rows) + value.shape[1:], value.dtype)
        for slot in range(1, count):
            source = lambda ranks, slot=slot: (pl.ds(pl.multiple_of((ranks["fsdp"] ^ slot) * rows, rows), rows),)
            self.copy((held, source), (target, (slot - 1,)), ("fsdp", slot), [], rows * 512)
        return target

    def spread(self, source, target, rows, size, pieces, needs):
        count = lax.axis_size("fsdp")
        bits = []
        while count >> (len(bits) + 1):
            bits.append(count >> (len(bits) + 1))
        upper = bits[:-1]
        turned = upper[len(upper) // 2 :] + upper[: len(upper) // 2]
        orders = [upper + [1], turned + [1]]
        for piece in range(pieces):
            inner = (pl.ds(piece * (rows // pieces), rows // pieces),) if pieces > 1 else ()
            came = {0: list(needs)}
            for bit in orders[piece % 2]:
                for slot in sorted(came):
                    origin = source(inner) if slot == 0 else (target, (reversed_bits(slot, count),) + inner)
                    goal = (target, (reversed_bits(slot | bit, count),) + inner)
                    came[slot | bit] = [self.copy(origin, goal, ("fsdp", bit), came[slot], size // pieces)]

    def gather_fsdp(self, value, pieces=2):
        count = lax.axis_size("fsdp")
        held, target = self.take(value), self.make((count,) + value.shape, value.dtype)
        self.spread(lambda inner: (held, inner), target, value.shape[0], value.size * 2, pieces, [])
        self.copy((held, ()), (target, (0,)), None, [], value.size)
        return target

    def gather_both(self, value):
        count, slots = lax.axis_size("fsdp"), lax.axis_size("tp")
        held, target = self.take(value), self.make((count, slots) + value.shape, value.dtype)
        needs = [self.copy((held, ()), (target, (0, 0)), None, [], value.size)]
        for slot in range(1, slots):
            needs.append(self.copy((held, ()), (target, (0, slot)), ("tp", slot), [], value.size * 2))
        self.spread(lambda inner: (target, (0,) + inner), target, slots, value.size * 2 * slots, 2, needs)
        return target

    def meet(self):
        ranks = {axis: lax.axis_index(axis) for axis in ("fsdp", "tp")}
        barrier = pltpu.get_barrier_semaphore()
        places = sorted({step[2] for step in self.steps if step[2]})
        for axis, bit in places:
            pl.semaphore_signal(
                barrier, inc=1, device_id={axis: ranks[axis] ^ bit}, device_id_type=pl.DeviceIdType.MESH
            )
        pl.semaphore_wait(barrier, len(places))

    def describe(self, number, ins, outs, send, recv):
        ranks = {axis: lax.axis_index(axis) for axis in ("fsdp", "tp")}

        def view(spot):
            (kind, which), index = spot
            ref = (ins if kind == "in" else outs)[which]
            index = index(ranks) if callable(index) else index
            return ref.at[index] if index else ref

        source, target, place = self.steps[number][:3]
        if place is None:
            return pltpu.make_async_copy(view(source), view(target), send.at[number])
        axis, bit = place
        return pltpu.make_async_remote_copy(
            src_ref=view(source),
            dst_ref=view(target),
            send_sem=send.at[number],
            recv_sem=recv.at[number],
            device_id={axis: ranks[axis] ^ bit},
            device_id_type=pl.DeviceIdType.MESH,
        )

    def begin(self, ins, outs, send, recv):
        self.meet()
        for number in range(len(self.steps)):
            self.describe(number, ins, outs, send, recv).start()

    def finish(self, ins, outs, send, recv):
        for number in range(len(self.steps)):
            self.describe(number, ins, outs, send, recv).wait()

    def kernel(self, *refs):
        ins, outs = refs[: len(self.inputs)], refs[len(self.inputs) : len(self.inputs) + len(self.outputs)]
        send, recv = refs[-2:]
        self.meet()
        started, arrived = {}, set()

        def arrive(number):
            if number not in arrived:
                arrived.add(number)
                if self.steps[number][2]:
                    started[number].wait_recv()
                else:
                    started[number].wait()

        for number in sorted(range(len(self.steps)), key=lambda i: self.steps[i][4]):
            for need in self.steps[number][3]:
                arrive(need)
            started[number] = self.describe(number, ins, outs, send, recv)
            started[number].start()
        for number in sorted(range(len(self.steps)), key=lambda i: self.steps[i][5]):
            arrive(number)
            if self.steps[number][2]:
                started[number].wait_send()

    def semaphores(self):
        return [pltpu.SemaphoreType.DMA((len(self.steps),)), pltpu.SemaphoreType.DMA((len(self.steps),))]

    def run(self, number, time, name):
        count = len(self.steps)
        anywhere = pl.BlockSpec(memory_space=pl.ANY)
        made = pl.pallas_call(
            self.kernel,
            out_shape=self.outputs,
            in_specs=[anywhere] * len(self.inputs),
            out_specs=[anywhere] * len(self.outputs),
            scratch_shapes=[pltpu.SemaphoreType.DMA((count,)), pltpu.SemaphoreType.DMA((count,))],
            compiler_params=pltpu.CompilerParams(collective_id=number, has_side_effects=True),
            cost_estimate=cost(time),
            name=name,
        )(*self.inputs)
        self.made = list(made)

    def get(self, spot):
        return [self.made[part[1]] for part in spot] if isinstance(spot, list) else self.made[spot[1]]


def trade_slots(blocks, axis):
    return [blocks[0]] + [exchange(blocks[slot], axis, slot) for slot in range(1, len(blocks))]


def after(value, *others):
    return lax.optimization_barrier((value, *others))[0]


def local(
    inputs,
    cotangent,
    lengths,
    routes,
    attn_gain,
    moe_gain,
    router_weight,
    query_weight,
    key_weight,
    value_weight,
    output_weight,
    gate_weight,
    up_weight,
    down_weight,
):
    tensor_count = lax.axis_size("tp")
    tensor_rank = lax.axis_index("tp")
    shard_rank = lax.axis_index("fsdp")
    micro, rows, width = inputs.shape
    span = rows * tensor_count
    experts, shard_width, hidden = gate_weight.shape
    steps = range(micro)
    slots, blocks = tensor_count, lax.axis_size("fsdp")
    slot_ranks = [tensor_rank ^ slot for slot in range(slots)]
    odd, upper = tensor_rank % 2 == 1, tensor_rank // 2 % 2 == 1
    info_all = jnp.concatenate([jnp.stack([shard_rank, tensor_rank]).astype(jnp.int32), lengths])
    infos = [jnp.stack([info_all[0], info_all[1], info_all[2 + m]]) for m in steps]

    small = jnp.concatenate([router_weight, attn_gain[:, None], moe_gain[:, None]], axis=1).astype(f32)
    small = jnp.pad(small, ((0, 0), (0, LANES - small.shape[1])))
    qkv_local = jnp.concatenate([query_weight, key_weight, value_weight], axis=1)
    qkv_cols = qkv_local.shape[1]

    stacked = jnp.stack(
        [gate_weight.transpose(1, 0, 2), up_weight.transpose(1, 0, 2), down_weight.transpose(2, 0, 1)], axis=1
    )
    expert_local = (
        stacked.reshape(shard_width, 3, experts // PAIR, PAIR, hidden)
        .transpose(0, 2, 1, 3, 4)
        .reshape(shard_width, 3 * experts * hidden)
    )

    row_place = jnp.arange(rows, dtype=jnp.int32)
    span_pos = jnp.concatenate([shard_rank * span + rank * rows + row_place for rank in slot_ranks])
    cos_row, sin_row = rope_tables(span_pos)
    row_pos = shard_rank * span + tensor_rank * rows + row_place
    valid = row_pos[None, :] < lengths[:, None]
    own_grads = jnp.where(valid[:, :, None], cotangent, jnp.zeros_like(cotangent))

    x_slots, queries, kvs, kv_alls, gm_slots = [], [], [], [], []
    for m in range(micro + 1):
        moves = Moves()
        wanted = {}
        if m < micro:
            wanted["x"] = moves.gather_tp(after(inputs[m], kvs[-1]) if m else inputs[m])
        if m:
            wanted["kv"] = moves.gather_fsdp(kvs[m - 1])
        if m == 0:
            wanted["weights"] = moves.gather_fsdp(qkv_local)
            wanted["small"] = moves.gather_both(small)
            wanted["out"] = moves.gather_both(output_weight.T)
        if m == micro:
            wanted["gm"] = moves.gather_tp(own_grads[0])
        moves.run(m, 25, "open")
        if m == 0:
            qkv_full, router_full, gains = place_weights(
                info_all, moves.get(wanted["weights"]), moves.get(wanted["small"]), experts
            )
            gain_attn, gain_moe = gains[0:1], gains[1:2]
            out_all = moves.get(wanted["out"])
        if m:
            kv_alls.append(moves.get(wanted["kv"]))
        if m < micro:
            x_slots.append([inputs[m]] + moves.get(wanted["x"]))
            query, kv = project_qkv(x_slots[m], gain_attn, qkv_full, cos_row, sin_row)
            queries.append(query)
            kvs.append(kv)
        else:
            gm_slots.append([own_grads[0]] + moves.get(wanted["gm"]))
    for m in range(1, micro):
        gm_slots.append(trade_slots([after(own_grads[m], gm_slots[m - 1][-1])] * slots, "tp"))

    expert_full = lax.all_gather(after(expert_local, kv_alls[-1]), "fsdp", axis=0, tiled=True)
    order = kv_alls[-1]
    attended, logs, att_owns, middles, normeds = [], [], [], [], []
    moves, spots = Moves(), []
    for m in steps:
        *att_slots, log_total = attend(after(infos[m], order), queries[m], kv_alls[m], rows)
        order = log_total
        attended.append(att_slots)
        logs.append(log_total)
        spots.append(moves.trade_tp(att_slots))
    out_full = place_output_weight(after(info_all, logs[0]), out_all)
    moves.run(micro + 1, 12, "trade")
    for m in steps:
        att_own, middle, normed = close_attention(
            inputs[m], gain_moe, out_full, [attended[m][0]] + moves.get(spots[m])
        )
        order = middle
        att_owns.append(att_own)
        middles.append(middle)
        normeds.append(normed)
    moves = Moves()
    spot = moves.gather_tp(normeds[0])
    moves.run(micro + 2, 18, "gather_normed")
    moe_slots = [[normeds[0]] + moves.get(spot)]

    expert_outs, gin_parts = [], []
    for m in steps:
        ride = Moves()
        ahead = ride.share_tp(normeds[m + 1]) if m + 1 < micro else None
        behind = ride.trade_tp(expert_outs[m - 1][:slots]) if m else None
        results = experts_both(
            after(infos[m], order),
            routes[m],
            router_full,
            expert_full,
            moe_slots[m],
            gm_slots[m],
            ride,
            2 * micro + 4 + m,
        )
        expert_outs.append(results)
        if ahead:
            moe_slots.append([normeds[m + 1]] + ride.get(ahead))
        if behind:
            gin_parts.append([expert_outs[m - 1][0]] + ride.get(behind))
        order = results[2 * slots]
    lows_g = [results[2 * slots + 1] for results in expert_outs]
    lows_h = [results[2 * slots + 2] for results in expert_outs]
    ride = Moves()
    behind = ride.trade_tp(expert_outs[-1][:slots])
    expert_grad = expert_grads(moe_slots, gm_slots, lows_g, lows_h, ride, 3 * micro + 4)
    gin_parts.append([expert_outs[-1][0]] + ride.get(behind))
    expert_sum = lax.psum_scatter(expert_grad, "fsdp", scatter_dimension=0, tiled=True)

    sums = 0.0
    order = expert_grad
    grad_middles, grad_attns, grad_slots = [], [], []
    moves = Moves()
    for m in steps:
        grad_middle, grad_attn, sums_moe, *grads = moe_back(
            after(infos[m], order),
            gin_parts[m],
            expert_outs[m][2 * slots],
            router_full,
            middles[m],
            normeds[m],
            gain_moe,
            cotangent[m],
            out_full,
            slots,
        )
        order = sums_moe
        sums = sums + sums_moe
        grad_middles.append(grad_middle)
        grad_attns.append(grad_attn)
        grad_slots.append((grads[0], moves.trade_tp(grads)))
    out_keep, out_send = weight_grad(after(info_all, order), grad_attns, att_owns, blocks)
    out_spot = moves.swap(out_send)
    moves.run(3 * micro + 5, 12, "trade_back")
    grad_slots = [[own] + moves.get(spots) for own, spots in grad_slots]
    order = out_keep
    out_stack = (out_keep.astype(f32) + moves.get(out_spot).astype(f32)).astype(bf16)

    dqs, dkvs, mixed_parts = [], [], []
    for m in steps:
        dq, keep, send = attend_back(
            after(infos[m], order), queries[m], kv_alls[m], logs[m], cos_row, sin_row, attended[m], grad_slots[m]
        )
        mixed = expert_outs[m][slots : 2 * slots]
        mixed_parts.append(trade_slots([mixed[0]] + [after(part, order) for part in mixed[1:]], "tp"))
        order = dq
        dqs.append(dq)
        met = exchange(send, "fsdp", 1)
        half = blocks // 2
        dkv = [(keep[j].astype(f32) + met[j].astype(f32)).astype(bf16) for j in range(half)]
        if m + 1 < micro:
            moves = Moves()
            came = moves.trade_fsdp(dkv)
            moves.run(3 * micro + 6 + m, 12, "early_keys")
            dkv = [dkv[0]] + moves.get(came)
        dkvs.append(dkv)

    normed_all, qkv_grads, normed_parts = [], [], []
    for m in steps:
        if m + 1 == micro:
            moves = Moves()
            came = moves.trade_fsdp(dkvs[m])
            met = [moves.trade_tp(parts) for parts in normed_parts]
            out_spot = moves.trade_stack(out_stack, 0, blocks)
            moves.run(2 * micro + 1, 24, "close_keys")
            out_came = moves.get(out_spot)
            dkvs[m] = [dkvs[m][0]] + moves.get(came)
            normed_parts = [[parts[0]] + moves.get(spots) for parts, spots in zip(normed_parts, met)]
        *parts, grads, normed_attn, sums_attn = qkv_back(
            dqs[m], dkvs[m], cos_row, sin_row, after(gain_attn, order), qkv_full, x_slots[m]
        )
        order = sums_attn
        sums = sums + jnp.pad(sums_attn[0:1], ((1, 22), (0, 0)))
        normed_all.append(normed_attn)
        qkv_grads.append(grads)
        normed_parts.append(parts)
    qkv_keep, qkv_send = weight_grad(after(info_all, order), normed_all, qkv_grads, blocks)
    table = jnp.pad(sums, ((0, LANES - sums.shape[0]), (0, 0))).T

    total = lambda first, *stacks: first.astype(f32) + sum(jnp.sum(stack.astype(f32), axis=0) for stack in stacks)
    head_cols, few = output_weight.shape[0], small.shape[0]
    moves = Moves()
    met = moves.trade_tp(normed_parts[-1])
    near, far = moves.trade_stack(qkv_keep, 0, blocks), moves.trade_stack(qkv_send, blocks // 2, blocks)
    out_sum = total(out_stack[0], out_came).astype(bf16)
    out_parts = [out_sum[:, slot * head_cols : (slot + 1) * head_cols] for slot in range(slots)]
    out_spots = moves.trade_tp(out_parts)
    table_spot = moves.trade_rows(table.astype(bf16), blocks)
    moves.run(2 * micro + 2, 24, "close_weights")
    normed_parts[-1] = [normed_parts[-1][0]] + moves.get(met)
    own_rows = lax.dynamic_slice_in_dim(table, shard_rank * shard_width, shard_width, 0)
    table_sum = total(own_rows, moves.get(table_spot))
    qkv_sum = total(qkv_keep[0], moves.get(near), moves.get(far))
    table_parts = [lax.dynamic_slice_in_dim(table_sum, rank * few, few, 0) for rank in slot_ranks]
    out_final = sum(part.astype(f32) for part in [out_parts[0]] + moves.get(out_spots))
    small_sum = sum(trade_slots(table_parts, "tp"))

    outputs = close_outputs(after(info_all, normed_parts[-1][-1]), mixed_parts, middles, slots)
    gate_sum, up_sum, down_sum = unpack_experts(expert_sum)
    input_grad = close_input_grad(normed_parts, grad_middles, inputs, gain_attn)
    q_cols, k_cols = query_weight.shape[1], key_weight.shape[1]
    return (
        outputs,
        input_grad,
        small_sum[:, 1],
        small_sum[:, 0],
        small_sum[:, 8 : 8 + experts],
        qkv_sum[:, :q_cols],
        qkv_sum[:, q_cols : q_cols + k_cols],
        qkv_sum[:, q_cols + k_cols : qkv_cols],
        out_final.T,
        gate_sum,
        up_sum,
        down_sum,
    )


def solution(mesh):
    rows_spec = P(None, ("fsdp", "tp"), None)
    small_specs = (P(("fsdp", "tp")), P(("fsdp", "tp")), P(("fsdp", "tp"), None))
    weight_specs = (
        P("fsdp", "tp"),
        P("fsdp", "tp"),
        P("fsdp", "tp"),
        P("tp", "fsdp"),
        P(None, "fsdp", "tp"),
        P(None, "fsdp", "tp"),
        P(None, "tp", "fsdp"),
    )
    in_specs = (rows_spec, rows_spec, P(), P(None, "fsdp", None)) + small_specs + weight_specs
    out_specs = (rows_spec, rows_spec) + small_specs + weight_specs
    return jax.shard_map(local, mesh=mesh, in_specs=in_specs, out_specs=out_specs, check_vma=False)
```
